256 devices in a mesh: grp: 4 (over x), ep: 64 (over y, z, core).
Axes of the slice: x: 4, y: 4, z: 8, core: 2. Of those that a mesh axis runs over, the one named last changes fastest.
Arguments:
- queries: bfloat16 [6144, 4096], P(('grp', 'ep')), may hold values from -9 to 9
- new_keys: bfloat16 [6144, 512], P(('grp', 'ep')), may hold values from -9 to 9
- new_values: bfloat16 [6144, 512], P(('grp', 'ep')), may hold values from -6 to 6
- key_cache: bfloat16 [4096, 48, 512], P(('grp', 'ep')), may hold values from -9 to 9
- value_cache: bfloat16 [4096, 48, 512], P(('grp', 'ep')), may hold values from -6 to 6
- cache_len: int32 [4096], P(('grp', 'ep')), may hold values from 2 to 48, as said below
- residual: bfloat16 [6144, 2048], P(('grp', 'ep')), may hold values from -17 to 17
- out_proj: bfloat16 [4096, 2048], P(None, 'grp'), may hold values from -0.09375 to 0.09375
- norm_gain: float32 [2048], P('grp'), may hold values from 0.1 to 1.9
- expert_ids: int32 [6144, 8], P(('grp', 'ep')), may hold values from 0 to 127, as said below
- route_weights: bfloat16 [6144, 8], P(('grp', 'ep')), may hold values from 0.049804688 to 1
- slot_expert: int32 [192], replicated, may hold values from 0 to 127, as said below
- gate_up: bfloat16 [192, 2048, 1536], P('ep', 'grp'), may hold values from -1 to 1, as said below
- down_proj: bfloat16 [192, 768, 2048], P('ep', None, 'grp'), may hold values from -2 to 2, as said below
Outputs:
- moe_out: bfloat16 [6144, 2048], P(('grp', 'ep'))
- layer_out: bfloat16 [6144, 2048], P(('grp', 'ep'))
The draws below stay inside these ranges and needn't reach their ends.
Inputs may be any that keep to these rules, and one draw needn't show every extreme that they name: `expert_ids`: each row names 8 different experts. In the rows of one device one expert, the same on all devices, is named by exactly 3 rows, and every other expert by at most 2 rows; some expert other than it is named by exactly 2 rows of a device. `slot_expert`: every expert is held by one or two slots; the expert named by 3 rows of every device is held by two. `cache_len`: some request has exactly 48 cached tokens. `gate_up`: slots holding the same expert hold equal weights. `down_proj`: slots holding the same expert hold equal weights.
All inputs are finite; a program needn't handle non-finite values.
Results may differ from the reference program's by a relative error of at most 0.033.
Values may be sent and summed in bfloat16 or wider, within the bound.
A program may use at most 128 MiB of HBM per device.

```python
import math
import jax
import jax.numpy as jnp
from jax import lax

D = 2048
HEADS = 32
KV_HEADS = 4
HEAD_DIM = 128
FF = 768
TOPK = 8
PRE = 8
DEC = 16
CACHE = 48
ROWS = 6144
REQS = 4096
DQ = 512
EXPERTS = 128
SLOTS = 192
CAP = 3
N_GRP = 4
N_EP = 64


def pick_hot(key):
    return jax.random.randint(jax.random.fold_in(key, 11), (), 0, EXPERTS)


def slot_table(key):
    hot_expert = pick_hot(key)
    others = jnp.arange(EXPERTS - 1, dtype=jnp.int32)
    others = others + (others >= hot_expert).astype(jnp.int32)
    shuffled = jax.random.permutation(jax.random.fold_in(key, 13), others)
    extra_slots = SLOTS - EXPERTS
    copies = jnp.concatenate([jnp.arange(EXPERTS, dtype=jnp.int32), hot_expert[None].astype(jnp.int32), shuffled[:extra_slots - 1]])
    return jax.random.permutation(jax.random.fold_in(key, 17), copies).astype(jnp.int32)


def draw_slot_expert(key, part):
    return slot_table(key)


def draw_expert_ids(key, part):
    rows_dev = PRE + DEC
    blocks = ROWS // rows_dev
    hot_expert = pick_hot(key)
    permuted = jax.vmap(lambda sub_key: jax.random.permutation(sub_key, EXPERTS - 1))(jax.random.split(jax.random.fold_in(key, 19), blocks))
    position = (jnp.arange(rows_dev)[:, None] * TOPK + jnp.arange(TOPK)[None, :]) % (EXPERTS - 1)
    chosen = permuted[:, position]
    chosen = chosen + (chosen >= hot_expert).astype(jnp.int32)
    hot_rank = jax.vmap(lambda sub_key: jax.random.permutation(sub_key, rows_dev))(jax.random.split(jax.random.fold_in(key, 23), blocks))
    hot_row = hot_rank < CAP
    last_route = jnp.arange(TOPK) == TOPK - 1
    chosen = jnp.where(hot_row[:, :, None] & last_route[None, None, :], hot_expert, chosen)
    order_keys = jax.random.randint(jax.random.fold_in(key, 29), (blocks, rows_dev, TOPK), 0, 1048576) * TOPK + jnp.arange(TOPK)[None, None, :]
    ordering = jnp.argsort(order_keys, axis=-1, stable=True)
    return jnp.take_along_axis(chosen, ordering, axis=-1).reshape(ROWS, TOPK).astype(jnp.int32)


def draw_cache_len(key, part):
    blocks = REQS // DEC
    device_top = jax.random.randint(jax.random.fold_in(key, 31), (blocks, 1), 2, CACHE + 1)
    lengths = jax.random.randint(jax.random.fold_in(key, 37), (blocks, DEC), 2, device_top + 1).reshape(REQS)
    full_index = jax.random.randint(jax.random.fold_in(key, 41), (), 0, REQS)
    return jnp.where(jnp.arange(REQS) == full_index, CACHE, lengths).astype(jnp.int32)


def base_field(key, shape):
    return jnp.clip(jax.random.normal(key, shape, jnp.float32), -6.0, 6.0)


def draw_queries(key, part):
    base_draw = base_field(jax.random.fold_in(key, 47), (ROWS, HEADS * HEAD_DIM))
    return base_draw.astype(jnp.bfloat16)


def draw_new_keys(key, part):
    base_draw = base_field(jax.random.fold_in(key, 53), (ROWS, KV_HEADS * HEAD_DIM))
    return base_draw.astype(jnp.bfloat16)


def draw_key_cache(key, part):
    base_draw = base_field(jax.random.fold_in(key, 59), (REQS, CACHE, KV_HEADS * HEAD_DIM))
    return base_draw.astype(jnp.bfloat16)


def draw_residual(key, part):
    column = jnp.arange(D, dtype=jnp.float32) / (D - 1)
    column_ramp = 1.0 + 2.0 * column
    base_draw = jnp.clip(jax.random.normal(jax.random.fold_in(key, 61), (ROWS, D), jnp.float32), -4.0, 4.0)
    rough_factor = jax.random.uniform(jax.random.fold_in(key, 67), (D,), jnp.float32, 0.6, 1.4)
    return (base_draw * column_ramp[None, :] * rough_factor[None, :]).astype(jnp.bfloat16)


def expert_matrix(key, expert, shape, scaling):
    sub_key = jax.random.fold_in(key, expert)
    values = jnp.clip(jax.random.normal(sub_key, shape, jnp.float32), -5.0, 5.0)
    return (values * scaling).astype(jnp.bfloat16)


def draw_gate_up(key, part):
    table_values = slot_table(key)
    weight_key = jax.random.fold_in(key, 71)
    return lax.map(lambda expert: expert_matrix(weight_key, expert, (D, 2 * FF), D ** (-0.5)), table_values)


def draw_down_proj(key, part):
    table_values = slot_table(key)
    weight_key = jax.random.fold_in(key, 73)
    return lax.map(lambda expert: expert_matrix(weight_key, expert, (FF, D), 2.0 * FF ** (-0.5)), table_values)


def levels(rng, shape, cuts, smallest, high):
    def one(dim, shards_of):
        draws = jax.random.uniform(jax.random.fold_in(jax.random.fold_in(rng, 6), dim), (shards_of,), jnp.float32, smallest / len(cuts), high / len(cuts))
        return jnp.repeat(jnp.exp(draws), shape[dim] // shards_of).reshape((-1,) + (1,) * (len(shape) - dim - 1))

    factor_of = one(*cuts[0])
    for cut in cuts[1:]:
        factor_of = factor_of * one(*cut)
    return factor_of


def gaussian(key, shape, deviation, bound, cuts=(), kind=jnp.bfloat16):
    factor_of = levels(key, shape, cuts, -0.22, 0.18) if cuts else 1.0
    entries = jax.random.normal(key, shape, jnp.float32) * deviation * factor_of
    return jnp.minimum(jnp.maximum(entries, -bound), bound).astype(kind)


def setup_inputs(seed: int = 0) -> dict:
    seeds = jax.random.split(jax.random.key(seed), 15)
    return {
        "queries": draw_queries(jax.random.fold_in(seeds[14], 71), 0),
        "new_keys": draw_new_keys(jax.random.fold_in(seeds[14], 71), 0),
        "new_values": gaussian(seeds[2], (ROWS, KV_HEADS * HEAD_DIM), 1.0, 6.0, ((0, 256),)),
        "key_cache": draw_key_cache(jax.random.fold_in(seeds[14], 71), 0),
        "value_cache": gaussian(seeds[4], (REQS, CACHE, KV_HEADS * HEAD_DIM), 1.0, 6.0, ((0, 256),)),
        "cache_len": draw_cache_len(jax.random.fold_in(seeds[14], 71), 0),
        "residual": draw_residual(jax.random.fold_in(seeds[14], 71), 0),
        "out_proj": gaussian(seeds[7], (HEADS * HEAD_DIM, D), (HEADS * HEAD_DIM) ** -0.5, 0.09375, ((1, 4),)),
        "norm_gain": jnp.clip(1.0 + 0.18 * jax.random.normal(seeds[8], (D,), jnp.float32), 0.1, 1.9),
        "expert_ids": draw_expert_ids(jax.random.fold_in(seeds[14], 71), 0),
        "route_weights": jnp.clip(jnp.exp(math.log(1.0) - 2.9996462 * jax.random.uniform(seeds[10], (ROWS, TOPK), jnp.float32) ** levels(seeds[10], (ROWS, TOPK), ((0, 256),), -0.2, 0.2)), 0.049804688, 1.0).astype(jnp.bfloat16),
        "slot_expert": draw_slot_expert(jax.random.fold_in(seeds[14], 71), 0),
        "gate_up": draw_gate_up(jax.random.fold_in(seeds[14], 71), 0),
        "down_proj": draw_down_proj(jax.random.fold_in(seeds[14], 71), 0),
    }


epsilon = 1e-06
masked_score = -1e+30

def bfloat_round(values):
    lowered = values.astype(jnp.bfloat16)
    return lax.optimization_barrier(lowered).astype(jnp.float32)

def reference(queries, new_keys, new_values, key_cache, value_cache, cache_len, residual, out_proj, norm_gain, expert_ids, route_weights, slot_expert, gate_up, down_proj):
    rows_dev = PRE + DEC
    blocks = ROWS // rows_dev
    head_group = HEADS // KV_HEADS
    scaling = 1.0 / math.sqrt(HEAD_DIM)
    highest = lax.Precision.HIGHEST
    query_all = queries.astype(jnp.float32).reshape(blocks, rows_dev, KV_HEADS, head_group, HEAD_DIM)
    keys_all = new_keys.astype(jnp.float32).reshape(blocks, rows_dev, KV_HEADS, HEAD_DIM)
    values_all = new_values.astype(jnp.float32).reshape(blocks, rows_dev, KV_HEADS, HEAD_DIM)
    pre_scores = jnp.einsum('bikgd,bjkd->bkgij', query_all[:, :PRE], keys_all[:, :PRE], precision=highest) * scaling
    causal = jnp.arange(PRE, dtype=jnp.int32)[:, None] >= jnp.arange(PRE, dtype=jnp.int32)[None, :]
    pre_scores = jnp.where(causal, pre_scores, masked_score)
    exponent = jnp.exp(pre_scores - lax.optimization_barrier(jnp.max(pre_scores, axis=-1, keepdims=True)))
    pre_probs = bfloat_round(exponent / lax.optimization_barrier(jnp.sum(exponent, axis=-1, keepdims=True)))
    pre_context = jnp.einsum('bkgij,bjkd->bikgd', pre_probs, values_all[:, :PRE], precision=highest)
    pre_context = pre_context.reshape(blocks, PRE, HEADS * HEAD_DIM)
    dec_query = query_all[:, PRE:].reshape(REQS, KV_HEADS, head_group, HEAD_DIM)
    dec_keys = keys_all[:, PRE:].reshape(REQS, KV_HEADS, HEAD_DIM)
    dec_values = values_all[:, PRE:].reshape(REQS, KV_HEADS, HEAD_DIM)
    cached_keys = key_cache.astype(jnp.float32).reshape(REQS, CACHE, KV_HEADS, HEAD_DIM)
    cached_values = value_cache.astype(jnp.float32).reshape(REQS, CACHE, KV_HEADS, HEAD_DIM)
    cache_scores = jnp.einsum('nkgd,ntkd->nkgt', dec_query, cached_keys, precision=highest) * scaling
    own_score = jnp.einsum('nkgd,nkd->nkg', dec_query, dec_keys, precision=highest) * scaling
    valid = jnp.arange(CACHE, dtype=jnp.int32)[None, :] < cache_len[:, None]
    cache_scores = jnp.where(valid[:, None, None, :], cache_scores, masked_score)
    top_score = jnp.maximum(lax.optimization_barrier(jnp.max(cache_scores, axis=-1)), own_score)
    cache_exp = jnp.exp(cache_scores - top_score[..., None])
    own_exp = jnp.exp(own_score - top_score)
    denominator = lax.optimization_barrier(jnp.sum(cache_exp, axis=-1)) + own_exp
    cache_probs = bfloat_round(cache_exp / denominator[..., None])
    own_probs = bfloat_round(own_exp / denominator)
    dec_context = jnp.einsum('nkgt,ntkd->nkgd', cache_probs, cached_values, precision=highest)
    dec_context = dec_context + own_probs[..., None] * dec_values[:, :, None, :]
    dec_context = dec_context.reshape(blocks, DEC, HEADS * HEAD_DIM)
    context = jnp.concatenate([pre_context, dec_context], axis=1).reshape(ROWS, HEADS * HEAD_DIM).astype(jnp.bfloat16)
    attended = (residual.astype(jnp.float32) + jnp.dot(context, out_proj, preferred_element_type=jnp.float32)).astype(jnp.bfloat16)
    attended_f = attended.astype(jnp.float32)
    mean_square = lax.optimization_barrier(jnp.mean(attended_f * attended_f, axis=-1))
    normed = (attended_f * lax.rsqrt(mean_square + epsilon)[:, None] * norm_gain[None, :]).astype(jnp.bfloat16)
    route_share = route_weights.astype(jnp.float32)
    route_share = route_share / lax.optimization_barrier(jnp.sum(route_share, axis=-1, keepdims=True))
    expert_range = jnp.arange(EXPERTS, dtype=jnp.int32)
    first_slot = jnp.argmax(slot_expert[None, :] == expert_range[:, None], axis=1).astype(jnp.int32)
    per_expert = N_GRP * N_EP * CAP
    flat_ids = expert_ids.reshape(-1)
    picked = (flat_ids[:, None] == expert_range[None, :]).astype(jnp.int32)
    before = jnp.cumsum(picked, axis=0) - picked
    ranking = lax.optimization_barrier(jnp.sum(picked * before, axis=1))
    position = flat_ids * per_expert + ranking
    source_rows = jnp.zeros((EXPERTS * per_expert,), jnp.int32).at[position].set(jnp.arange(ROWS * TOPK, dtype=jnp.int32) // TOPK)
    slot_share = jnp.zeros((EXPERTS * per_expert,), jnp.float32).at[position].set(route_share.reshape(-1))
    quarters = D // DQ

    def one_expert(mixture, expert):
        rows_here = lax.dynamic_slice_in_dim(source_rows, expert * per_expert, per_expert)
        share_here = lax.dynamic_slice_in_dim(slot_share, expert * per_expert, per_expert)
        inputs_here = normed[rows_here].astype(jnp.float32).reshape(per_expert, quarters, DQ)
        slot_index = first_slot[expert]
        weights_here = gate_up[slot_index].astype(jnp.float32).reshape(quarters, DQ, 2 * FF)
        partial_value = jnp.einsum('cqd,qdf->qcf', inputs_here, weights_here, precision=highest)
        summed = lax.optimization_barrier(jnp.sum(bfloat_round(partial_value), axis=0))
        hidden = (jax.nn.silu(summed[:, :FF]) * summed[:, FF:]).astype(jnp.bfloat16)
        produced = jnp.dot(hidden, down_proj[slot_index], preferred_element_type=jnp.float32).astype(jnp.bfloat16)
        mixture = mixture.at[rows_here].add(share_here[:, None] * produced.astype(jnp.float32))
        return (mixture, None)
    mixture, unused_out = lax.scan(one_expert, jnp.zeros((ROWS, D), jnp.float32), expert_range)
    moe_out = mixture.astype(jnp.bfloat16)
    layer_out = (attended_f + mixture).astype(jnp.bfloat16)
    return (moe_out, layer_out)
```

```python
import math

import jax
import jax.numpy as jnp
from jax import lax
from jax.sharding import PartitionSpec as P

D = 2048
HEADS = 32
KV_HEADS = 4
HEAD_DIM = 128
FF = 768
TOPK = 8
EXP_DEV = 2
SLOTS_DEV = 3
PRE = 8


masked_score = -1e30
epsilon = 1e-06


def prefill_context(queries, new_keys, new_values):
    head_group = HEADS // KV_HEADS
    scaling = 1.0 / math.sqrt(HEAD_DIM)
    query_pre = queries[:PRE].reshape(PRE, KV_HEADS, head_group, HEAD_DIM)
    keys_pre = new_keys[:PRE].reshape(PRE, KV_HEADS, HEAD_DIM)
    values_pre = new_values[:PRE].reshape(PRE, KV_HEADS, HEAD_DIM)
    scores = (
        jnp.einsum("ikgd,jkd->kgij", query_pre, keys_pre, preferred_element_type=jnp.float32)
        * scaling
    )
    causal = jnp.arange(PRE)[:, None] >= jnp.arange(PRE)[None, :]
    scores = jnp.where(causal, scores, masked_score)
    exponent = jnp.exp(scores - jnp.max(scores, axis=-1, keepdims=True))
    attn_probs = (exponent / jnp.sum(exponent, axis=-1, keepdims=True)).astype(jnp.bfloat16)
    mixed_values = jnp.einsum(
        "kgij,jkd->ikgd", attn_probs, values_pre, preferred_element_type=jnp.float32
    )
    return mixed_values.astype(jnp.bfloat16).reshape(PRE, HEADS * HEAD_DIM)


def decode_context(queries, new_keys, new_values, key_cache, value_cache, cache_len):
    requests = key_cache.shape[0]
    cache_slots = key_cache.shape[1]
    head_group = HEADS // KV_HEADS
    scaling = 1.0 / math.sqrt(HEAD_DIM)
    query_dec = queries[PRE:].reshape(requests, KV_HEADS, head_group, HEAD_DIM)
    keys_dec = new_keys[PRE:].reshape(requests, KV_HEADS, HEAD_DIM)
    values_dec = new_values[PRE:].reshape(requests, KV_HEADS, HEAD_DIM)
    cached_keys = key_cache.reshape(requests, cache_slots, KV_HEADS, HEAD_DIM)
    cached_values = value_cache.reshape(requests, cache_slots, KV_HEADS, HEAD_DIM)
    cache_scores = (
        jnp.einsum("nkgd,ntkd->nkgt", query_dec, cached_keys, preferred_element_type=jnp.float32)
        * scaling
    )
    own_score = (
        jnp.einsum("nkgd,nkd->nkg", query_dec, keys_dec, preferred_element_type=jnp.float32)
        * scaling
    )
    valid = jnp.arange(cache_slots)[None, :] < cache_len[:, None]
    cache_scores = jnp.where(valid[:, None, None, :], cache_scores, masked_score)
    top_score = jnp.maximum(jnp.max(cache_scores, axis=-1), own_score)
    cache_exp = jnp.exp(cache_scores - top_score[..., None])
    own_exp = jnp.exp(own_score - top_score)
    denominator = jnp.sum(cache_exp, axis=-1) + own_exp
    cache_probs = (cache_exp / denominator[..., None]).astype(jnp.bfloat16)
    own_probs = (own_exp / denominator).astype(jnp.bfloat16)
    mixed_values = jnp.einsum(
        "nkgt,ntkd->nkgd", cache_probs, cached_values, preferred_element_type=jnp.float32
    )
    mixed_values = (
        mixed_values
        + own_probs.astype(jnp.float32)[..., None] * values_dec.astype(jnp.float32)[:, :, None, :]
    )
    return mixed_values.astype(jnp.bfloat16).reshape(requests, HEADS * HEAD_DIM)


def activate(summed):
    return (jax.nn.silu(summed[..., :FF]) * summed[..., FF:]).astype(jnp.bfloat16)


def local(
    queries,
    new_keys,
    new_values,
    key_cache,
    value_cache,
    cache_len,
    residual,
    out_proj,
    norm_gain,
    expert_ids,
    route_weights,
    slot_expert,
    gate_up,
    down_proj,
):
    rows_dev = queries.shape[0]
    width_part = out_proj.shape[1]
    ep_devices = lax.axis_size("ep")
    group_devices = lax.axis_size("grp")
    experts_all = EXP_DEV * ep_devices
    most_rows = min(rows_dev, (TOPK * rows_dev + experts_all - 2) // (experts_all - 1) + 1)
    context = jnp.concatenate(
        [
            prefill_context(queries, new_keys, new_values),
            decode_context(queries, new_keys, new_values, key_cache, value_cache, cache_len),
        ],
        axis=0,
    )
    context_col, ids_col, weights_col = (
        lax.all_gather(context, "grp", axis=0, tiled=True),
        lax.all_gather(expert_ids, "grp", axis=0, tiled=True),
        lax.all_gather(route_weights, "grp", axis=0, tiled=True),
    )
    residual_col = lax.all_to_all(residual, "grp", split_axis=1, concat_axis=0, tiled=True)
    attended = (
        residual_col.astype(jnp.float32)
        + jnp.dot(context_col, out_proj, preferred_element_type=jnp.float32)
    ).astype(jnp.bfloat16)
    attended_f = attended.astype(jnp.float32)
    sum_squares = lax.psum(jnp.sum(attended_f * attended_f, axis=1), "grp")
    normed = (
        attended_f * lax.rsqrt(sum_squares / D + epsilon)[:, None] * norm_gain[None, :]
    ).astype(jnp.bfloat16)
    route_share = weights_col.astype(jnp.float32)
    route_share = route_share / jnp.sum(route_share, axis=-1, keepdims=True)
    column_rows = normed.shape[0]
    slot_rows = 2 * group_devices
    ep_index = lax.axis_index("ep")
    ids_all = lax.all_gather(ids_col, "ep", axis=0)
    share_all = lax.all_gather(route_share, "ep", axis=0)
    rows_all = lax.all_gather(normed, "ep", axis=0)
    mine = lax.dynamic_slice_in_dim(slot_expert, ep_index * SLOTS_DEV, SLOTS_DEV)
    slots = jnp.arange(slot_expert.shape[0], dtype=jnp.int32)
    same = slot_expert[None, :] == mine[:, None]
    copies = jnp.sum(same, axis=1)
    place = ep_index * SLOTS_DEV + jnp.arange(SLOTS_DEV)
    copy_index = jnp.sum(same & (slots[None, :] < place[:, None]), axis=1)
    hit = ids_all[:, None, :, :] == mine[None, :, None, None]
    share = jnp.sum(jnp.where(hit, share_all[:, None, :, :], 0.0), axis=-1)
    named = jnp.any(hit, axis=-1)
    count = named.astype(jnp.int32)
    ranking = jnp.cumsum(count, axis=-1) - count
    position = ranking // copies[None, :, None]
    taken = named & (ranking % copies[None, :, None] == copy_index[None, :, None])
    pick = taken[:, :, None, :] & (
        position[:, :, None, :] == jnp.arange(slot_rows)[None, None, :, None]
    )
    received = jnp.einsum(
        "sjtr,srd->jstd",
        pick.astype(jnp.bfloat16),
        rows_all,
        preferred_element_type=jnp.float32,
    ).astype(jnp.bfloat16)
    received = received.reshape(SLOTS_DEV, ep_devices * slot_rows, width_part)
    partial_term = jnp.einsum(
        "jnd,jdf->jnf", received, gate_up, preferred_element_type=jnp.float32
    ).astype(jnp.bfloat16)
    summed = lax.psum_scatter(partial_term, "grp", scatter_dimension=1, tiled=True)
    hidden = activate(summed.astype(jnp.float32))
    hidden = lax.all_gather(hidden, "grp", axis=1, tiled=True)
    expert_out = jnp.einsum(
        "jnh,jhd->jnd", hidden, down_proj, preferred_element_type=jnp.float32
    ).astype(jnp.bfloat16)
    expert_out = expert_out.reshape(SLOTS_DEV, ep_devices, slot_rows, width_part)
    weighted = jnp.where(pick, share[:, :, None, :], 0.0).astype(jnp.bfloat16)
    mixture = jnp.einsum(
        "sjtr,jstd->srd", weighted, expert_out, preferred_element_type=jnp.float32
    ).astype(jnp.bfloat16)
    mixture = lax.psum_scatter(mixture, "ep", scatter_dimension=0, tiled=False)
    mixture = mixture.astype(jnp.float32)
    moe_col = mixture.astype(jnp.bfloat16)
    layer_col = (attended_f + mixture).astype(jnp.bfloat16)
    moe_out, layer_out = (
        lax.all_to_all(moe_col, "grp", split_axis=0, concat_axis=1, tiled=True),
        lax.all_to_all(layer_col, "grp", split_axis=0, concat_axis=1, tiled=True),
    )
    return (moe_out, layer_out)


def solution(mesh):
    placed = (
        P(("grp", "ep"), None),
        P(("grp", "ep"), None),
        P(("grp", "ep"), None),
        P(("grp", "ep"), None, None),
        P(("grp", "ep"), None, None),
        P(("grp", "ep")),
        P(("grp", "ep"), None),
        P(None, "grp"),
        P("grp"),
        P(("grp", "ep"), None),
        P(("grp", "ep"), None),
        P(),
        P("ep", "grp", None),
        P("ep", None, "grp"),
    )
    return jax.shard_map(
        local,
        mesh=mesh,
        in_specs=placed,
        out_specs=(P(("grp", "ep"), None), P(("grp", "ep"), None)),
        check_vma=False,
    )
```

```python
import functools
import math

import jax
import jax.numpy as jnp
from jax import lax
from jax.experimental import pallas as pl
from jax.experimental.pallas import tpu as pltpu
from jax.sharding import PartitionSpec as P

D = 2048
HEADS = 32
KV_HEADS = 4
HEAD_DIM = 128
FF = 768
TOPK = 8
SLOTS_DEV = 3
PRE = 8
DEV_ROWS = 24
COL_ROWS = 96
DQ = 512
HALF = 256
NX = 4
NY = 4
NZ = 8
SPAN = 8

MESH = pl.DeviceIdType.MESH
F32 = jnp.float32
BF16 = jnp.bfloat16

masked_score = -1e30
epsilon = 1e-06


def prefill_context(queries, new_keys, new_values):
    head_group = HEADS // KV_HEADS
    scaling = 1.0 / math.sqrt(HEAD_DIM)
    query_pre = queries[:PRE].reshape(PRE, KV_HEADS, head_group, HEAD_DIM)
    keys_pre = new_keys[:PRE].reshape(PRE, KV_HEADS, HEAD_DIM)
    values_pre = new_values[:PRE].reshape(PRE, KV_HEADS, HEAD_DIM)
    scores = (
        jnp.einsum("ikgd,jkd->kgij", query_pre, keys_pre, preferred_element_type=jnp.float32)
        * scaling
    )
    causal = jnp.arange(PRE)[:, None] >= jnp.arange(PRE)[None, :]
    scores = jnp.where(causal, scores, masked_score)
    exponent = jnp.exp(scores - jnp.max(scores, axis=-1, keepdims=True))
    attn_probs = (exponent / jnp.sum(exponent, axis=-1, keepdims=True)).astype(jnp.bfloat16)
    mixed_values = jnp.einsum(
        "kgij,jkd->ikgd", attn_probs, values_pre, preferred_element_type=jnp.float32
    )
    return mixed_values.astype(jnp.bfloat16).reshape(PRE, HEADS * HEAD_DIM)


def decode_context(queries, new_keys, new_values, key_cache, value_cache, cache_len):
    requests = key_cache.shape[0]
    cache_slots = key_cache.shape[1]
    head_group = HEADS // KV_HEADS
    scaling = 1.0 / math.sqrt(HEAD_DIM)
    query_dec = queries[PRE:].reshape(requests, KV_HEADS, head_group, HEAD_DIM)
    keys_dec = new_keys[PRE:].reshape(requests, KV_HEADS, HEAD_DIM)
    values_dec = new_values[PRE:].reshape(requests, KV_HEADS, HEAD_DIM)
    cached_keys = key_cache.reshape(requests, cache_slots, KV_HEADS, HEAD_DIM)
    cached_values = value_cache.reshape(requests, cache_slots, KV_HEADS, HEAD_DIM)
    cache_scores = (
        jnp.einsum("nkgd,ntkd->nkgt", query_dec, cached_keys, preferred_element_type=jnp.float32)
        * scaling
    )
    own_score = (
        jnp.einsum("nkgd,nkd->nkg", query_dec, keys_dec, preferred_element_type=jnp.float32)
        * scaling
    )
    valid = jnp.arange(cache_slots)[None, :] < cache_len[:, None]
    cache_scores = jnp.where(valid[:, None, None, :], cache_scores, masked_score)
    top_score = jnp.maximum(jnp.max(cache_scores, axis=-1), own_score)
    cache_exp = jnp.exp(cache_scores - top_score[..., None])
    own_exp = jnp.exp(own_score - top_score)
    denominator = jnp.sum(cache_exp, axis=-1) + own_exp
    cache_probs = (cache_exp / denominator[..., None]).astype(jnp.bfloat16)
    own_probs = (own_exp / denominator).astype(jnp.bfloat16)
    mixed_values = jnp.einsum(
        "nkgt,ntkd->nkgd", cache_probs, cached_values, preferred_element_type=jnp.float32
    )
    mixed_values = (
        mixed_values
        + own_probs.astype(jnp.float32)[..., None] * values_dec.astype(jnp.float32)[:, :, None, :]
    )
    return mixed_values.astype(jnp.bfloat16).reshape(requests, HEADS * HEAD_DIM)


CTX_R, CTX_L, CTX_FR, CTX_FL = 0, 1, 2, 3
SIDE = 4
SQUARES = 7
A_RING_R, A_RING_L = 10, 14
B_Y = 17
B_RING_R, B_RING_L = 21, 25
A_Y = 28
A_RELAY = 44
CORE_A = 60
CORE_B = 64
S1_R, S1_L, S2_R, S2_L = 72, 80, 88, 96
H1_R, H1_L, H2_R, H2_L = 104, 112, 120, 128
CORE_MIX = 136
CHAIN = 144
Y_ONE = 152
Y_TWO = 154
FINAL = 156
COPIES = 160


def layer_kernel(
    ctx_ref,
    side_ref,
    out_proj_hbm,
    gain_ref,
    table_ref,
    gate_up_hbm,
    down_hbm,
    moe_ref,
    layer_ref,
    ctx_all,
    side_all,
    proj,
    gate_up,
    down,
    squares,
    attended,
    rows_a,
    rows_b,
    picks,
    picked,
    partial,
    first_in,
    second_in,
    hidden,
    expert_out,
    mixed,
    core_in,
    chain_out,
    chain_in,
    y_part,
    y_one,
    y_two,
    final_out,
    final_in,
    send_sem,
    recv_sem,
    load_sem,
):
    x = lax.axis_index("grp")
    ep = lax.axis_index("ep")
    core = ep % 2
    z = (ep // 2) % NZ
    y = ep // (2 * NZ)

    def x_dev(step):
        return ((x + step) % NX, ep)

    def y_dev(step):
        return (x, (((y + step) % NY) * NZ + z) * 2 + core)

    def z_dev(step):
        return (x, (y * NZ + (z + step) % NZ) * 2 + core)

    partner = (x, (y * NZ + z) * 2 + 1 - core)

    def copy(source, target, index, device):
        return pltpu.make_async_remote_copy(
            src_ref=source,
            dst_ref=target,
            send_sem=send_sem.at[index],
            recv_sem=recv_sem.at[index],
            device_id=device,
            device_id_type=MESH,
        )

    peers = [x_dev(1), x_dev(2), x_dev(3), y_dev(1), y_dev(3), z_dev(1), z_dev(7), partner]
    barrier = pltpu.get_barrier_semaphore()
    for peer in peers:
        pl.semaphore_signal(barrier, inc=1, device_id=peer, device_id_type=MESH)

    loads = [
        pltpu.make_async_copy(out_proj_hbm, proj, load_sem.at[0]),
        pltpu.make_async_copy(gate_up_hbm, gate_up, load_sem.at[1]),
        pltpu.make_async_copy(down_hbm, down, load_sem.at[2]),
        pltpu.make_async_copy(ctx_ref, ctx_all.at[x], load_sem.at[3]),
        pltpu.make_async_copy(side_ref.at[x], side_all.at[x], load_sem.at[4]),
    ]
    for load in loads:
        load.start()
    pl.semaphore_wait(barrier, len(peers))

    pending = []

    def send(source, target, index, device):
        made = copy(source, target, index, device)
        made.start()
        pending.append(made)
        return made

    ctx_r = send(ctx_ref, ctx_all.at[x], CTX_R, x_dev(1))
    ctx_l = send(ctx_ref, ctx_all.at[x], CTX_L, x_dev(3))
    sides = []
    for step in (1, 2, 3):
        there = (x + step) % NX
        sides.append(send(side_ref.at[there], side_all.at[x], SIDE + step - 1, x_dev(step)))
    from_l, from_r = (x + 3) % NX, (x + 1) % NX
    ctx_r.wait_recv()
    low, high = pl.ds(0, D // 2), pl.ds(D // 2, D // 2)
    fwd_r = send(
        ctx_all.at[from_l, :, low], ctx_all.at[from_l, :, low], CTX_FR, x_dev(1)
    )
    ctx_l.wait_recv()
    fwd_l = send(
        ctx_all.at[from_r, :, high], ctx_all.at[from_r, :, high], CTX_FL, x_dev(3)
    )
    loads[0].wait()
    loads[3].wait()
    loads[4].wait()
    for side in sides:
        side.wait_recv()
    fwd_r.wait_recv()
    fwd_l.wait_recv()

    context = ctx_all[...].reshape(NX * 2 * DEV_ROWS, D)
    first = jnp.dot(context, proj[0:D, :], preferred_element_type=F32)
    second = jnp.dot(context, proj[D : 2 * D, :], preferred_element_type=F32)
    for g in range(NX):
        base = g * 2 * DEV_ROWS
        block = first[base : base + DEV_ROWS] + second[base + DEV_ROWS : base + 2 * DEV_ROWS]
        residual = side_all[g, 0:32, :].astype(F32)[0:DEV_ROWS]
        attended[g * DEV_ROWS : (g + 1) * DEV_ROWS, :] = (
            (residual + block).astype(BF16).astype(F32)
        )
    att = attended[...]
    total = jnp.sum(att * att, axis=1, keepdims=True)
    squares[x] = jnp.broadcast_to(total, (COL_ROWS, 128))
    shares = [
        send(squares.at[x], squares.at[x], SQUARES + step - 1, x_dev(step)) for step in (1, 2, 3)
    ]
    meta = (
        side_all[0, 32:48, 0:HALF].astype(F32)
        + side_all[1, 32:48, 0:HALF].astype(F32)
        + side_all[2, 32:48, 0:HALF].astype(F32)
        + side_all[3, 32:48, 0:HALF].astype(F32)
    )
    rows_a[core, y, z, COL_ROWS : COL_ROWS + 16, :] = meta.astype(BF16)
    for share in shares:
        share.wait_recv()
    total = squares[0][:, 0:1] + squares[1][:, 0:1] + squares[2][:, 0:1] + squares[3][:, 0:1]
    normed = (att * lax.rsqrt(total / D + epsilon) * gain_ref[...]).astype(BF16)
    rows_a[core, y, z, 0:COL_ROWS, :] = normed[:, 0:HALF]
    rows_b[core, z, y] = normed[:, HALF:DQ]

    def own_a(where):
        return rows_a.at[core, y, where]

    b_right = send(rows_b.at[core, z, y], rows_b.at[core, z, y], B_Y, y_dev(1))
    b_left = send(rows_b.at[core, z, y], rows_b.at[core, z, y], B_Y + 1, y_dev(3))
    a_right = [send(own_a(z), own_a(z), A_RING_R, z_dev(1))]
    a_left = [send(own_a(z), own_a(z), A_RING_L, z_dev(7))]
    a_over = []

    def a_out(where, number):
        a_over.append(send(own_a(where), own_a(where), A_Y + 2 * number, y_dev(1)))
        a_over.append(send(own_a(where), own_a(where), A_Y + 2 * number + 1, y_dev(3)))

    a_out(z, 0)
    y_l, y_r = (y + 3) % NY, (y + 1) % NY
    top, bottom = pl.ds(0, 48), pl.ds(48, 48)
    b_right.wait_recv()
    b_fr = send(rows_b.at[core, z, y_l, top], rows_b.at[core, z, y_l, top], B_Y + 2, y_dev(1))
    b_left.wait_recv()
    b_fl = send(
        rows_b.at[core, z, y_r, bottom], rows_b.at[core, z, y_r, bottom], B_Y + 3, y_dev(3)
    )
    a_right[0].wait_recv()
    left = (z + 7) % NZ
    a_right.append(send(own_a(left), own_a(left), A_RING_R + 1, z_dev(1)))
    a_out(left, 1)
    a_left[0].wait_recv()
    right = (z + 1) % NZ
    a_left.append(send(own_a(right), own_a(right), A_RING_L + 1, z_dev(7)))
    a_out(right, 2)
    b_fr.wait_recv()
    b_fl.wait_recv()
    b_slab = rows_b.at[core, z]
    z_right = [send(b_slab, b_slab, B_RING_R, z_dev(1))]
    z_left = [send(b_slab, b_slab, B_RING_L, z_dev(7))]
    core_copies = [send(b_slab, b_slab, CORE_B, partner)]
    number = 3
    for step in (2, 3, 4):
        a_right[step - 1].wait_recv()
        left = (z + NZ - step) % NZ
        if step < 4:
            a_right.append(send(own_a(left), own_a(left), A_RING_R + step, z_dev(1)))
        a_out(left, number)
        number += 1
        if step < 4:
            a_left[step - 1].wait_recv()
            right = (z + step) % NZ
            if step < 3:
                a_left.append(send(own_a(right), own_a(right), A_RING_L + step, z_dev(7)))
            a_out(right, number)
            number += 1
    core_copies.append(send(rows_a.at[core, y], rows_a.at[core, y], CORE_A, partner))

    def a_relay(number, where):
        a_over[2 * number].wait_recv()
        a_over[2 * number + 1].wait_recv()
        if number % 2 == 0:
            block = rows_a.at[core, y_l, where]
            return send(block, block, A_RELAY + number, y_dev(1))
        block = rows_a.at[core, y_r, where]
        return send(block, block, A_RELAY + number, y_dev(3))

    order = [z, (z + 7) % NZ, (z + 1) % NZ, (z + 6) % NZ, (z + 2) % NZ, (z + 5) % NZ]
    order += [(z + 3) % NZ, (z + 4) % NZ]
    relays = []
    for step in (1, 2, 3, 4):
        z_right[step - 1].wait_recv()
        slab = rows_b.at[core, (z + NZ - step) % NZ]
        if step < 4:
            z_right.append(send(slab, slab, B_RING_R + step, z_dev(1)))
        core_copies.append(send(slab, slab, CORE_B + 2 * step - 1, partner))
        for number in (2 * step - 2, 2 * step - 1):
            relays.append(a_relay(number, order[number]))
        if step < 4:
            z_left[step - 1].wait_recv()
            slab = rows_b.at[core, (z + step) % NZ]
            if step < 3:
                z_left.append(send(slab, slab, B_RING_L + step, z_dev(7)))
            core_copies.append(send(slab, slab, CORE_B + 2 * step, partner))
    for there, number in ((y_l, 1), (y_r, 2)):
        slab = rows_a.at[core, there]
        core_copies.append(send(slab, slab, CORE_A + number, partner))
    for relay in relays:
        relay.wait_recv()
    slab = rows_a.at[core, (y + 2) % NY]
    core_copies.append(send(slab, slab, CORE_A + 3, partner))
    for made in core_copies:
        made.wait_recv()
    loads[1].wait()
    loads[2].wait()

    opposite = (x + 2) % NX
    lower, upper = pl.ds(0, FF), pl.ds(FF, FF)

    def chunk_of(k):
        odd = k % 2
        return (z + NZ + (1 - odd) * (4 - k // 2) + odd * (k // 2 - 3)) % NZ

    def first_copies(k):
        return (
            copy(partial.at[k, opposite, :, lower], first_in.at[k, 0], S1_R + k, x_dev(1)),
            copy(partial.at[k, opposite, :, upper], first_in.at[k, 1], S1_L + k, x_dev(3)),
        )

    def second_copies(k):
        return (
            copy(partial.at[k, from_r], second_in.at[k, 0], S2_R + k, x_dev(1)),
            copy(partial.at[k, from_l], second_in.at[k, 1], S2_L + k, x_dev(3)),
        )

    def hidden_copies(k):
        return (
            copy(hidden.at[k, x], hidden.at[k, x], H1_R + k, x_dev(1)),
            copy(hidden.at[k, x], hidden.at[k, x], H1_L + k, x_dev(3)),
        )

    near, far = pl.ds(0, FF // 2), pl.ds(FF // 2, FF // 2)

    def forward_copies(k):
        return (
            copy(hidden.at[k, from_l, :, near], hidden.at[k, from_l, :, near], H2_R + k, x_dev(1)),
            copy(hidden.at[k, from_r, :, far], hidden.at[k, from_r, :, far], H2_L + k, x_dev(3)),
        )

    def core_copy(k):
        return copy(mixed.at[k, 1 - core], core_in.at[k], CORE_MIX + k, partner)

    def chain_right(k):
        return copy(chain_out.at[k], chain_in.at[k], CHAIN + k, z_dev(1))

    def chain_left(k):
        return copy(chain_out.at[k], chain_in.at[k], CHAIN + k, z_dev(7))

    row_iota = lax.broadcasted_iota(jnp.int32, (COL_ROWS, COL_ROWS), 0)
    lane_iota = lax.broadcasted_iota(jnp.int32, (COL_ROWS, COL_ROWS), 1)
    earlier = (row_iota < lane_iota).astype(F32).astype(BF16)
    place = lax.broadcasted_iota(jnp.int32, (SPAN, COL_ROWS), 0).astype(F32)

    def pick_and_multiply(k):
        g = chunk_of(k)
        for column in range(2 * NY):
            cy, cc = column // 2, column % 2
            meta = rows_a[cc, cy, g, COL_ROWS : COL_ROWS + 16, :].astype(F32)[:, 0:COL_ROWS]
            ids, weights = meta[0:TOPK], meta[TOPK : 2 * TOPK]
            scale = 1.0 / jnp.sum(weights, axis=0, keepdims=True)
            named, share = [], []
            for j in range(SLOTS_DEV):
                same = (ids == table_ref[j : j + 1, 0:COL_ROWS]).astype(F32)
                named.append(jnp.sum(same, axis=0, keepdims=True))
                share.append(jnp.sum(same * weights, axis=0, keepdims=True) * scale)
            padded = jnp.concatenate(
                named + [jnp.zeros((SPAN - SLOTS_DEV, COL_ROWS), F32)], axis=0
            )
            ranks = jnp.dot(padded.astype(BF16), earlier, preferred_element_type=F32)
            chosen, weighted = [], []
            for j in range(SLOTS_DEV):
                rank = ranks[j : j + 1]
                twice = table_ref[3 + j : 4 + j, 0:COL_ROWS]
                parity = table_ref[6 + j : 7 + j, 0:COL_ROWS]
                halved = jnp.floor(rank * 0.5)
                where = jnp.where(twice > 0.5, halved, rank)
                odd = rank - 2.0 * halved
                good = (named[j] > 0.5) & ((twice < 0.5) | (odd == parity))
                key = jnp.where(good, where, -1.0)
                pick = (jnp.broadcast_to(key, (SPAN, COL_ROWS)) == place).astype(F32)
                chosen.append(pick)
                weighted.append(pick * share[j])
            pick = jnp.concatenate(chosen, axis=0).astype(BF16)
            picks[k % 8, column] = jnp.concatenate(weighted, axis=0)
            got_a = jnp.dot(pick, rows_a[cc, cy, g, 0:COL_ROWS, :], preferred_element_type=F32)
            got_b = jnp.dot(pick, rows_b[cc, g, cy], preferred_element_type=F32)
            for j in range(SLOTS_DEV):
                span = slice(j * SPAN, (j + 1) * SPAN)
                picked[j, column * SPAN : (column + 1) * SPAN, 0:HALF] = got_a[span]
                picked[j, column * SPAN : (column + 1) * SPAN, HALF:DQ] = got_b[span]
        for j in range(SLOTS_DEV):
            inputs = picked[j].astype(BF16)
            for part in range(3):
                lanes = slice(part * DQ, (part + 1) * DQ)
                product = jnp.dot(inputs, gate_up[j, :, lanes], preferred_element_type=F32)
                product = product.astype(BF16)
                for o in range(NX):
                    partial[k, o, j * 16 : (j + 1) * 16, lanes] = product[o * 16 : (o + 1) * 16]
        for made in first_copies(k):
            made.start()

    def add_first(k):
        for made in first_copies(k):
            made.wait_recv()
        partial[k, from_r, :, 0:FF] = (
            partial[k, from_r, :, 0:FF].astype(F32) + first_in[k, 0].astype(F32)
        ).astype(BF16)
        partial[k, from_l, :, FF : 2 * FF] = (
            partial[k, from_l, :, FF : 2 * FF].astype(F32) + first_in[k, 1].astype(F32)
        ).astype(BF16)
        for made in second_copies(k):
            made.start()

    def add_second(k):
        for made in second_copies(k):
            made.wait_recv()
        summed = (
            partial[k, x].astype(F32) + second_in[k, 0].astype(F32) + second_in[k, 1].astype(F32)
        )
        gate, up = summed[:, 0:FF], summed[:, FF : 2 * FF]
        hidden[k, x] = (gate / (1.0 + jnp.exp(-gate)) * up).astype(BF16)
        for made in hidden_copies(k):
            made.start()

    def pass_hidden(k):
        for made in hidden_copies(k):
            made.wait_recv()
        for made in forward_copies(k):
            made.start()

    def mix(k):
        for made in forward_copies(k):
            made.wait_recv()
        for j in range(SLOTS_DEV):
            inputs = hidden[k, :, j * 16 : (j + 1) * 16, :].reshape(NX * 16, FF)
            product = jnp.dot(inputs, down[j], preferred_element_type=F32)
            expert_out[j] = product.astype(BF16).astype(F32)
        for column in range(2 * NY):
            cy, cc = column // 2, column % 2
            span = slice(column * SPAN, (column + 1) * SPAN)
            results = jnp.concatenate([expert_out[j, span] for j in range(SLOTS_DEV)], axis=0)
            mixture = lax.dot_general(
                picks[k % 8, column].astype(BF16),
                results.astype(BF16),
                (((0,), (0,)), ((), ())),
                preferred_element_type=F32,
            )
            mixed[k, cc, cy] = mixture.astype(BF16)
        core_copy(k).start()

    def chain(k):
        core_copy(k).wait_recv()

        @pl.when(k < 2)
        def _():
            chain_out[k] = (mixed[k, core].astype(F32) + core_in[k].astype(F32)).astype(BF16)

        @pl.when((k >= 2) & (k < NZ - 1))
        def _():
            chain_right(k - 2).wait_recv()
            chain_out[k] = (
                mixed[k, core].astype(F32) + core_in[k].astype(F32) + chain_in[k - 2].astype(F32)
            ).astype(BF16)

        @pl.when((k < NZ - 1) & (k % 2 == 0))
        def _():
            chain_right(k).start()

        @pl.when((k < NZ - 1) & (k % 2 == 1))
        def _():
            chain_left(k).start()

    def tick(t, carry):
        for stage, work in ((5, chain), (4, mix), (3, pass_hidden), (2, add_second), (1, add_first)):
            pl.when((t >= stage) & (t < NZ + stage))(functools.partial(work, t - stage))
        pl.when(t < NZ)(functools.partial(pick_and_multiply, t))
        return carry

    lax.fori_loop(0, NZ + 6, tick, 0)

    last = NZ - 1
    chain_right(last - 2).wait_recv()
    chain_right(last - 1).wait_recv()
    for there in range(NY):
        y_part[there] = (
            mixed[last, core, there].astype(F32)
            + core_in[last, there].astype(F32)
            + chain_in[last - 2, there].astype(F32)
            + chain_in[last - 1, there].astype(F32)
        ).astype(BF16)
    y_far = (y + 2) % NY
    one_r = send(y_part.at[y_far, top], y_one.at[0], Y_ONE, y_dev(1))
    one_l = send(y_part.at[y_far, bottom], y_one.at[1], Y_ONE + 1, y_dev(3))
    one_r.wait_recv()
    y_part[y_r, 0:48, :] = (
        y_part[y_r, 0:48, :].astype(F32) + y_one[0].astype(F32)
    ).astype(BF16)
    two_r = send(y_part.at[y_r], y_two.at[0], Y_TWO, y_dev(1))
    one_l.wait_recv()
    y_part[y_l, 48:96, :] = (
        y_part[y_l, 48:96, :].astype(F32) + y_one[1].astype(F32)
    ).astype(BF16)
    two_l = send(y_part.at[y_l], y_two.at[1], Y_TWO + 1, y_dev(3))
    two_r.wait_recv()
    two_l.wait_recv()
    mixture = y_part[y].astype(F32) + y_two[0].astype(F32) + y_two[1].astype(F32)
    both = attended[...] + mixture
    for g in range(NX):
        span = slice(g * DEV_ROWS, (g + 1) * DEV_ROWS)
        final_out[g] = jnp.concatenate([mixture[span], both[span]], axis=0).astype(BF16)
    finals = []
    for step in (1, 2, 3):
        there = (x + step) % NX
        finals.append(send(final_out.at[there], final_in.at[x], FINAL + step - 1, x_dev(step)))
    final_in[x] = final_out[x]
    for made in finals:
        made.wait_recv()
    for g in range(NX):
        block = final_in[g].astype(F32)
        lanes = slice(g * DQ, (g + 1) * DQ)
        moe_ref[:, lanes] = block[0:DEV_ROWS].astype(BF16)
        layer_ref[:, lanes] = block[DEV_ROWS : 2 * DEV_ROWS].astype(BF16)

    def drain(k, carry):
        for made in (
            *first_copies(k),
            *second_copies(k),
            *hidden_copies(k),
            *forward_copies(k),
            core_copy(k),
        ):
            made.wait_send()

        @pl.when(k < NZ - 1)
        def _():
            chain_right(k).wait_send()

        return carry

    lax.fori_loop(0, NZ, drain, 0)
    for made in pending:
        made.wait_send()


def whole_layer(ctx, side, out_proj, gain, table, gate_up, down_proj):
    vmem = pl.BlockSpec(memory_space=pltpu.VMEM)
    hbm = pl.BlockSpec(memory_space=pl.ANY)
    return pl.pallas_call(
        layer_kernel,
        out_shape=(
            jax.ShapeDtypeStruct((DEV_ROWS, D), BF16),
            jax.ShapeDtypeStruct((DEV_ROWS, D), BF16),
        ),
        in_specs=[vmem, vmem, hbm, vmem, vmem, hbm, hbm],
        out_specs=(vmem, vmem),
        scratch_shapes=[
            pltpu.VMEM((NX, 2 * DEV_ROWS, D), BF16),
            pltpu.VMEM((NX, 48, DQ), BF16),
            pltpu.VMEM((2 * D, DQ), BF16),
            pltpu.VMEM((SLOTS_DEV, DQ, 2 * FF), BF16),
            pltpu.VMEM((SLOTS_DEV, FF, DQ), BF16),
            pltpu.VMEM((NX, COL_ROWS, 128), F32),
            pltpu.VMEM((COL_ROWS, DQ), F32),
            pltpu.VMEM((2, NY, NZ, COL_ROWS + 16, HALF), BF16),
            pltpu.VMEM((2, NZ, NY, COL_ROWS, HALF), BF16),
            pltpu.VMEM((NZ, 2 * NY, SLOTS_DEV * SPAN, COL_ROWS), F32),
            pltpu.VMEM((SLOTS_DEV, 2 * NY * SPAN, DQ), F32),
            pltpu.VMEM((NZ, NX, 48, 2 * FF), BF16),
            pltpu.VMEM((NZ, 2, 48, FF), BF16),
            pltpu.VMEM((NZ, 2, 48, 2 * FF), BF16),
            pltpu.VMEM((NZ, NX, 48, FF), BF16),
            pltpu.VMEM((SLOTS_DEV, 2 * NY * SPAN, DQ), F32),
            pltpu.VMEM((NZ, 2, NY, COL_ROWS, DQ), BF16),
            pltpu.VMEM((NZ, NY, COL_ROWS, DQ), BF16),
            pltpu.VMEM((NZ, NY, COL_ROWS, DQ), BF16),
            pltpu.VMEM((NZ, NY, COL_ROWS, DQ), BF16),
            pltpu.VMEM((NY, COL_ROWS, DQ), BF16),
            pltpu.VMEM((2, COL_ROWS // 2, DQ), BF16),
            pltpu.VMEM((2, COL_ROWS, DQ), BF16),
            pltpu.VMEM((NX, 48, DQ), BF16),
            pltpu.VMEM((NX, 48, DQ), BF16),
            pltpu.SemaphoreType.DMA((COPIES,)),
            pltpu.SemaphoreType.DMA((COPIES,)),
            pltpu.SemaphoreType.DMA((5,)),
        ],
        compiler_params=pltpu.CompilerParams(
            collective_id=0, has_side_effects=True, vmem_limit_bytes=67043328
        ),
    )(ctx, side, out_proj, gain, table, gate_up, down_proj)


def local(
    queries,
    new_keys,
    new_values,
    key_cache,
    value_cache,
    cache_len,
    residual,
    out_proj,
    norm_gain,
    expert_ids,
    route_weights,
    slot_expert,
    gate_up,
    down_proj,
):
    x = lax.axis_index("grp")
    ep = lax.axis_index("ep")
    context = jnp.concatenate(
        [
            prefill_context(queries, new_keys, new_values),
            decode_context(queries, new_keys, new_values, key_cache, value_cache, cache_len),
        ],
        axis=0,
    )
    ctx = jnp.concatenate([context[:, :D], context[:, D:]], axis=0)
    lane = jnp.arange(HALF)[None, :] - x * DEV_ROWS
    spread = (lane == jnp.arange(DEV_ROWS)[:, None]).astype(BF16)
    both = jnp.concatenate([(expert_ids + 1).astype(BF16), route_weights], axis=1)
    meta = lax.dot_general(
        both, spread, (((0,), (0,)), ((), ())), preferred_element_type=F32
    ).astype(BF16)
    quarters = residual.reshape(DEV_ROWS, NX, DQ).transpose(1, 0, 2)
    quarters = jnp.pad(quarters, ((0, 0), (0, 8), (0, 0)))
    meta = jnp.broadcast_to(jnp.pad(meta, ((0, 0), (0, DQ - HALF)))[None], (NX, 16, DQ))
    side = jnp.concatenate([quarters, meta], axis=1)
    place = ep * SLOTS_DEV + jnp.arange(SLOTS_DEV)
    mine = lax.dynamic_slice_in_dim(slot_expert, ep * SLOTS_DEV, SLOTS_DEV)
    same = slot_expert[None, :] == mine[:, None]
    twice = jnp.sum(same, axis=1) > 1
    earlier = jnp.sum(same & (jnp.arange(slot_expert.shape[0])[None, :] < place[:, None]), axis=1)
    table = jnp.concatenate([mine + 1, twice.astype(jnp.int32), earlier, jnp.zeros((7,), jnp.int32)])
    table = jnp.broadcast_to(table.astype(F32)[:, None], (16, 128))
    return whole_layer(ctx, side, out_proj, norm_gain[None, :], table, gate_up, down_proj)


def solution(mesh):
    placed = (
        P(("grp", "ep"), None),
        P(("grp", "ep"), None),
        P(("grp", "ep"), None),
        P(("grp", "ep"), None, None),
        P(("grp", "ep"), None, None),
        P(("grp", "ep")),
        P(("grp", "ep"), None),
        P(None, "grp"),
        P("grp"),
        P(("grp", "ep"), None),
        P(("grp", "ep"), None),
        P(),
        P("ep", "grp", None),
        P("ep", None, "grp"),
    )
    return jax.shard_map(
        local,
        mesh=mesh,
        in_specs=placed,
        out_specs=(P(("grp", "ep"), None), P(("grp", "ep"), None)),
        check_vma=False,
    )
```

```python
import functools
import math

import jax
import jax.numpy as jnp
from jax import lax
from jax.experimental import pallas as pl
from jax.experimental.pallas import tpu as pltpu
from jax.sharding import PartitionSpec as P

D = 2048
HEADS = 32
KV_HEADS = 4
HEAD_DIM = 128
FF = 768
TOPK = 8
SLOTS_DEV = 3
PRE = 8
DEV_ROWS = 24
COL_ROWS = 96
DQ = 512
HALF = 256
NX = 4
NY = 4
NZ = 8
SPAN = 8

MESH = pl.DeviceIdType.MESH
F32 = jnp.float32
BF16 = jnp.bfloat16

masked_score = -1e30
epsilon = 1e-06


def prefill_context(queries, new_keys, new_values):
    head_group = HEADS // KV_HEADS
    scaling = 1.0 / math.sqrt(HEAD_DIM)
    query_pre = queries[:PRE].reshape(PRE, KV_HEADS, head_group, HEAD_DIM)
    keys_pre = new_keys[:PRE].reshape(PRE, KV_HEADS, HEAD_DIM)
    values_pre = new_values[:PRE].reshape(PRE, KV_HEADS, HEAD_DIM)
    scores = (
        jnp.einsum("ikgd,jkd->kgij", query_pre, keys_pre, preferred_element_type=jnp.float32)
        * scaling
    )
    causal = jnp.arange(PRE)[:, None] >= jnp.arange(PRE)[None, :]
    scores = jnp.where(causal, scores, masked_score)
    exponent = jnp.exp(scores - jnp.max(scores, axis=-1, keepdims=True))
    attn_probs = (exponent / jnp.sum(exponent, axis=-1, keepdims=True)).astype(jnp.bfloat16)
    mixed_values = jnp.einsum(
        "kgij,jkd->ikgd", attn_probs, values_pre, preferred_element_type=jnp.float32
    )
    return mixed_values.astype(jnp.bfloat16).reshape(PRE, HEADS * HEAD_DIM)


def decode_context(queries, new_keys, new_values, key_cache, value_cache, cache_len):
    requests = key_cache.shape[0]
    cache_slots = key_cache.shape[1]
    head_group = HEADS // KV_HEADS
    scaling = 1.0 / math.sqrt(HEAD_DIM)
    query_dec = queries[PRE:].reshape(requests, KV_HEADS, head_group, HEAD_DIM)
    keys_dec = new_keys[PRE:].reshape(requests, KV_HEADS, HEAD_DIM)
    values_dec = new_values[PRE:].reshape(requests, KV_HEADS, HEAD_DIM)
    cached_keys = key_cache.reshape(requests, cache_slots, KV_HEADS, HEAD_DIM)
    cached_values = value_cache.reshape(requests, cache_slots, KV_HEADS, HEAD_DIM)
    cache_scores = (
        jnp.einsum("nkgd,ntkd->nkgt", query_dec, cached_keys, preferred_element_type=jnp.float32)
        * scaling
    )
    own_score = (
        jnp.einsum("nkgd,nkd->nkg", query_dec, keys_dec, preferred_element_type=jnp.float32)
        * scaling
    )
    valid = jnp.arange(cache_slots)[None, :] < cache_len[:, None]
    cache_scores = jnp.where(valid[:, None, None, :], cache_scores, masked_score)
    top_score = jnp.maximum(jnp.max(cache_scores, axis=-1), own_score)
    cache_exp = jnp.exp(cache_scores - top_score[..., None])
    own_exp = jnp.exp(own_score - top_score)
    denominator = jnp.sum(cache_exp, axis=-1) + own_exp
    cache_probs = (cache_exp / denominator[..., None]).astype(jnp.bfloat16)
    own_probs = (own_exp / denominator).astype(jnp.bfloat16)
    mixed_values = jnp.einsum(
        "nkgt,ntkd->nkgd", cache_probs, cached_values, preferred_element_type=jnp.float32
    )
    mixed_values = (
        mixed_values
        + own_probs.astype(jnp.float32)[..., None] * values_dec.astype(jnp.float32)[:, :, None, :]
    )
    return mixed_values.astype(jnp.bfloat16).reshape(requests, HEADS * HEAD_DIM)


CTX_R, CTX_L, CTX_FR, CTX_FL = 0, 1, 2, 3
SIDE = 4
SQUARES = 7
RING_R, RING_L = 10, 14
OVER_R, OVER_L = 17, 25
RELAY = 33
CORE_ROW = 41
CORE_SLAB = 49
S1_R, S1_L, S2_R, S2_L = 52, 60, 68, 76
H1_R, H1_L, H2_R, H2_L = 84, 92, 100, 108
CORE_MIX = 116
CHAIN = 124
Y_SUM = 152
FINAL = 155
COPIES = 158

NEAR = (2, -1, 1, 0)
FAR = (4, -3, 3, -2)


def layer_kernel(
    ctx_ref,
    side_ref,
    out_proj_hbm,
    gain_ref,
    table_ref,
    gate_up_hbm,
    down_hbm,
    moe_ref,
    layer_ref,
    ctx_all,
    side_all,
    proj,
    gate_up,
    down,
    squares,
    attended,
    rows,
    picks,
    picked,
    partial,
    first_in,
    second_in,
    hidden,
    expert_out,
    mixed,
    core_in,
    chain_out,
    chain_in,
    z_sum,
    y_in,
    final_out,
    final_in,
    send_sem,
    recv_sem,
    load_sem,
):
    x = lax.axis_index("grp")
    ep = lax.axis_index("ep")
    core = ep % 2
    z = (ep // 2) % NZ
    y = ep // (2 * NZ)

    def x_dev(step):
        return ((x + step) % NX, ep)

    def y_dev(step):
        return (x, (((y + step) % NY) * NZ + z) * 2 + core)

    def z_dev(step):
        return (x, (y * NZ + (z + step) % NZ) * 2 + core)

    partner = (x, (y * NZ + z) * 2 + 1 - core)

    def copy(source, target, index, device):
        return pltpu.make_async_remote_copy(
            src_ref=source,
            dst_ref=target,
            send_sem=send_sem.at[index],
            recv_sem=recv_sem.at[index],
            device_id=device,
            device_id_type=MESH,
        )

    peers = [x_dev(1), x_dev(2), x_dev(3), y_dev(1), y_dev(2), y_dev(3), z_dev(1), z_dev(7), partner]
    barrier = pltpu.get_barrier_semaphore()
    for peer in peers:
        pl.semaphore_signal(barrier, inc=1, device_id=peer, device_id_type=MESH)

    loads = [
        pltpu.make_async_copy(out_proj_hbm, proj, load_sem.at[0]),
        pltpu.make_async_copy(gate_up_hbm, gate_up, load_sem.at[1]),
        pltpu.make_async_copy(down_hbm, down, load_sem.at[2]),
        pltpu.make_async_copy(ctx_ref, ctx_all.at[x], load_sem.at[3]),
        pltpu.make_async_copy(side_ref.at[x], side_all.at[x], load_sem.at[4]),
    ]
    for load in loads:
        load.start()
    pl.semaphore_wait(barrier, len(peers))

    pending = []

    def send(source, target, index, device):
        made = copy(source, target, index, device)
        made.start()
        pending.append(made)
        return made

    ctx_r = send(ctx_ref, ctx_all.at[x], CTX_R, x_dev(1))
    ctx_l = send(ctx_ref, ctx_all.at[x], CTX_L, x_dev(3))
    sides = []
    for step in (1, 2, 3):
        there = (x + step) % NX
        sides.append(send(side_ref.at[there], side_all.at[x], SIDE + step - 1, x_dev(step)))
    from_l, from_r = (x + 3) % NX, (x + 1) % NX
    ctx_r.wait_recv()
    low, high = pl.ds(0, D // 2), pl.ds(D // 2, D // 2)
    fwd_r = send(
        ctx_all.at[from_l, :, low], ctx_all.at[from_l, :, low], CTX_FR, x_dev(1)
    )
    ctx_l.wait_recv()
    fwd_l = send(
        ctx_all.at[from_r, :, high], ctx_all.at[from_r, :, high], CTX_FL, x_dev(3)
    )
    loads[0].wait()
    loads[3].wait()
    loads[4].wait()
    for side in sides:
        side.wait_recv()
    fwd_r.wait_recv()
    fwd_l.wait_recv()

    context = ctx_all[...].reshape(NX * 2 * DEV_ROWS, D)
    first = jnp.dot(context, proj[0:D, :], preferred_element_type=F32)
    second = jnp.dot(context, proj[D : 2 * D, :], preferred_element_type=F32)
    for g in range(NX):
        base = g * 2 * DEV_ROWS
        term = first[base : base + DEV_ROWS] + second[base + DEV_ROWS : base + 2 * DEV_ROWS]
        residual = side_all[g, 0:32, :].astype(F32)[0:DEV_ROWS]
        attended[g * DEV_ROWS : (g + 1) * DEV_ROWS, :] = (
            (residual + term).astype(BF16).astype(F32)
        )
    att = attended[...]
    total = jnp.sum(att * att, axis=1, keepdims=True)
    squares[x] = jnp.broadcast_to(total, (COL_ROWS, 128))
    shares = [
        send(squares.at[x], squares.at[x], SQUARES + step - 1, x_dev(step)) for step in (1, 2, 3)
    ]
    meta = (
        side_all[0, 32:48, 0:HALF].astype(F32)
        + side_all[1, 32:48, 0:HALF].astype(F32)
        + side_all[2, 32:48, 0:HALF].astype(F32)
        + side_all[3, 32:48, 0:HALF].astype(F32)
    )
    rows[core, y, z, COL_ROWS : COL_ROWS + 16, 0:HALF] = meta.astype(BF16)
    rows[core, y, z, COL_ROWS : COL_ROWS + 16, HALF:DQ] = jnp.zeros((16, HALF), BF16)
    for share in shares:
        share.wait_recv()
    total = squares[0][:, 0:1] + squares[1][:, 0:1] + squares[2][:, 0:1] + squares[3][:, 0:1]
    normed = (att * lax.rsqrt(total / D + epsilon) * gain_ref[...]).astype(BF16)
    rows[core, y, z, 0:COL_ROWS, :] = normed
    loads[1].wait()
    loads[2].wait()

    opposite = (x + 2) % NX
    lower, upper = pl.ds(0, FF), pl.ds(FF, FF)

    def group_of(k):
        u = k // 2
        return (y + u + 2 * (u % 2) * (1 - u // 2) - u // 2) % NY

    def z_of(k, o):
        near = (k + 1 - (k // 2 + 3) // 4) % 2
        return (z + NZ + near * NEAR[o] + (1 - near) * FAR[o]) % NZ

    def first_copies(k):
        return (
            copy(partial.at[k, opposite, :, lower], first_in.at[k, 0], S1_R + k, x_dev(1)),
            copy(partial.at[k, opposite, :, upper], first_in.at[k, 1], S1_L + k, x_dev(3)),
        )

    def second_copies(k):
        return (
            copy(partial.at[k, from_r], second_in.at[k, 0], S2_R + k, x_dev(1)),
            copy(partial.at[k, from_l], second_in.at[k, 1], S2_L + k, x_dev(3)),
        )

    def hidden_copies(k):
        return (
            copy(hidden.at[k, x], hidden.at[k, x], H1_R + k, x_dev(1)),
            copy(hidden.at[k, x], hidden.at[k, x], H1_L + k, x_dev(3)),
        )

    near, far = pl.ds(0, FF // 2), pl.ds(FF // 2, FF // 2)

    def forward_copies(k):
        return (
            copy(hidden.at[k, from_l, :, near], hidden.at[k, from_l, :, near], H2_R + k, x_dev(1)),
            copy(hidden.at[k, from_r, :, far], hidden.at[k, from_r, :, far], H2_L + k, x_dev(3)),
        )

    def core_copy(k):
        return copy(mixed.at[k, 1 - core], core_in.at[k], CORE_MIX + k, partner)

    row_iota = lax.broadcasted_iota(jnp.int32, (COL_ROWS, COL_ROWS), 0)
    lane_iota = lax.broadcasted_iota(jnp.int32, (COL_ROWS, COL_ROWS), 1)
    earlier = (row_iota < lane_iota).astype(F32).astype(BF16)
    place = lax.broadcasted_iota(jnp.int32, (SPAN, COL_ROWS), 0).astype(F32)

    def pick_and_multiply(k):
        group = group_of(k)
        for column in range(2 * NY):
            there, cc = z_of(k, column // 2), column % 2
            meta = rows[cc, group, there, COL_ROWS : COL_ROWS + 16, 0:128].astype(F32)
            meta = meta[:, 0:COL_ROWS]
            ids, weights = meta[0:TOPK], meta[TOPK : 2 * TOPK]
            scale = 1.0 / jnp.sum(weights, axis=0, keepdims=True)
            named, share = [], []
            for j in range(SLOTS_DEV):
                same = (ids == table_ref[j : j + 1, 0:COL_ROWS]).astype(F32)
                named.append(jnp.sum(same, axis=0, keepdims=True))
                share.append(jnp.sum(same * weights, axis=0, keepdims=True) * scale)
            padded = jnp.concatenate(
                named + [jnp.zeros((SPAN - SLOTS_DEV, COL_ROWS), F32)], axis=0
            )
            ranks = jnp.dot(padded.astype(BF16), earlier, preferred_element_type=F32)
            chosen, weighted = [], []
            for j in range(SLOTS_DEV):
                rank = ranks[j : j + 1]
                twice = table_ref[3 + j : 4 + j, 0:COL_ROWS]
                parity = table_ref[6 + j : 7 + j, 0:COL_ROWS]
                halved = jnp.floor(rank * 0.5)
                where = jnp.where(twice > 0.5, halved, rank)
                odd = rank - 2.0 * halved
                good = (named[j] > 0.5) & ((twice < 0.5) | (odd == parity))
                key = jnp.where(good, where, -1.0)
                pick = (jnp.broadcast_to(key, (SPAN, COL_ROWS)) == place).astype(F32)
                chosen.append(pick)
                weighted.append(pick * share[j])
            pick = jnp.concatenate(chosen, axis=0).astype(BF16)
            picks[k % 8, column] = jnp.concatenate(weighted, axis=0)
            got = jnp.dot(pick, rows[cc, group, there, 0:COL_ROWS, :], preferred_element_type=F32)
            for j in range(SLOTS_DEV):
                picked[j, column * SPAN : (column + 1) * SPAN, :] = got[j * SPAN : (j + 1) * SPAN]
        for j in range(SLOTS_DEV):
            inputs = picked[j].astype(BF16)
            for part in range(3):
                lanes = slice(part * DQ, (part + 1) * DQ)
                product = jnp.dot(inputs, gate_up[j, :, lanes], preferred_element_type=F32)
                product = product.astype(BF16)
                for o in range(NX):
                    partial[k, o, j * 16 : (j + 1) * 16, lanes] = product[o * 16 : (o + 1) * 16]
        for made in first_copies(k):
            made.start()

    def add_first(k):
        for made in first_copies(k):
            made.wait_recv()
        partial[k, from_r, :, 0:FF] = (
            partial[k, from_r, :, 0:FF].astype(F32) + first_in[k, 0].astype(F32)
        ).astype(BF16)
        partial[k, from_l, :, FF : 2 * FF] = (
            partial[k, from_l, :, FF : 2 * FF].astype(F32) + first_in[k, 1].astype(F32)
        ).astype(BF16)
        for made in second_copies(k):
            made.start()

    def add_second(k):
        for made in second_copies(k):
            made.wait_recv()
        summed = (
            partial[k, x].astype(F32) + second_in[k, 0].astype(F32) + second_in[k, 1].astype(F32)
        )
        gate, up = summed[:, 0:FF], summed[:, FF : 2 * FF]
        hidden[k, x] = (gate / (1.0 + jnp.exp(-gate)) * up).astype(BF16)
        for made in hidden_copies(k):
            made.start()

    def pass_hidden(k):
        for made in hidden_copies(k):
            made.wait_recv()
        for made in forward_copies(k):
            made.start()

    def mix(k):
        for made in forward_copies(k):
            made.wait_recv()
        for j in range(SLOTS_DEV):
            inputs = hidden[k, :, j * 16 : (j + 1) * 16, :].reshape(NX * 16, FF)
            product = jnp.dot(inputs, down[j], preferred_element_type=F32)
            expert_out[j] = product.astype(BF16).astype(F32)
        for column in range(2 * NY):
            cc = column % 2
            span = slice(column * SPAN, (column + 1) * SPAN)
            results = jnp.concatenate([expert_out[j, span] for j in range(SLOTS_DEV)], axis=0)
            mixture = lax.dot_general(
                picks[k % 8, column].astype(BF16),
                results.astype(BF16),
                (((0,), (0,)), ((), ())),
                preferred_element_type=F32,
            )
            mixed[k, cc, column // 2] = mixture.astype(BF16)
        core_copy(k).start()

    def chunk_with(group, offset):
        near = offset in NEAR
        index = (NEAR if near else FAR).index(offset)
        first_half = near if group == 0 else not near
        return 2 * group + (0 if first_half else 1), index

    def chain_copy(group, leg, step):
        index = leg * 4 + step
        device = z_dev(1) if leg == 0 else z_dev(7)
        return copy(
            chain_out.at[group, index],
            chain_in.at[group, index],
            CHAIN + 7 * group + index,
            device,
        )

    def block(group, offset):
        k, index = chunk_with(group, offset)
        return mixed[k, core, index].astype(F32) + core_in[k, index].astype(F32)

    def chain(group, step):
        for leg, offset in ((0, 4 - step), (1, step - 3)):
            if offset == 0:
                continue
            value = block(group, offset)
            if step > 0:
                chain_copy(group, leg, step - 1).wait_recv()
                value = value + chain_in[group, leg * 4 + step - 1].astype(F32)
            chain_out[group, leg * 4 + step] = value.astype(BF16)
            chain_copy(group, leg, step).start()

    def y_copy(group):
        step = (0, 3, 1, 2)[group]
        return copy(z_sum.at[group], y_in.at[group - 1], Y_SUM + group - 1, y_dev(step))

    def close(group):
        chain_copy(group, 1, 2).wait_recv()
        chain_copy(group, 0, 3).wait_recv()
        value = block(group, 0)
        value = value + chain_in[group, 3].astype(F32) + chain_in[group, 6].astype(F32)
        z_sum[group] = value.astype(BF16)
        if group > 0:
            y_copy(group).start()

    y_l, y_r = (y + 3) % NY, (y + 1) % NY

    def own_row(where):
        return rows.at[core, y, where % NZ]

    def ring(leg, step):
        where, device = (z + NZ - step, z_dev(1)) if leg == 0 else (z + step, z_dev(7))
        index = (RING_R if leg == 0 else RING_L) + step
        return copy(own_row(where), own_row(where), index, device)

    arrivals = (0, -1, 1, -2, 2, -3, 3, 4)

    def over(number, leg):
        block_ref = own_row(z + NZ + arrivals[number])
        index = (OVER_R if leg == 0 else OVER_L) + number
        return copy(block_ref, block_ref, index, y_dev(1) if leg == 0 else y_dev(3))

    def relay(number):
        where = (z + NZ + arrivals[number]) % NZ
        block_ref = rows.at[core, y_l if number % 2 == 0 else y_r, where]
        return copy(block_ref, block_ref, RELAY + number, y_dev(1) if number % 2 == 0 else y_dev(3))

    def core_row(number):
        block_ref = own_row(z + NZ + arrivals[number])
        return copy(block_ref, block_ref, CORE_ROW + number, partner)

    def core_slab(group):
        slab = rows.at[core, (y + (0, 3, 1, 2)[group]) % NY]
        return copy(slab, slab, CORE_SLAB + group - 1, partner)

    def spread(number):
        core_row(number).start()
        over(number, 0).start()
        over(number, 1).start()

    ring(0, 0).start()
    ring(1, 0).start()
    spread(0)
    for step in (1, 2):
        ring(1, step - 1).wait_recv()
        if step < 3:
            ring(1, step).start()
        spread(2 * step)
        ring(0, step - 1).wait_recv()
        ring(0, step).start()
        spread(2 * step - 1)
    for number in (0, 1, 2, 4):
        core_row(number).wait_recv()
    pick_and_multiply(0)
    ring(1, 2).wait_recv()
    spread(6)
    ring(0, 2).wait_recv()
    ring(0, 3).start()
    spread(5)
    ring(0, 3).wait_recv()
    spread(7)

    def receive_left():
        for number in range(NZ):
            over(number, 0).wait_recv()
            if number % 2 == 0:
                relay(number).start()
        core_slab(1).start()

    def receive_right():
        for number in range(NZ):
            over(number, 1).wait_recv()
            if number % 2 == 1:
                relay(number).start()
        core_slab(2).start()

    def receive_far():
        for number in range(NZ):
            relay(number).wait_recv()
        core_slab(3).start()

    events = {
        1: [receive_left],
        2: [receive_right],
        4: [receive_far],
    }
    ready = {
        1: [functools.partial(lambda n: core_row(n).wait_recv(), n) for n in (3, 5, 6, 7)],
        2: [lambda: core_slab(1).wait_recv()],
        4: [lambda: core_slab(2).wait_recv()],
        6: [lambda: core_slab(3).wait_recv()],
    }
    chains = {}
    for group in range(NY):
        start = 2 * group + 5 + (group == 0)
        for step in range(4):
            chains.setdefault(start + step, []).append(functools.partial(chain, group, step))
        chains.setdefault(start + 4, []).append(functools.partial(close, group))

    def at(t, table):
        for when, works in table.items():

            @pl.when(t == when)
            def _(works=works):
                for work in works:
                    work()

    def core_arrived(k):
        core_copy(k).wait_recv()

    def tick(t, carry):
        pl.when((t >= 5) & (t < NZ + 5))(functools.partial(core_arrived, t - 5))
        at(t, chains)
        for stage, work in ((4, mix), (3, pass_hidden), (2, add_second), (1, add_first)):
            pl.when((t >= stage) & (t < NZ + stage))(functools.partial(work, t - stage))
        at(t, ready)
        pl.when(t < NZ)(functools.partial(pick_and_multiply, t))
        at(t, events)
        return carry

    lax.fori_loop(1, max(chains) + 1, tick, 0)

    for group in range(1, NY):
        y_copy(group).wait_recv()
    mixture = z_sum[0].astype(F32)
    for group in range(1, NY):
        mixture = mixture + y_in[group - 1].astype(F32)
    both = attended[...] + mixture
    for g in range(NX):
        span = slice(g * DEV_ROWS, (g + 1) * DEV_ROWS)
        final_out[g] = jnp.concatenate([mixture[span], both[span]], axis=0).astype(BF16)
    finals = []
    for step in (1, 2, 3):
        there = (x + step) % NX
        finals.append(send(final_out.at[there], final_in.at[x], FINAL + step - 1, x_dev(step)))
    final_in[x] = final_out[x]
    for made in finals:
        made.wait_recv()
    for g in range(NX):
        ended = final_in[g].astype(F32)
        lanes = slice(g * DQ, (g + 1) * DQ)
        moe_ref[:, lanes] = ended[0:DEV_ROWS].astype(BF16)
        layer_ref[:, lanes] = ended[DEV_ROWS : 2 * DEV_ROWS].astype(BF16)

    def drain(k, carry):
        for made in (
            *first_copies(k),
            *second_copies(k),
            *hidden_copies(k),
            *forward_copies(k),
            core_copy(k),
        ):
            made.wait_send()

        return carry

    lax.fori_loop(0, NZ, drain, 0)
    for step in range(4):
        ring(0, step).wait_send()
        if step < 3:
            ring(1, step).wait_send()
    for number in range(NZ):
        for made in (over(number, 0), over(number, 1), relay(number), core_row(number)):
            made.wait_send()
    for group in range(NY):
        for step in range(4):
            chain_copy(group, 0, step).wait_send()
            if step < 3:
                chain_copy(group, 1, step).wait_send()
        if group > 0:
            core_slab(group).wait_send()
            y_copy(group).wait_send()
    for made in pending:
        made.wait_send()


def whole_layer(ctx, side, out_proj, gain, table, gate_up, down_proj):
    vmem = pl.BlockSpec(memory_space=pltpu.VMEM)
    hbm = pl.BlockSpec(memory_space=pl.ANY)
    return pl.pallas_call(
        layer_kernel,
        out_shape=(
            jax.ShapeDtypeStruct((DEV_ROWS, D), BF16),
            jax.ShapeDtypeStruct((DEV_ROWS, D), BF16),
        ),
        in_specs=[vmem, vmem, hbm, vmem, vmem, hbm, hbm],
        out_specs=(vmem, vmem),
        scratch_shapes=[
            pltpu.VMEM((NX, 2 * DEV_ROWS, D), BF16),
            pltpu.VMEM((NX, 48, DQ), BF16),
            pltpu.VMEM((2 * D, DQ), BF16),
            pltpu.VMEM((SLOTS_DEV, DQ, 2 * FF), BF16),
            pltpu.VMEM((SLOTS_DEV, FF, DQ), BF16),
            pltpu.VMEM((NX, COL_ROWS, 128), F32),
            pltpu.VMEM((COL_ROWS, DQ), F32),
            pltpu.VMEM((2, NY, NZ, COL_ROWS + 16, DQ), BF16),
            pltpu.VMEM((NZ, 2 * NY, SLOTS_DEV * SPAN, COL_ROWS), F32),
            pltpu.VMEM((SLOTS_DEV, 2 * NY * SPAN, DQ), F32),
            pltpu.VMEM((NZ, NX, 48, 2 * FF), BF16),
            pltpu.VMEM((NZ, 2, 48, FF), BF16),
            pltpu.VMEM((NZ, 2, 48, 2 * FF), BF16),
            pltpu.VMEM((NZ, NX, 48, FF), BF16),
            pltpu.VMEM((SLOTS_DEV, 2 * NY * SPAN, DQ), F32),
            pltpu.VMEM((NZ, 2, NY, COL_ROWS, DQ), BF16),
            pltpu.VMEM((NZ, NY, COL_ROWS, DQ), BF16),
            pltpu.VMEM((NY, 7, COL_ROWS, DQ), BF16),
            pltpu.VMEM((NY, 7, COL_ROWS, DQ), BF16),
            pltpu.VMEM((NY, COL_ROWS, DQ), BF16),
            pltpu.VMEM((NY - 1, COL_ROWS, DQ), BF16),
            pltpu.VMEM((NX, 48, DQ), BF16),
            pltpu.VMEM((NX, 48, DQ), BF16),
            pltpu.SemaphoreType.DMA((COPIES,)),
            pltpu.SemaphoreType.DMA((COPIES,)),
            pltpu.SemaphoreType.DMA((5,)),
        ],
        compiler_params=pltpu.CompilerParams(
            collective_id=0, has_side_effects=True, vmem_limit_bytes=67043328
        ),
    )(ctx, side, out_proj, gain, table, gate_up, down_proj)


def local(
    queries,
    new_keys,
    new_values,
    key_cache,
    value_cache,
    cache_len,
    residual,
    out_proj,
    norm_gain,
    expert_ids,
    route_weights,
    slot_expert,
    gate_up,
    down_proj,
):
    x = lax.axis_index("grp")
    ep = lax.axis_index("ep")
    context = jnp.concatenate(
        [
            prefill_context(queries, new_keys, new_values),
            decode_context(queries, new_keys, new_values, key_cache, value_cache, cache_len),
        ],
        axis=0,
    )
    ctx = jnp.concatenate([context[:, :D], context[:, D:]], axis=0)
    lane = jnp.arange(HALF)[None, :] - x * DEV_ROWS
    spread = (lane == jnp.arange(DEV_ROWS)[:, None]).astype(BF16)
    both = jnp.concatenate([(expert_ids + 1).astype(BF16), route_weights], axis=1)
    meta = lax.dot_general(
        both, spread, (((0,), (0,)), ((), ())), preferred_element_type=F32
    ).astype(BF16)
    quarters = residual.reshape(DEV_ROWS, NX, DQ).transpose(1, 0, 2)
    quarters = jnp.pad(quarters, ((0, 0), (0, 8), (0, 0)))
    meta = jnp.broadcast_to(jnp.pad(meta, ((0, 0), (0, DQ - HALF)))[None], (NX, 16, DQ))
    side = jnp.concatenate([quarters, meta], axis=1)
    place = ep * SLOTS_DEV + jnp.arange(SLOTS_DEV)
    mine = lax.dynamic_slice_in_dim(slot_expert, ep * SLOTS_DEV, SLOTS_DEV)
    same = slot_expert[None, :] == mine[:, None]
    twice = jnp.sum(same, axis=1) > 1
    earlier = jnp.sum(same & (jnp.arange(slot_expert.shape[0])[None, :] < place[:, None]), axis=1)
    table = jnp.concatenate([mine + 1, twice.astype(jnp.int32), earlier, jnp.zeros((7,), jnp.int32)])
    table = jnp.broadcast_to(table.astype(F32)[:, None], (16, 128))
    return whole_layer(ctx, side, out_proj, norm_gain[None, :], table, gate_up, down_proj)


def solution(mesh):
    placed = (
        P(("grp", "ep"), None),
        P(("grp", "ep"), None),
        P(("grp", "ep"), None),
        P(("grp", "ep"), None, None),
        P(("grp", "ep"), None, None),
        P(("grp", "ep")),
        P(("grp", "ep"), None),
        P(None, "grp"),
        P("grp"),
        P(("grp", "ep"), None),
        P(("grp", "ep"), None),
        P(),
        P("ep", "grp", None),
        P("ep", None, "grp"),
    )
    return jax.shard_map(
        local,
        mesh=mesh,
        in_specs=placed,
        out_specs=(P(("grp", "ep"), None), P(("grp", "ep"), None)),
        check_vma=False,
    )
```

```python
import functools
import math

import jax
import jax.numpy as jnp
from jax import lax
from jax.experimental import pallas as pl
from jax.experimental.pallas import tpu as pltpu
from jax.sharding import PartitionSpec as P

D = 2048
HEADS = 32
KV_HEADS = 4
HEAD_DIM = 128
FF = 768
TOPK = 8
SLOTS_DEV = 3
PRE = 8
DEV_ROWS = 24
COL_ROWS = 96
DQ = 512
HALF = 256
NX = 4
NY = 4
NZ = 8
SPAN = 8

MESH = pl.DeviceIdType.MESH
F32 = jnp.float32
BF16 = jnp.bfloat16

masked_score = -1e30
epsilon = 1e-06

CTX_R, CTX_L, CTX_FR, CTX_FL = 0, 1, 2, 3
SIDE = 4
SQUARES = 7
RING_R, RING_L = 10, 14
OVER_R, OVER_L = 17, 25
RELAY = 33
CORE_ROW = 41
CORE_SLAB = 49
S1_R, S1_L, S2_R, S2_L = 52, 60, 68, 76
H1_R, H1_L, H2_R, H2_L = 84, 92, 100, 108
CORE_MIX = 116
CHAIN = 124
Y_SUM = 152
FINAL = 155
COPIES = 158

NEAR = (2, -1, 1, 0)
FAR = (4, -3, 3, -2)


def layer_kernel(
    queries_hbm,
    new_keys_hbm,
    new_values_hbm,
    key_cache_hbm,
    value_cache_hbm,
    cache_len_ref,
    residual_hbm,
    out_proj_hbm,
    gain_ref,
    ids_ref,
    weights_ref,
    slots_ref,
    gate_up_hbm,
    down_hbm,
    moe_ref,
    layer_ref,
    queries,
    new_keys,
    new_values,
    key_cache,
    value_cache,
    residual,
    by_head,
    context_head,
    own_keys,
    own_values,
    table_ref,
    side_out,
    ctx_all,
    side_all,
    proj,
    gate_up,
    down,
    squares,
    attended,
    rows,
    picks,
    picked,
    partial,
    first_in,
    second_in,
    hidden,
    expert_out,
    mixed,
    core_in,
    chain_out,
    chain_in,
    z_sum,
    y_in,
    final_out,
    final_in,
    send_sem,
    recv_sem,
    load_sem,
):
    x = lax.axis_index("grp")
    ep = lax.axis_index("ep")
    core = ep % 2
    z = (ep // 2) % NZ
    y = ep // (2 * NZ)

    def x_dev(step):
        return ((x + step) % NX, ep)

    def y_dev(step):
        return (x, (((y + step) % NY) * NZ + z) * 2 + core)

    def z_dev(step):
        return (x, (y * NZ + (z + step) % NZ) * 2 + core)

    partner = (x, (y * NZ + z) * 2 + 1 - core)

    def copy(source, target, index, device):
        return pltpu.make_async_remote_copy(
            src_ref=source,
            dst_ref=target,
            send_sem=send_sem.at[index],
            recv_sem=recv_sem.at[index],
            device_id=device,
            device_id_type=MESH,
        )

    peers = [x_dev(1), x_dev(2), x_dev(3), y_dev(1), y_dev(2), y_dev(3), z_dev(1), z_dev(7), partner]
    barrier = pltpu.get_barrier_semaphore()
    for peer in peers:
        pl.semaphore_signal(barrier, inc=1, device_id=peer, device_id_type=MESH)

    early = [
        pltpu.make_async_copy(queries_hbm, queries, load_sem.at[0]),
        pltpu.make_async_copy(new_keys_hbm, new_keys, load_sem.at[1]),
        pltpu.make_async_copy(new_values_hbm, new_values, load_sem.at[2]),
        pltpu.make_async_copy(key_cache_hbm, key_cache, load_sem.at[3]),
        pltpu.make_async_copy(value_cache_hbm, value_cache, load_sem.at[4]),
        pltpu.make_async_copy(residual_hbm, residual, load_sem.at[5]),
    ]
    loads = [
        pltpu.make_async_copy(out_proj_hbm, proj, load_sem.at[6]),
        pltpu.make_async_copy(gate_up_hbm, gate_up, load_sem.at[7]),
        pltpu.make_async_copy(down_hbm, down, load_sem.at[8]),
    ]
    for load in early + loads:
        load.start()

    slots = slots_ref[...].astype(F32)
    slot_lane = lax.broadcasted_iota(jnp.int32, slots.shape, 1)
    for j in range(SLOTS_DEV):
        here = ep * SLOTS_DEV + j
        mine = jnp.sum(jnp.where(slot_lane == here, slots, 0.0), axis=1, keepdims=True)
        same = jnp.where(slots == mine, 1.0, 0.0)
        twice = jnp.sum(same, axis=1, keepdims=True) - 1.0
        before = jnp.sum(jnp.where(slot_lane < here, same, 0.0), axis=1, keepdims=True)
        for row, value in ((j, mine + 1.0), (3 + j, twice), (6 + j, before)):
            table_ref[row : row + 1, :] = jnp.broadcast_to(value, (1, 128))
    spread_row = lax.broadcasted_iota(jnp.int32, (DEV_ROWS, HALF), 0)
    spread_lane = lax.broadcasted_iota(jnp.int32, (DEV_ROWS, HALF), 1)
    to_lane = jnp.where(spread_lane == spread_row + x * DEV_ROWS, 1.0, 0.0).astype(BF16)
    routes = [
        lax.dot_general(
            value.astype(BF16), to_lane, (((0,), (0,)), ((), ())), preferred_element_type=F32
        )
        for value in (ids_ref[...].astype(F32) + 1.0, weights_ref[...].astype(F32))
    ]
    routes = jnp.concatenate(routes, axis=0).astype(BF16)
    for load in early:
        load.wait()
    for g in range(NX):
        side_out[g, 0:DEV_ROWS, :] = residual[:, g * DQ : (g + 1) * DQ]
        side_out[g, 32:48, 0:HALF] = routes

    own_keys[...] = new_keys[...].astype(F32)
    own_values[...] = new_values[...].astype(F32)
    for h in range(HEADS):
        by_head[pl.ds(h, DEV_ROWS, stride=HEADS), :] = queries[
            :, h * HEAD_DIM : (h + 1) * HEAD_DIM
        ].astype(F32)
    width = KV_HEADS * HEAD_DIM
    head_row = lax.broadcasted_iota(jnp.int32, (HEADS, width), 0)
    head_lane = lax.broadcasted_iota(jnp.int32, (HEADS, width), 1)
    same_head = head_row // (HEADS // KV_HEADS) == head_lane // HEAD_DIM
    scaling = 1.0 / math.sqrt(HEAD_DIM)

    def spread_query(row):
        query = by_head[pl.ds(row * HEADS, HEADS), :]
        return jnp.where(same_head, jnp.concatenate([query] * KV_HEADS, axis=1), 0.0)

    def join(mixed_values):
        mixed_values = jnp.where(same_head, mixed_values, 0.0)
        joined = mixed_values[:, 0:HEAD_DIM]
        for kv in range(1, KV_HEADS):
            joined = joined + mixed_values[:, kv * HEAD_DIM : (kv + 1) * HEAD_DIM]
        return joined

    def score(query, keys):
        return (
            lax.dot_general(
                query.astype(BF16), keys, (((1,), (1,)), ((), ())), preferred_element_type=F32
            )
            * scaling
        )

    def prefill_row(row):
        query = spread_query(row)
        scores = score(query, new_keys[0 : 2 * PRE, :])
        token = lax.broadcasted_iota(jnp.int32, scores.shape, 1)
        scores = jnp.where(token <= row, scores, masked_score)
        exponent = jnp.exp(scores - jnp.max(scores, axis=1, keepdims=True))
        probs = (exponent / jnp.sum(exponent, axis=1, keepdims=True)).astype(BF16)
        values = jnp.dot(probs, new_values[0 : 2 * PRE, :], preferred_element_type=F32)
        context_head[pl.ds(row * HEADS, HEADS), :] = join(values)

    def decode_row(request):
        row = PRE + request
        query = spread_query(row)
        scores = score(query, key_cache[request])
        token = lax.broadcasted_iota(jnp.int32, scores.shape, 1)
        scores = jnp.where(token < cache_len_ref[request], scores, masked_score)
        own = jnp.sum(query * own_keys[pl.ds(row, 1), :], axis=1, keepdims=True) * scaling
        top = jnp.maximum(jnp.max(scores, axis=1, keepdims=True), own)
        exponent = jnp.exp(scores - top)
        own_exp = jnp.exp(own - top)
        total = jnp.sum(exponent, axis=1, keepdims=True) + own_exp
        probs = (exponent / total).astype(BF16)
        own_prob = (own_exp / total).astype(BF16).astype(F32)
        values = jnp.dot(probs, value_cache[request], preferred_element_type=F32)
        values = values + own_prob * own_values[pl.ds(row, 1), :]
        context_head[pl.ds(row * HEADS, HEADS), :] = join(values)

    def four(work):
        def body(i, carry):
            for part in range(4):
                work(i * 4 + part)
            return carry

        return body

    lax.fori_loop(0, PRE // 4, four(prefill_row), 0)
    lax.fori_loop(0, (DEV_ROWS - PRE) // 4, four(decode_row), 0)
    for h in range(HEADS // 2):
        pair = [
            context_head[pl.ds(there, DEV_ROWS, stride=HEADS), :] for there in (h, h + HEADS // 2)
        ]
        ctx_all[x, :, h * HEAD_DIM : (h + 1) * HEAD_DIM] = jnp.concatenate(pair, axis=0).astype(
            BF16
        )
    side_all[x] = side_out[x]
    pl.semaphore_wait(barrier, len(peers))

    pending = []

    def send(source, target, index, device):
        made = copy(source, target, index, device)
        made.start()
        pending.append(made)
        return made

    ctx_r = send(ctx_all.at[x], ctx_all.at[x], CTX_R, x_dev(1))
    ctx_l = send(ctx_all.at[x], ctx_all.at[x], CTX_L, x_dev(3))
    sides = []
    for step in (1, 2, 3):
        there = (x + step) % NX
        sides.append(send(side_out.at[there], side_all.at[x], SIDE + step - 1, x_dev(step)))
    from_l, from_r = (x + 3) % NX, (x + 1) % NX
    ctx_r.wait_recv()
    low, high = pl.ds(0, D // 2), pl.ds(D // 2, D // 2)
    fwd_r = send(
        ctx_all.at[from_l, :, low], ctx_all.at[from_l, :, low], CTX_FR, x_dev(1)
    )
    ctx_l.wait_recv()
    fwd_l = send(
        ctx_all.at[from_r, :, high], ctx_all.at[from_r, :, high], CTX_FL, x_dev(3)
    )
    loads[0].wait()
    for side in sides:
        side.wait_recv()
    fwd_r.wait_recv()
    fwd_l.wait_recv()

    context = ctx_all[...].reshape(NX * 2 * DEV_ROWS, D)
    first = jnp.dot(context, proj[0:D, :], preferred_element_type=F32)
    second = jnp.dot(context, proj[D : 2 * D, :], preferred_element_type=F32)
    for g in range(NX):
        base = g * 2 * DEV_ROWS
        term = first[base : base + DEV_ROWS] + second[base + DEV_ROWS : base + 2 * DEV_ROWS]
        residual = side_all[g, 0:32, :].astype(F32)[0:DEV_ROWS]
        attended[g * DEV_ROWS : (g + 1) * DEV_ROWS, :] = (
            (residual + term).astype(BF16).astype(F32)
        )
    att = attended[...]
    total = jnp.sum(att * att, axis=1, keepdims=True)
    squares[x] = jnp.broadcast_to(total, (COL_ROWS, 128))
    shares = [
        send(squares.at[x], squares.at[x], SQUARES + step - 1, x_dev(step)) for step in (1, 2, 3)
    ]
    meta = (
        side_all[0, 32:48, 0:HALF].astype(F32)
        + side_all[1, 32:48, 0:HALF].astype(F32)
        + side_all[2, 32:48, 0:HALF].astype(F32)
        + side_all[3, 32:48, 0:HALF].astype(F32)
    )
    rows[core, y, z, COL_ROWS : COL_ROWS + 16, 0:HALF] = meta.astype(BF16)
    rows[core, y, z, COL_ROWS : COL_ROWS + 16, HALF:DQ] = jnp.zeros((16, HALF), BF16)
    for share in shares:
        share.wait_recv()
    total = squares[0][:, 0:1] + squares[1][:, 0:1] + squares[2][:, 0:1] + squares[3][:, 0:1]
    normed = (att * lax.rsqrt(total / D + epsilon) * gain_ref[...]).astype(BF16)
    rows[core, y, z, 0:COL_ROWS, :] = normed
    loads[1].wait()
    loads[2].wait()

    opposite = (x + 2) % NX
    lower, upper = pl.ds(0, FF), pl.ds(FF, FF)

    def group_of(k):
        u = k // 2
        return (y + u + 2 * (u % 2) * (1 - u // 2) - u // 2) % NY

    def z_of(k, o):
        near = (k + 1 - (k // 2 + 3) // 4) % 2
        return (z + NZ + near * NEAR[o] + (1 - near) * FAR[o]) % NZ

    def first_copies(k):
        return (
            copy(partial.at[k, opposite, :, lower], first_in.at[k, 0], S1_R + k, x_dev(1)),
            copy(partial.at[k, opposite, :, upper], first_in.at[k, 1], S1_L + k, x_dev(3)),
        )

    def second_copies(k):
        return (
            copy(partial.at[k, from_r], second_in.at[k, 0], S2_R + k, x_dev(1)),
            copy(partial.at[k, from_l], second_in.at[k, 1], S2_L + k, x_dev(3)),
        )

    def hidden_copies(k):
        return (
            copy(hidden.at[k, x], hidden.at[k, x], H1_R + k, x_dev(1)),
            copy(hidden.at[k, x], hidden.at[k, x], H1_L + k, x_dev(3)),
        )

    near, far = pl.ds(0, FF // 2), pl.ds(FF // 2, FF // 2)

    def forward_copies(k):
        return (
            copy(hidden.at[k, from_l, :, near], hidden.at[k, from_l, :, near], H2_R + k, x_dev(1)),
            copy(hidden.at[k, from_r, :, far], hidden.at[k, from_r, :, far], H2_L + k, x_dev(3)),
        )

    def core_copy(k):
        return copy(mixed.at[k, 1 - core], core_in.at[k], CORE_MIX + k, partner)

    row_iota = lax.broadcasted_iota(jnp.int32, (COL_ROWS, COL_ROWS), 0)
    lane_iota = lax.broadcasted_iota(jnp.int32, (COL_ROWS, COL_ROWS), 1)
    earlier = (row_iota < lane_iota).astype(F32).astype(BF16)
    place = lax.broadcasted_iota(jnp.int32, (SPAN, COL_ROWS), 0).astype(F32)

    def pick_and_multiply(k):
        group = group_of(k)
        for column in range(2 * NY):
            there, cc = z_of(k, column // 2), column % 2
            meta = rows[cc, group, there, COL_ROWS : COL_ROWS + 16, 0:128].astype(F32)
            meta = meta[:, 0:COL_ROWS]
            ids, weights = meta[0:TOPK], meta[TOPK : 2 * TOPK]
            scale = 1.0 / jnp.sum(weights, axis=0, keepdims=True)
            named, share = [], []
            for j in range(SLOTS_DEV):
                same = (ids == table_ref[j : j + 1, 0:COL_ROWS]).astype(F32)
                named.append(jnp.sum(same, axis=0, keepdims=True))
                share.append(jnp.sum(same * weights, axis=0, keepdims=True) * scale)
            padded = jnp.concatenate(
                named + [jnp.zeros((SPAN - SLOTS_DEV, COL_ROWS), F32)], axis=0
            )
            ranks = jnp.dot(padded.astype(BF16), earlier, preferred_element_type=F32)
            chosen, weighted = [], []
            for j in range(SLOTS_DEV):
                rank = ranks[j : j + 1]
                twice = table_ref[3 + j : 4 + j, 0:COL_ROWS]
                parity = table_ref[6 + j : 7 + j, 0:COL_ROWS]
                halved = jnp.floor(rank * 0.5)
                where = jnp.where(twice > 0.5, halved, rank)
                odd = rank - 2.0 * halved
                good = (named[j] > 0.5) & ((twice < 0.5) | (odd == parity))
                key = jnp.where(good, where, -1.0)
                pick = (jnp.broadcast_to(key, (SPAN, COL_ROWS)) == place).astype(F32)
                chosen.append(pick)
                weighted.append(pick * share[j])
            pick = jnp.concatenate(chosen, axis=0).astype(BF16)
            picks[k % 8, column] = jnp.concatenate(weighted, axis=0)
            got = jnp.dot(pick, rows[cc, group, there, 0:COL_ROWS, :], preferred_element_type=F32)
            for j in range(SLOTS_DEV):
                picked[j, column * SPAN : (column + 1) * SPAN, :] = got[j * SPAN : (j + 1) * SPAN]
        for j in range(SLOTS_DEV):
            inputs = picked[j].astype(BF16)
            for part in range(3):
                lanes = slice(part * DQ, (part + 1) * DQ)
                product = jnp.dot(inputs, gate_up[j, :, lanes], preferred_element_type=F32)
                product = product.astype(BF16)
                for o in range(NX):
                    partial[k, o, j * 16 : (j + 1) * 16, lanes] = product[o * 16 : (o + 1) * 16]
        for made in first_copies(k):
            made.start()

    def add_first(k):
        for made in first_copies(k):
            made.wait_recv()
        partial[k, from_r, :, 0:FF] = (
            partial[k, from_r, :, 0:FF].astype(F32) + first_in[k, 0].astype(F32)
        ).astype(BF16)
        partial[k, from_l, :, FF : 2 * FF] = (
            partial[k, from_l, :, FF : 2 * FF].astype(F32) + first_in[k, 1].astype(F32)
        ).astype(BF16)
        for made in second_copies(k):
            made.start()

    def add_second(k):
        for made in second_copies(k):
            made.wait_recv()
        summed = (
            partial[k, x].astype(F32) + second_in[k, 0].astype(F32) + second_in[k, 1].astype(F32)
        )
        gate, up = summed[:, 0:FF], summed[:, FF : 2 * FF]
        hidden[k, x] = (gate / (1.0 + jnp.exp(-gate)) * up).astype(BF16)
        for made in hidden_copies(k):
            made.start()

    def pass_hidden(k):
        for made in hidden_copies(k):
            made.wait_recv()
        for made in forward_copies(k):
            made.start()

    def mix(k):
        for made in forward_copies(k):
            made.wait_recv()
        for j in range(SLOTS_DEV):
            inputs = hidden[k, :, j * 16 : (j + 1) * 16, :].reshape(NX * 16, FF)
            product = jnp.dot(inputs, down[j], preferred_element_type=F32)
            expert_out[j] = product.astype(BF16).astype(F32)
        for column in range(2 * NY):
            cc = column % 2
            span = slice(column * SPAN, (column + 1) * SPAN)
            results = jnp.concatenate([expert_out[j, span] for j in range(SLOTS_DEV)], axis=0)
            mixture = lax.dot_general(
                picks[k % 8, column].astype(BF16),
                results.astype(BF16),
                (((0,), (0,)), ((), ())),
                preferred_element_type=F32,
            )
            mixed[k, cc, column // 2] = mixture.astype(BF16)
        core_copy(k).start()

    def chunk_with(group, offset):
        near = offset in NEAR
        index = (NEAR if near else FAR).index(offset)
        first_half = near if group == 0 else not near
        return 2 * group + (0 if first_half else 1), index

    def chain_copy(group, leg, step):
        index = leg * 4 + step
        device = z_dev(1) if leg == 0 else z_dev(7)
        return copy(
            chain_out.at[group, index],
            chain_in.at[group, index],
            CHAIN + 7 * group + index,
            device,
        )

    def block(group, offset):
        k, index = chunk_with(group, offset)
        return mixed[k, core, index].astype(F32) + core_in[k, index].astype(F32)

    def chain(group, step):
        for leg, offset in ((0, 4 - step), (1, step - 3)):
            if offset == 0:
                continue
            value = block(group, offset)
            if step > 0:
                chain_copy(group, leg, step - 1).wait_recv()
                value = value + chain_in[group, leg * 4 + step - 1].astype(F32)
            chain_out[group, leg * 4 + step] = value.astype(BF16)
            chain_copy(group, leg, step).start()

    def y_copy(group):
        step = (0, 3, 1, 2)[group]
        return copy(z_sum.at[group], y_in.at[group - 1], Y_SUM + group - 1, y_dev(step))

    def close(group):
        chain_copy(group, 1, 2).wait_recv()
        chain_copy(group, 0, 3).wait_recv()
        value = block(group, 0)
        value = value + chain_in[group, 3].astype(F32) + chain_in[group, 6].astype(F32)
        z_sum[group] = value.astype(BF16)
        if group > 0:
            y_copy(group).start()

    y_l, y_r = (y + 3) % NY, (y + 1) % NY

    def own_row(where):
        return rows.at[core, y, where % NZ]

    def ring(leg, step):
        where, device = (z + NZ - step, z_dev(1)) if leg == 0 else (z + step, z_dev(7))
        index = (RING_R if leg == 0 else RING_L) + step
        return copy(own_row(where), own_row(where), index, device)

    arrivals = (0, -1, 1, -2, 2, -3, 3, 4)

    def over(number, leg):
        block_ref = own_row(z + NZ + arrivals[number])
        index = (OVER_R if leg == 0 else OVER_L) + number
        return copy(block_ref, block_ref, index, y_dev(1) if leg == 0 else y_dev(3))

    def relay(number):
        where = (z + NZ + arrivals[number]) % NZ
        block_ref = rows.at[core, y_l if number % 2 == 0 else y_r, where]
        return copy(block_ref, block_ref, RELAY + number, y_dev(1) if number % 2 == 0 else y_dev(3))

    def core_row(number):
        block_ref = own_row(z + NZ + arrivals[number])
        return copy(block_ref, block_ref, CORE_ROW + number, partner)

    def core_slab(group):
        slab = rows.at[core, (y + (0, 3, 1, 2)[group]) % NY]
        return copy(slab, slab, CORE_SLAB + group - 1, partner)

    def spread(number):
        core_row(number).start()
        over(number, 0).start()
        over(number, 1).start()

    ring(0, 0).start()
    ring(1, 0).start()
    spread(0)
    for step in (1, 2):
        ring(1, step - 1).wait_recv()
        if step < 3:
            ring(1, step).start()
        spread(2 * step)
        ring(0, step - 1).wait_recv()
        ring(0, step).start()
        spread(2 * step - 1)
    for number in (0, 1, 2, 4):
        core_row(number).wait_recv()
    pick_and_multiply(0)
    ring(1, 2).wait_recv()
    spread(6)
    ring(0, 2).wait_recv()
    ring(0, 3).start()
    spread(5)
    ring(0, 3).wait_recv()
    spread(7)

    def receive_left():
        for number in range(NZ):
            over(number, 0).wait_recv()
            if number % 2 == 0:
                relay(number).start()
        core_slab(1).start()

    def receive_right():
        for number in range(NZ):
            over(number, 1).wait_recv()
            if number % 2 == 1:
                relay(number).start()
        core_slab(2).start()

    def receive_far():
        for number in range(NZ):
            relay(number).wait_recv()
        core_slab(3).start()

    events = {
        1: [receive_left],
        2: [receive_right],
        4: [receive_far],
    }
    ready = {
        1: [functools.partial(lambda n: core_row(n).wait_recv(), n) for n in (3, 5, 6, 7)],
        2: [lambda: core_slab(1).wait_recv()],
        4: [lambda: core_slab(2).wait_recv()],
        6: [lambda: core_slab(3).wait_recv()],
    }
    chains = {}
    for group in range(NY):
        start = 2 * group + 5 + (group == 0)
        for step in range(4):
            chains.setdefault(start + step, []).append(functools.partial(chain, group, step))
        chains.setdefault(start + 4, []).append(functools.partial(close, group))

    def at(t, table):
        for when, works in table.items():

            @pl.when(t == when)
            def _(works=works):
                for work in works:
                    work()

    def core_arrived(k):
        core_copy(k).wait_recv()

    def tick(t, carry):
        pl.when((t >= 5) & (t < NZ + 5))(functools.partial(core_arrived, t - 5))
        at(t, chains)
        for stage, work in ((4, mix), (3, pass_hidden), (2, add_second), (1, add_first)):
            pl.when((t >= stage) & (t < NZ + stage))(functools.partial(work, t - stage))
        at(t, ready)
        pl.when(t < NZ)(functools.partial(pick_and_multiply, t))
        at(t, events)
        return carry

    lax.fori_loop(1, max(chains) + 1, tick, 0)

    for group in range(1, NY):
        y_copy(group).wait_recv()
    mixture = z_sum[0].astype(F32)
    for group in range(1, NY):
        mixture = mixture + y_in[group - 1].astype(F32)
    both = attended[...] + mixture
    for g in range(NX):
        span = slice(g * DEV_ROWS, (g + 1) * DEV_ROWS)
        final_out[g] = jnp.concatenate([mixture[span], both[span]], axis=0).astype(BF16)
    finals = []
    for step in (1, 2, 3):
        there = (x + step) % NX
        finals.append(send(final_out.at[there], final_in.at[x], FINAL + step - 1, x_dev(step)))
    final_in[x] = final_out[x]
    for made in finals:
        made.wait_recv()
    for g in range(NX):
        ended = final_in[g].astype(F32)
        lanes = slice(g * DQ, (g + 1) * DQ)
        moe_ref[:, lanes] = ended[0:DEV_ROWS].astype(BF16)
        layer_ref[:, lanes] = ended[DEV_ROWS : 2 * DEV_ROWS].astype(BF16)

    def drain(k, carry):
        for made in (
            *first_copies(k),
            *second_copies(k),
            *hidden_copies(k),
            *forward_copies(k),
            core_copy(k),
        ):
            made.wait_send()

        return carry

    lax.fori_loop(0, NZ, drain, 0)
    for step in range(4):
        ring(0, step).wait_send()
        if step < 3:
            ring(1, step).wait_send()
    for number in range(NZ):
        for made in (over(number, 0), over(number, 1), relay(number), core_row(number)):
            made.wait_send()
    for group in range(NY):
        for step in range(4):
            chain_copy(group, 0, step).wait_send()
            if step < 3:
                chain_copy(group, 1, step).wait_send()
        if group > 0:
            core_slab(group).wait_send()
            y_copy(group).wait_send()
    for made in pending:
        made.wait_send()


def local(
    queries,
    new_keys,
    new_values,
    key_cache,
    value_cache,
    cache_len,
    residual,
    out_proj,
    norm_gain,
    expert_ids,
    route_weights,
    slot_expert,
    gate_up,
    down_proj,
):
    vmem = pl.BlockSpec(memory_space=pltpu.VMEM)
    smem = pl.BlockSpec(memory_space=pltpu.SMEM)
    hbm = pl.BlockSpec(memory_space=pl.ANY)
    requests, cached, width = key_cache.shape
    return pl.pallas_call(
        layer_kernel,
        out_shape=(
            jax.ShapeDtypeStruct((DEV_ROWS, D), BF16),
            jax.ShapeDtypeStruct((DEV_ROWS, D), BF16),
        ),
        in_specs=[hbm] * 5 + [smem] + [hbm] * 2 + [vmem] * 4 + [hbm] * 2,
        out_specs=(vmem, vmem),
        scratch_shapes=[
            pltpu.VMEM((DEV_ROWS, 2 * D), BF16),
            pltpu.VMEM((DEV_ROWS, width), BF16),
            pltpu.VMEM((DEV_ROWS, width), BF16),
            pltpu.VMEM((requests, cached, width), BF16),
            pltpu.VMEM((requests, cached, width), BF16),
            pltpu.VMEM((DEV_ROWS, D), BF16),
            pltpu.VMEM((DEV_ROWS * HEADS, HEAD_DIM), F32),
            pltpu.VMEM((DEV_ROWS * HEADS, HEAD_DIM), F32),
            pltpu.VMEM((DEV_ROWS, width), F32),
            pltpu.VMEM((DEV_ROWS, width), F32),
            pltpu.VMEM((16, 128), F32),
            pltpu.VMEM((NX, 48, DQ), BF16),
            pltpu.VMEM((NX, 2 * DEV_ROWS, D), BF16),
            pltpu.VMEM((NX, 48, DQ), BF16),
            pltpu.VMEM((2 * D, DQ), BF16),
            pltpu.VMEM((SLOTS_DEV, DQ, 2 * FF), BF16),
            pltpu.VMEM((SLOTS_DEV, FF, DQ), BF16),
            pltpu.VMEM((NX, COL_ROWS, 128), F32),
            pltpu.VMEM((COL_ROWS, DQ), F32),
            pltpu.VMEM((2, NY, NZ, COL_ROWS + 16, DQ), BF16),
            pltpu.VMEM((NZ, 2 * NY, SLOTS_DEV * SPAN, COL_ROWS), F32),
            pltpu.VMEM((SLOTS_DEV, 2 * NY * SPAN, DQ), F32),
            pltpu.VMEM((NZ, NX, 48, 2 * FF), BF16),
            pltpu.VMEM((NZ, 2, 48, FF), BF16),
            pltpu.VMEM((NZ, 2, 48, 2 * FF), BF16),
            pltpu.VMEM((NZ, NX, 48, FF), BF16),
            pltpu.VMEM((SLOTS_DEV, 2 * NY * SPAN, DQ), F32),
            pltpu.VMEM((NZ, 2, NY, COL_ROWS, DQ), BF16),
            pltpu.VMEM((NZ, NY, COL_ROWS, DQ), BF16),
            pltpu.VMEM((NY, 7, COL_ROWS, DQ), BF16),
            pltpu.VMEM((NY, 7, COL_ROWS, DQ), BF16),
            pltpu.VMEM((NY, COL_ROWS, DQ), BF16),
            pltpu.VMEM((NY - 1, COL_ROWS, DQ), BF16),
            pltpu.VMEM((NX, 48, DQ), BF16),
            pltpu.VMEM((NX, 48, DQ), BF16),
            pltpu.SemaphoreType.DMA((COPIES,)),
            pltpu.SemaphoreType.DMA((COPIES,)),
            pltpu.SemaphoreType.DMA((9,)),
        ],
        compiler_params=pltpu.CompilerParams(
            collective_id=0, has_side_effects=True, vmem_limit_bytes=67043328
        ),
    )(
        queries,
        new_keys,
        new_values,
        key_cache,
        value_cache,
        cache_len,
        residual,
        out_proj,
        norm_gain[None, :],
        expert_ids,
        route_weights,
        slot_expert[None, :],
        gate_up,
        down_proj,
    )


def solution(mesh):
    placed = (
        P(("grp", "ep"), None),
        P(("grp", "ep"), None),
        P(("grp", "ep"), None),
        P(("grp", "ep"), None, None),
        P(("grp", "ep"), None, None),
        P(("grp", "ep")),
        P(("grp", "ep"), None),
        P(None, "grp"),
        P("grp"),
        P(("grp", "ep"), None),
        P(("grp", "ep"), None),
        P(),
        P("ep", "grp", None),
        P("ep", None, "grp"),
    )
    return jax.shard_map(
        local,
        mesh=mesh,
        in_specs=placed,
        out_specs=(P(("grp", "ep"), None), P(("grp", "ep"), None)),
        check_vma=False,
    )
```

```python
import functools
import math

import jax
import jax.numpy as jnp
from jax import lax
from jax.experimental import pallas as pl
from jax.experimental.pallas import tpu as pltpu
from jax.sharding import PartitionSpec as P

D = 2048
HEADS = 32
KV_HEADS = 4
HEAD_DIM = 128
FF = 768
TOPK = 8
SLOTS_DEV = 3
PRE = 8
DEV_ROWS = 24
COL_ROWS = 96
DQ = 512
HALF = 256
NX = 4
NY = 4
NZ = 8
SPAN = 8

MESH = pl.DeviceIdType.MESH
F32 = jnp.float32
BF16 = jnp.bfloat16

masked_score = -1e30
epsilon = 1e-06

CTX_R, CTX_L, CTX_FR, CTX_FL = 0, 1, 2, 3
SIDE = 4
SQUARES = 7
RING_R, RING_L = 10, 14
OVER_R, OVER_L = 17, 25
RELAY = 33
CORE_ROW = 41
CORE_SLAB = 49
S1_R, S1_L, S2_R, S2_L = 52, 60, 68, 76
H1_R, H1_L, H2_R, H2_L = 84, 92, 100, 108
CORE_MIX = 116
CHAIN = 148
Y_SUM = 176
FINAL = 179
CTX_LATE_R, CTX_LATE_L = 182, 183
COPIES = 184

NEAR = (2, -1, 1, 0)
FAR = (4, -3, 3, -2)


def layer_kernel(
    queries_hbm,
    new_keys_hbm,
    new_values_hbm,
    key_cache_hbm,
    value_cache_hbm,
    cache_len_ref,
    residual_hbm,
    out_proj_hbm,
    gain_ref,
    ids_ref,
    weights_ref,
    slots_ref,
    gate_up_hbm,
    down_hbm,
    moe_ref,
    layer_ref,
    queries,
    new_keys,
    new_values,
    key_cache,
    value_cache,
    residual,
    by_head,
    context_head,
    own_keys,
    own_values,
    table_ref,
    side_out,
    ctx_all,
    side_all,
    proj,
    gate_up,
    down,
    squares,
    attended,
    rows,
    picks,
    picked,
    partial,
    first_in,
    second_in,
    hidden,
    expert_out,
    mixed,
    core_in,
    chain_out,
    chain_in,
    z_sum,
    y_in,
    final_out,
    final_in,
    send_sem,
    recv_sem,
    load_sem,
):
    x = lax.axis_index("grp")
    ep = lax.axis_index("ep")
    core = ep % 2
    z = (ep // 2) % NZ
    y = ep // (2 * NZ)

    def x_dev(step):
        return ((x + step) % NX, ep)

    def y_dev(step):
        return (x, (((y + step) % NY) * NZ + z) * 2 + core)

    def z_dev(step):
        return (x, (y * NZ + (z + step) % NZ) * 2 + core)

    partner = (x, (y * NZ + z) * 2 + 1 - core)

    def copy(source, target, index, device):
        return pltpu.make_async_remote_copy(
            src_ref=source,
            dst_ref=target,
            send_sem=send_sem.at[index],
            recv_sem=recv_sem.at[index],
            device_id=device,
            device_id_type=MESH,
        )

    peers = [x_dev(1), x_dev(2), x_dev(3), y_dev(1), y_dev(2), y_dev(3), z_dev(1), z_dev(7), partner]
    barrier = pltpu.get_barrier_semaphore()
    for peer in peers:
        pl.semaphore_signal(barrier, inc=1, device_id=peer, device_id_type=MESH)

    early = [
        pltpu.make_async_copy(queries_hbm, queries, load_sem.at[0]),
        pltpu.make_async_copy(new_keys_hbm, new_keys, load_sem.at[1]),
        pltpu.make_async_copy(new_values_hbm, new_values, load_sem.at[2]),
        pltpu.make_async_copy(key_cache_hbm, key_cache, load_sem.at[3]),
        pltpu.make_async_copy(value_cache_hbm, value_cache, load_sem.at[4]),
        pltpu.make_async_copy(residual_hbm, residual, load_sem.at[5]),
    ]
    loads = [
        pltpu.make_async_copy(out_proj_hbm, proj, load_sem.at[6]),
        pltpu.make_async_copy(gate_up_hbm, gate_up, load_sem.at[7]),
        pltpu.make_async_copy(down_hbm, down, load_sem.at[8]),
    ]
    for load in early + loads:
        load.start()

    slots = slots_ref[...].astype(F32)
    slot_lane = lax.broadcasted_iota(jnp.int32, slots.shape, 1)
    for j in range(SLOTS_DEV):
        here = ep * SLOTS_DEV + j
        mine = jnp.sum(jnp.where(slot_lane == here, slots, 0.0), axis=1, keepdims=True)
        same = jnp.where(slots == mine, 1.0, 0.0)
        twice = jnp.sum(same, axis=1, keepdims=True) - 1.0
        before = jnp.sum(jnp.where(slot_lane < here, same, 0.0), axis=1, keepdims=True)
        for row, value in ((j, mine + 1.0), (3 + j, twice), (6 + j, before)):
            table_ref[row : row + 1, :] = jnp.broadcast_to(value, (1, 128))
    spread_row = lax.broadcasted_iota(jnp.int32, (DEV_ROWS, 128), 0)
    spread_lane = lax.broadcasted_iota(jnp.int32, (DEV_ROWS, 128), 1)
    to_lane = jnp.where(spread_lane == spread_row + x * DEV_ROWS, 1.0, 0.0).astype(BF16)
    routes = [
        jnp.dot(value.astype(BF16), to_lane, preferred_element_type=F32)
        for value in (ids_ref[...].astype(F32) + 1.0, weights_ref[...].astype(F32))
    ]
    routes = jnp.concatenate(routes, axis=1)
    for load in early:
        load.wait()
    for g in range(NX):
        quarter = residual[:, g * DQ : (g + 1) * DQ].astype(F32)
        routes_wide = jnp.concatenate([routes, jnp.zeros((TOPK, DQ - HALF), F32)], axis=1)
        side_out[g] = jnp.concatenate([quarter, routes_wide], axis=0).astype(BF16)

    own_keys[...] = new_keys[...].astype(F32)
    own_values[...] = new_values[...].astype(F32)
    for h in range(HEADS):
        by_head[pl.ds(h, DEV_ROWS, stride=HEADS), :] = queries[
            :, h * HEAD_DIM : (h + 1) * HEAD_DIM
        ].astype(F32)
    width = KV_HEADS * HEAD_DIM
    head_row = lax.broadcasted_iota(jnp.int32, (HEADS, width), 0)
    head_lane = lax.broadcasted_iota(jnp.int32, (HEADS, width), 1)
    same_head = head_row // (HEADS // KV_HEADS) == head_lane // HEAD_DIM
    scaling = 1.0 / math.sqrt(HEAD_DIM)

    def spread_query(row):
        query = by_head[pl.ds(row * HEADS, HEADS), :]
        return jnp.where(same_head, jnp.concatenate([query] * KV_HEADS, axis=1), 0.0)

    def join(mixed_values):
        mixed_values = jnp.where(same_head, mixed_values, 0.0)
        joined = mixed_values[:, 0:HEAD_DIM]
        for kv in range(1, KV_HEADS):
            joined = joined + mixed_values[:, kv * HEAD_DIM : (kv + 1) * HEAD_DIM]
        return joined

    def score(query, keys):
        return (
            lax.dot_general(
                query.astype(BF16), keys, (((1,), (1,)), ((), ())), preferred_element_type=F32
            )
            * scaling
        )

    def prefill_row(row):
        query = spread_query(row)
        scores = score(query, new_keys[0 : 2 * PRE, :])
        token = lax.broadcasted_iota(jnp.int32, scores.shape, 1)
        scores = jnp.where(token <= row, scores, masked_score)
        exponent = jnp.exp(scores - jnp.max(scores, axis=1, keepdims=True))
        probs = (exponent / jnp.sum(exponent, axis=1, keepdims=True)).astype(BF16)
        values = jnp.dot(probs, new_values[0 : 2 * PRE, :], preferred_element_type=F32)
        context_head[pl.ds(row * HEADS, HEADS), :] = join(values)

    def decode_row(request):
        row = PRE + request
        query = spread_query(row)
        scores = score(query, key_cache[request])
        token = lax.broadcasted_iota(jnp.int32, scores.shape, 1)
        scores = jnp.where(token < cache_len_ref[request], scores, masked_score)
        own = jnp.sum(query * own_keys[pl.ds(row, 1), :], axis=1, keepdims=True) * scaling
        top = jnp.maximum(jnp.max(scores, axis=1, keepdims=True), own)
        exponent = jnp.exp(scores - top)
        own_exp = jnp.exp(own - top)
        total = jnp.sum(exponent, axis=1, keepdims=True) + own_exp
        probs = (exponent / total).astype(BF16)
        own_prob = (own_exp / total).astype(BF16).astype(F32)
        values = jnp.dot(probs, value_cache[request], preferred_element_type=F32)
        values = values + own_prob * own_values[pl.ds(row, 1), :]
        context_head[pl.ds(row * HEADS, HEADS), :] = join(values)

    def four(work):
        def body(i, carry):
            for part in range(4):
                work(i * 4 + part)
            return carry

        return body

    lax.fori_loop(0, PRE // 4, four(prefill_row), 0)
    lax.fori_loop(0, (DEV_ROWS - PRE) // 4, four(decode_row), 0)
    for h in range(HEADS // 2):
        pair = [
            context_head[pl.ds(there, DEV_ROWS, stride=HEADS), :] for there in (h, h + HEADS // 2)
        ]
        ctx_all[x, :, h * HEAD_DIM : (h + 1) * HEAD_DIM] = jnp.concatenate(pair, axis=0).astype(
            BF16
        )
    side_all[x] = side_out[x]
    pl.semaphore_wait(barrier, len(peers))

    pending = []

    def send(source, target, index, device):
        made = copy(source, target, index, device)
        made.start()
        pending.append(made)
        return made

    low, high = pl.ds(0, D // 2), pl.ds(D // 2, D // 2)

    def context_part(owner, lanes, index, device):
        part = ctx_all.at[owner, :, lanes]
        return send(part, part, index, device)

    sides = []
    for step in (1, 2, 3):
        there = (x + step) % NX
        sides.append(send(side_out.at[there], side_all.at[x], SIDE + step - 1, x_dev(step)))
    first_r = context_part(x, low, CTX_R, x_dev(1))
    first_l = context_part(x, high, CTX_L, x_dev(3))
    later_r = context_part(x, high, CTX_LATE_R, x_dev(1))
    later_l = context_part(x, low, CTX_LATE_L, x_dev(3))
    from_l, from_r = (x + 3) % NX, (x + 1) % NX
    first_r.wait_recv()
    fwd_r = context_part(from_l, low, CTX_FR, x_dev(1))
    first_l.wait_recv()
    fwd_l = context_part(from_r, high, CTX_FL, x_dev(3))
    later_r.wait_recv()
    later_l.wait_recv()
    loads[0].wait()
    for side in sides:
        side.wait_recv()
    fwd_r.wait_recv()
    fwd_l.wait_recv()

    context = ctx_all[...].reshape(NX * 2 * DEV_ROWS, D)
    first = jnp.dot(context, proj[0:D, :], preferred_element_type=F32)
    second = jnp.dot(context, proj[D : 2 * D, :], preferred_element_type=F32)
    for g in range(NX):
        base = g * 2 * DEV_ROWS
        term = first[base : base + DEV_ROWS] + second[base + DEV_ROWS : base + 2 * DEV_ROWS]
        kept = side_all[g].astype(F32)[0:DEV_ROWS]
        attended[g * DEV_ROWS : (g + 1) * DEV_ROWS, :] = (
            (kept + term).astype(BF16).astype(F32)
        )
    att = attended[...]
    total = jnp.sum(att * att, axis=1, keepdims=True)
    squares[x] = jnp.broadcast_to(total, (COL_ROWS, 128))
    shares = [
        send(squares.at[x], squares.at[x], SQUARES + step - 1, x_dev(step)) for step in (1, 2, 3)
    ]
    meta = (
        side_all[0].astype(F32)[DEV_ROWS:]
        + side_all[1].astype(F32)[DEV_ROWS:]
        + side_all[2].astype(F32)[DEV_ROWS:]
        + side_all[3].astype(F32)[DEV_ROWS:]
    )
    meta = jnp.concatenate([meta[:, 0:128], meta[:, 128:256]], axis=0)
    meta = jnp.concatenate([meta, jnp.zeros((16, DQ - 128), F32)], axis=1)
    rows[core, y, z, COL_ROWS : COL_ROWS + 16, :] = meta.astype(BF16)
    for share in shares:
        share.wait_recv()
    total = squares[0][:, 0:1] + squares[1][:, 0:1] + squares[2][:, 0:1] + squares[3][:, 0:1]
    normed = (att * lax.rsqrt(total / D + epsilon) * gain_ref[...]).astype(BF16)
    rows[core, y, z, 0:COL_ROWS, :] = normed
    loads[1].wait()
    loads[2].wait()

    opposite = (x + 2) % NX
    lower, upper = pl.ds(0, FF), pl.ds(FF, FF)

    def group_of(k):
        u = k // 2
        return (y + u + 2 * (u % 2) * (1 - u // 2) - u // 2) % NY

    def z_of(k, o):
        near = (k + 1 - (k // 2 + 3) // 4) % 2
        return (z + NZ + near * NEAR[o] + (1 - near) * FAR[o]) % NZ

    def first_copies(k):
        return (
            copy(partial.at[k, opposite, :, lower], first_in.at[k, 0], S1_R + k, x_dev(1)),
            copy(partial.at[k, opposite, :, upper], first_in.at[k, 1], S1_L + k, x_dev(3)),
        )

    def second_copies(k):
        return (
            copy(partial.at[k, from_r], second_in.at[k, 0], S2_R + k, x_dev(1)),
            copy(partial.at[k, from_l], second_in.at[k, 1], S2_L + k, x_dev(3)),
        )

    def hidden_copies(k):
        return (
            copy(hidden.at[k, x], hidden.at[k, x], H1_R + k, x_dev(1)),
            copy(hidden.at[k, x], hidden.at[k, x], H1_L + k, x_dev(3)),
        )

    near, far = pl.ds(0, FF // 2), pl.ds(FF // 2, FF // 2)

    def forward_copies(k):
        return (
            copy(hidden.at[k, from_l, :, near], hidden.at[k, from_l, :, near], H2_R + k, x_dev(1)),
            copy(hidden.at[k, from_r, :, far], hidden.at[k, from_r, :, far], H2_L + k, x_dev(3)),
        )

    def core_copy(k, o):
        return copy(mixed.at[k, 1 - core, o], core_in.at[k, o], CORE_MIX + 4 * k + o, partner)

    row_iota = lax.broadcasted_iota(jnp.int32, (COL_ROWS, COL_ROWS), 0)
    lane_iota = lax.broadcasted_iota(jnp.int32, (COL_ROWS, COL_ROWS), 1)
    earlier = (row_iota < lane_iota).astype(F32).astype(BF16)
    place = lax.broadcasted_iota(jnp.int32, (SPAN, COL_ROWS), 0).astype(F32)

    def pick_and_multiply(k):
        group = group_of(k)
        for column in range(2 * NY):
            there, cc = z_of(k, column // 2), column % 2
            meta = rows[cc, group, there, COL_ROWS : COL_ROWS + 16, 0:128].astype(F32)
            meta = meta[:, 0:COL_ROWS]
            ids, weights = meta[0:TOPK], meta[TOPK : 2 * TOPK]
            scale = 1.0 / jnp.sum(weights, axis=0, keepdims=True)
            named, share = [], []
            for j in range(SLOTS_DEV):
                same = (ids == table_ref[j : j + 1, 0:COL_ROWS]).astype(F32)
                named.append(jnp.sum(same, axis=0, keepdims=True))
                share.append(jnp.sum(same * weights, axis=0, keepdims=True) * scale)
            padded = jnp.concatenate(
                named + [jnp.zeros((SPAN - SLOTS_DEV, COL_ROWS), F32)], axis=0
            )
            ranks = jnp.dot(padded.astype(BF16), earlier, preferred_element_type=F32)
            chosen, weighted = [], []
            for j in range(SLOTS_DEV):
                rank = ranks[j : j + 1]
                twice = table_ref[3 + j : 4 + j, 0:COL_ROWS]
                parity = table_ref[6 + j : 7 + j, 0:COL_ROWS]
                halved = jnp.floor(rank * 0.5)
                where = jnp.where(twice > 0.5, halved, rank)
                odd = rank - 2.0 * halved
                good = (named[j] > 0.5) & ((twice < 0.5) | (odd == parity))
                key = jnp.where(good, where, -1.0)
                pick = (jnp.broadcast_to(key, (SPAN, COL_ROWS)) == place).astype(F32)
                chosen.append(pick)
                weighted.append(pick * share[j])
            pick = jnp.concatenate(chosen, axis=0).astype(BF16)
            picks[k % 8, column] = jnp.concatenate(weighted, axis=0)
            got = jnp.dot(pick, rows[cc, group, there, 0:COL_ROWS, :], preferred_element_type=F32)
            for j in range(SLOTS_DEV):
                picked[j, column * SPAN : (column + 1) * SPAN, :] = got[j * SPAN : (j + 1) * SPAN]
        for j in range(SLOTS_DEV):
            inputs = picked[j].astype(BF16)
            for part in range(3):
                lanes = slice(part * DQ, (part + 1) * DQ)
                product = jnp.dot(inputs, gate_up[j, :, lanes], preferred_element_type=F32)
                product = product.astype(BF16)
                for o in range(NX):
                    partial[k, o, j * 16 : (j + 1) * 16, lanes] = product[o * 16 : (o + 1) * 16]
        for made in first_copies(k):
            made.start()

    def add_first(k):
        for made in first_copies(k):
            made.wait_recv()
        partial[k, from_r, :, 0:FF] = (
            partial[k, from_r, :, 0:FF].astype(F32) + first_in[k, 0].astype(F32)
        ).astype(BF16)
        partial[k, from_l, :, FF : 2 * FF] = (
            partial[k, from_l, :, FF : 2 * FF].astype(F32) + first_in[k, 1].astype(F32)
        ).astype(BF16)
        for made in second_copies(k):
            made.start()

    def add_second(k):
        for made in second_copies(k):
            made.wait_recv()
        summed = (
            partial[k, x].astype(F32) + second_in[k, 0].astype(F32) + second_in[k, 1].astype(F32)
        )
        gate, up = summed[:, 0:FF], summed[:, FF : 2 * FF]
        hidden[k, x] = (gate / (1.0 + jnp.exp(-gate)) * up).astype(BF16)
        for made in hidden_copies(k):
            made.start()

    def pass_hidden(k):
        for made in hidden_copies(k):
            made.wait_recv()
        for made in forward_copies(k):
            made.start()

    def mix(k):
        for made in forward_copies(k):
            made.wait_recv()
        for j in range(SLOTS_DEV):
            inputs = hidden[k, :, j * 16 : (j + 1) * 16, :].reshape(NX * 16, FF)
            product = jnp.dot(inputs, down[j], preferred_element_type=F32)
            expert_out[j] = product.astype(BF16).astype(F32)
        for column in range(2 * NY):
            cc = column % 2
            span = slice(column * SPAN, (column + 1) * SPAN)
            results = jnp.concatenate([expert_out[j, span] for j in range(SLOTS_DEV)], axis=0)
            mixture = lax.dot_general(
                picks[k % 8, column].astype(BF16),
                results.astype(BF16),
                (((0,), (0,)), ((), ())),
                preferred_element_type=F32,
            )
            mixed[k, cc, column // 2] = mixture.astype(BF16)
            if cc == 1:
                core_copy(k, column // 2).start()

    def chunk_with(group, offset):
        near = offset in NEAR
        index = (NEAR if near else FAR).index(offset)
        first_half = near if group == 0 else not near
        return 2 * group + (0 if first_half else 1), index

    def chain_copy(group, leg, step):
        index = leg * 4 + step
        device = z_dev(1) if leg == 0 else z_dev(7)
        return copy(
            chain_out.at[group, index],
            chain_in.at[group, index],
            CHAIN + 7 * group + index,
            device,
        )

    def block(group, offset):
        k, index = chunk_with(group, offset)
        if k == NZ - 1:
            core_copy(k, index).wait_recv()
        return mixed[k, core, index].astype(F32) + core_in[k, index].astype(F32)

    def chain(group, step):
        for leg, offset in ((0, 4 - step), (1, step - 3)):
            if offset == 0:
                continue
            value = block(group, offset)
            if step > 0:
                chain_copy(group, leg, step - 1).wait_recv()
                value = value + chain_in[group, leg * 4 + step - 1].astype(F32)
            chain_out[group, leg * 4 + step] = value.astype(BF16)
            chain_copy(group, leg, step).start()

    def y_copy(group):
        step = (0, 3, 1, 2)[group]
        return copy(z_sum.at[group], y_in.at[group - 1], Y_SUM + group - 1, y_dev(step))

    def close(group):
        chain_copy(group, 1, 2).wait_recv()
        chain_copy(group, 0, 3).wait_recv()
        value = block(group, 0)
        value = value + chain_in[group, 3].astype(F32) + chain_in[group, 6].astype(F32)
        z_sum[group] = value.astype(BF16)
        if group > 0:
            y_copy(group).start()

    y_l, y_r = (y + 3) % NY, (y + 1) % NY

    def own_row(where):
        return rows.at[core, y, where % NZ]

    def ring(leg, step):
        where, device = (z + NZ - step, z_dev(1)) if leg == 0 else (z + step, z_dev(7))
        index = (RING_R if leg == 0 else RING_L) + step
        return copy(own_row(where), own_row(where), index, device)

    arrivals = (0, -1, 1, -2, 2, -3, 3, 4)

    def over(number, leg):
        block_ref = own_row(z + NZ + arrivals[number])
        index = (OVER_R if leg == 0 else OVER_L) + number
        return copy(block_ref, block_ref, index, y_dev(1) if leg == 0 else y_dev(3))

    def relay(number):
        where = (z + NZ + arrivals[number]) % NZ
        block_ref = rows.at[core, y_l if number % 2 == 0 else y_r, where]
        return copy(block_ref, block_ref, RELAY + number, y_dev(1) if number % 2 == 0 else y_dev(3))

    def core_row(number):
        block_ref = own_row(z + NZ + arrivals[number])
        return copy(block_ref, block_ref, CORE_ROW + number, partner)

    def core_slab(group):
        slab = rows.at[core, (y + (0, 3, 1, 2)[group]) % NY]
        return copy(slab, slab, CORE_SLAB + group - 1, partner)

    def spread(number):
        core_row(number).start()
        over(number, 0).start()
        over(number, 1).start()

    ring(0, 0).start()
    ring(1, 0).start()
    spread(0)
    for step in (1, 2):
        ring(1, step - 1).wait_recv()
        if step < 3:
            ring(1, step).start()
        spread(2 * step)
        ring(0, step - 1).wait_recv()
        ring(0, step).start()
        spread(2 * step - 1)
    for number in (0, 1, 2, 4):
        core_row(number).wait_recv()
    pick_and_multiply(0)
    ring(1, 2).wait_recv()
    spread(6)
    ring(0, 2).wait_recv()
    ring(0, 3).start()
    spread(5)
    ring(0, 3).wait_recv()
    spread(7)

    def receive_left():
        for number in range(NZ):
            over(number, 0).wait_recv()
            if number % 2 == 0:
                relay(number).start()
        core_slab(1).start()

    def receive_right():
        for number in range(NZ):
            over(number, 1).wait_recv()
            if number % 2 == 1:
                relay(number).start()
        core_slab(2).start()

    def receive_far():
        for number in range(NZ):
            relay(number).wait_recv()
        core_slab(3).start()

    events = {
        1: [receive_left],
        2: [receive_right],
        4: [receive_far],
    }
    ready = {
        1: [functools.partial(lambda n: core_row(n).wait_recv(), n) for n in (3, 5, 6, 7)],
        2: [lambda: core_slab(1).wait_recv()],
        4: [lambda: core_slab(2).wait_recv()],
        6: [lambda: core_slab(3).wait_recv()],
    }
    chains = {}
    for group in range(NY):
        start = 2 * group + 5 + (group == 0)
        for step in range(4):
            chains.setdefault(start + step, []).append(functools.partial(chain, group, step))
        chains.setdefault(start + 4, []).append(functools.partial(close, group))

    def at(t, table):
        for when, works in table.items():

            @pl.when(t == when)
            def _(works=works):
                for work in works:
                    work()

    def core_arrived(k):
        for o in range(4):
            core_copy(k, o).wait_recv()

    def tick(t, carry):
        pl.when((t >= 5) & (t < NZ + 4))(functools.partial(core_arrived, t - 5))
        at(t, chains)
        for stage, work in ((4, mix), (3, pass_hidden), (2, add_second), (1, add_first)):
            pl.when((t >= stage) & (t < NZ + stage))(functools.partial(work, t - stage))
        at(t, ready)
        pl.when(t < NZ)(functools.partial(pick_and_multiply, t))
        at(t, events)
        return carry

    lax.fori_loop(1, max(chains) + 1, tick, 0)

    for group in range(1, NY):
        y_copy(group).wait_recv()
    mixture = z_sum[0].astype(F32)
    for group in range(1, NY):
        mixture = mixture + y_in[group - 1].astype(F32)
    both = attended[...] + mixture
    for g in range(NX):
        span = slice(g * DEV_ROWS, (g + 1) * DEV_ROWS)
        final_out[g] = jnp.concatenate([mixture[span], both[span]], axis=0).astype(BF16)
    finals = []
    for step in (1, 2, 3):
        there = (x + step) % NX
        finals.append(send(final_out.at[there], final_in.at[x], FINAL + step - 1, x_dev(step)))
    final_in[x] = final_out[x]
    for made in finals:
        made.wait_recv()
    for g in range(NX):
        ended = final_in[g].astype(F32)
        lanes = slice(g * DQ, (g + 1) * DQ)
        moe_ref[:, lanes] = ended[0:DEV_ROWS].astype(BF16)
        layer_ref[:, lanes] = ended[DEV_ROWS : 2 * DEV_ROWS].astype(BF16)

    def drain(k, carry):
        for made in (
            *first_copies(k),
            *second_copies(k),
            *hidden_copies(k),
            *forward_copies(k),
            *(core_copy(k, o) for o in range(4)),
        ):
            made.wait_send()

        return carry

    lax.fori_loop(0, NZ, drain, 0)
    for step in range(4):
        ring(0, step).wait_send()
        if step < 3:
            ring(1, step).wait_send()
    for number in range(NZ):
        for made in (over(number, 0), over(number, 1), relay(number), core_row(number)):
            made.wait_send()
    for group in range(NY):
        for step in range(4):
            chain_copy(group, 0, step).wait_send()
            if step < 3:
                chain_copy(group, 1, step).wait_send()
        if group > 0:
            core_slab(group).wait_send()
            y_copy(group).wait_send()
    for made in pending:
        made.wait_send()


def local(
    queries,
    new_keys,
    new_values,
    key_cache,
    value_cache,
    cache_len,
    residual,
    out_proj,
    norm_gain,
    expert_ids,
    route_weights,
    slot_expert,
    gate_up,
    down_proj,
):
    vmem = pl.BlockSpec(memory_space=pltpu.VMEM)
    smem = pl.BlockSpec(memory_space=pltpu.SMEM)
    hbm = pl.BlockSpec(memory_space=pl.ANY)
    requests, cached, width = key_cache.shape
    return pl.pallas_call(
        layer_kernel,
        out_shape=(
            jax.ShapeDtypeStruct((DEV_ROWS, D), BF16),
            jax.ShapeDtypeStruct((DEV_ROWS, D), BF16),
        ),
        in_specs=[hbm] * 5 + [smem] + [hbm] * 2 + [vmem] * 4 + [hbm] * 2,
        out_specs=(vmem, vmem),
        scratch_shapes=[
            pltpu.VMEM((DEV_ROWS, 2 * D), BF16),
            pltpu.VMEM((DEV_ROWS, width), BF16),
            pltpu.VMEM((DEV_ROWS, width), BF16),
            pltpu.VMEM((requests, cached, width), BF16),
            pltpu.VMEM((requests, cached, width), BF16),
            pltpu.VMEM((DEV_ROWS, D), BF16),
            pltpu.VMEM((DEV_ROWS * HEADS, HEAD_DIM), F32),
            pltpu.VMEM((DEV_ROWS * HEADS, HEAD_DIM), F32),
            pltpu.VMEM((DEV_ROWS, width), F32),
            pltpu.VMEM((DEV_ROWS, width), F32),
            pltpu.VMEM((16, 128), F32),
            pltpu.VMEM((NX, 32, DQ), BF16),
            pltpu.VMEM((NX, 2 * DEV_ROWS, D), BF16),
            pltpu.VMEM((NX, 32, DQ), BF16),
            pltpu.VMEM((2 * D, DQ), BF16),
            pltpu.VMEM((SLOTS_DEV, DQ, 2 * FF), BF16),
            pltpu.VMEM((SLOTS_DEV, FF, DQ), BF16),
            pltpu.VMEM((NX, COL_ROWS, 128), F32),
            pltpu.VMEM((COL_ROWS, DQ), F32),
            pltpu.VMEM((2, NY, NZ, COL_ROWS + 16, DQ), BF16),
            pltpu.VMEM((NZ, 2 * NY, SLOTS_DEV * SPAN, COL_ROWS), F32),
            pltpu.VMEM((SLOTS_DEV, 2 * NY * SPAN, DQ), F32),
            pltpu.VMEM((NZ, NX, 48, 2 * FF), BF16),
            pltpu.VMEM((NZ, 2, 48, FF), BF16),
            pltpu.VMEM((NZ, 2, 48, 2 * FF), BF16),
            pltpu.VMEM((NZ, NX, 48, FF), BF16),
            pltpu.VMEM((SLOTS_DEV, 2 * NY * SPAN, DQ), F32),
            pltpu.VMEM((NZ, 2, NY, COL_ROWS, DQ), BF16),
            pltpu.VMEM((NZ, NY, COL_ROWS, DQ), BF16),
            pltpu.VMEM((NY, 7, COL_ROWS, DQ), BF16),
            pltpu.VMEM((NY, 7, COL_ROWS, DQ), BF16),
            pltpu.VMEM((NY, COL_ROWS, DQ), BF16),
            pltpu.VMEM((NY - 1, COL_ROWS, DQ), BF16),
            pltpu.VMEM((NX, 48, DQ), BF16),
            pltpu.VMEM((NX, 48, DQ), BF16),
            pltpu.SemaphoreType.DMA((COPIES,)),
            pltpu.SemaphoreType.DMA((COPIES,)),
            pltpu.SemaphoreType.DMA((9,)),
        ],
        compiler_params=pltpu.CompilerParams(
            collective_id=0, has_side_effects=True, vmem_limit_bytes=67043328
        ),
    )(
        queries,
        new_keys,
        new_values,
        key_cache,
        value_cache,
        cache_len,
        residual,
        out_proj,
        norm_gain[None, :],
        expert_ids.T,
        route_weights.T,
        slot_expert[None, :],
        gate_up,
        down_proj,
    )


def solution(mesh):
    placed = (
        P(("grp", "ep"), None),
        P(("grp", "ep"), None),
        P(("grp", "ep"), None),
        P(("grp", "ep"), None, None),
        P(("grp", "ep"), None, None),
        P(("grp", "ep")),
        P(("grp", "ep"), None),
        P(None, "grp"),
        P("grp"),
        P(("grp", "ep"), None),
        P(("grp", "ep"), None),
        P(),
        P("ep", "grp", None),
        P("ep", None, "grp"),
    )
    return jax.shard_map(
        local,
        mesh=mesh,
        in_specs=placed,
        out_specs=(P(("grp", "ep"), None), P(("grp", "ep"), None)),
        check_vma=False,
    )
```

```python
import functools
import math

import jax
import jax.numpy as jnp
from jax import lax
from jax.experimental import pallas as pl
from jax.experimental.pallas import tpu as pltpu
from jax.sharding import PartitionSpec as P

D = 2048
HEADS = 32
KV_HEADS = 4
HEAD_DIM = 128
FF = 768
TOPK = 8
SLOTS_DEV = 3
PRE = 8
DEV_ROWS = 24
COL_ROWS = 96
DQ = 512
HALF = 256
NX = 4
NY = 4
NZ = 8
SPAN = 8

MESH = pl.DeviceIdType.MESH
F32 = jnp.float32
BF16 = jnp.bfloat16

masked_score = -1e30
epsilon = 1e-06

CTX_R, CTX_L, CTX_FR, CTX_FL = 0, 1, 2, 3
SIDE = 4
SQUARES = 7
RING_R, RING_L = 10, 14
OVER_R, OVER_L = 17, 25
RELAY = 33
CORE_ROW = 41
CORE_SLAB = 49
S1_R, S1_L, S2_R, S2_L = 52, 60, 68, 76
H1_R, H1_L, H2_R, H2_L = 84, 92, 100, 108
CORE_MIX = 116
CHAIN = 148
Y_SUM = 176
FINAL = 179
CTX_LATE_R, CTX_LATE_L = 182, 183
COPIES = 184

NEAR = (2, -1, 1, 0)
FAR = (4, -3, 3, -2)


def layer_kernel(
    queries_hbm,
    new_keys_hbm,
    new_values_hbm,
    key_cache_hbm,
    value_cache_hbm,
    cache_len_ref,
    residual_hbm,
    out_proj_hbm,
    gain_ref,
    ids_ref,
    weights_ref,
    slots_ref,
    gate_up_hbm,
    down_hbm,
    result_ref,
    queries,
    new_keys,
    new_values,
    key_cache,
    value_cache,
    residual,
    by_head,
    context_head,
    own_keys,
    own_values,
    table_ref,
    side_out,
    ctx_all,
    side_all,
    proj,
    gate_up,
    down,
    squares,
    attended,
    rows,
    picks,
    picked,
    partial,
    first_in,
    second_in,
    hidden,
    expert_out,
    mixed,
    core_in,
    chain_out,
    chain_in,
    z_sum,
    y_in,
    final_out,
    final_in,
    send_sem,
    recv_sem,
    load_sem,
):
    x = lax.axis_index("grp")
    ep = lax.axis_index("ep")
    core = ep % 2
    z = (ep // 2) % NZ
    y = ep // (2 * NZ)

    def x_dev(step):
        return ((x + step) % NX, ep)

    def y_dev(step):
        return (x, (((y + step) % NY) * NZ + z) * 2 + core)

    def z_dev(step):
        return (x, (y * NZ + (z + step) % NZ) * 2 + core)

    partner = (x, (y * NZ + z) * 2 + 1 - core)

    def copy(source, target, index, device):
        return pltpu.make_async_remote_copy(
            src_ref=source,
            dst_ref=target,
            send_sem=send_sem.at[index],
            recv_sem=recv_sem.at[index],
            device_id=device,
            device_id_type=MESH,
        )

    peers = [x_dev(1), x_dev(2), x_dev(3), y_dev(1), y_dev(2), y_dev(3), z_dev(1), z_dev(7), partner]
    barrier = pltpu.get_barrier_semaphore()
    for peer in peers:
        pl.semaphore_signal(barrier, inc=1, device_id=peer, device_id_type=MESH)

    early = [
        pltpu.make_async_copy(queries_hbm, queries, load_sem.at[0]),
        pltpu.make_async_copy(new_keys_hbm, new_keys, load_sem.at[1]),
        pltpu.make_async_copy(new_values_hbm, new_values, load_sem.at[2]),
        pltpu.make_async_copy(key_cache_hbm, key_cache, load_sem.at[3]),
        pltpu.make_async_copy(value_cache_hbm, value_cache, load_sem.at[4]),
        pltpu.make_async_copy(residual_hbm, residual, load_sem.at[5]),
    ]
    loads = [
        pltpu.make_async_copy(out_proj_hbm, proj, load_sem.at[6]),
        pltpu.make_async_copy(gate_up_hbm, gate_up, load_sem.at[7]),
        pltpu.make_async_copy(down_hbm, down, load_sem.at[8]),
    ]
    for load in early + loads:
        load.start()

    slots = slots_ref[...].astype(F32)
    slot_lane = lax.broadcasted_iota(jnp.int32, slots.shape, 1)
    for j in range(SLOTS_DEV):
        here = ep * SLOTS_DEV + j
        mine = jnp.sum(jnp.where(slot_lane == here, slots, 0.0), axis=1, keepdims=True)
        same = jnp.where(slots == mine, 1.0, 0.0)
        twice = jnp.sum(same, axis=1, keepdims=True) - 1.0
        before = jnp.sum(jnp.where(slot_lane < here, same, 0.0), axis=1, keepdims=True)
        for row, value in ((j, mine + 1.0), (3 + j, twice), (6 + j, before)):
            table_ref[row : row + 1, :] = jnp.broadcast_to(value, (1, 128))
    spread_row = lax.broadcasted_iota(jnp.int32, (DEV_ROWS, 128), 0)
    spread_lane = lax.broadcasted_iota(jnp.int32, (DEV_ROWS, 128), 1)
    to_lane = jnp.where(spread_lane == spread_row + x * DEV_ROWS, 1.0, 0.0).astype(BF16)
    routes = [
        jnp.dot(value.astype(BF16), to_lane, preferred_element_type=F32)
        for value in (ids_ref[...].astype(F32) + 1.0, weights_ref[...].astype(F32))
    ]
    routes = jnp.concatenate(routes, axis=1)
    for load in early:
        load.wait()
    for g in range(NX):
        quarter = residual[:, g * DQ : (g + 1) * DQ].astype(F32)
        routes_wide = jnp.concatenate([routes, jnp.zeros((TOPK, DQ - HALF), F32)], axis=1)
        side_out[g] = jnp.concatenate([quarter, routes_wide], axis=0).astype(BF16)

    own_keys[...] = new_keys[...].astype(F32)
    own_values[...] = new_values[...].astype(F32)
    for h in range(HEADS):
        by_head[pl.ds(h, DEV_ROWS, stride=HEADS), :] = queries[
            :, h * HEAD_DIM : (h + 1) * HEAD_DIM
        ].astype(F32)
    width = KV_HEADS * HEAD_DIM
    head_row = lax.broadcasted_iota(jnp.int32, (HEADS, width), 0)
    head_lane = lax.broadcasted_iota(jnp.int32, (HEADS, width), 1)
    same_head = head_row // (HEADS // KV_HEADS) == head_lane // HEAD_DIM
    scaling = 1.0 / math.sqrt(HEAD_DIM)

    def spread_query(row):
        query = by_head[pl.ds(row * HEADS, HEADS), :]
        return jnp.where(same_head, jnp.concatenate([query] * KV_HEADS, axis=1), 0.0)

    def join(mixed_values):
        mixed_values = jnp.where(same_head, mixed_values, 0.0)
        joined = mixed_values[:, 0:HEAD_DIM]
        for kv in range(1, KV_HEADS):
            joined = joined + mixed_values[:, kv * HEAD_DIM : (kv + 1) * HEAD_DIM]
        return joined

    def score(query, keys):
        return (
            lax.dot_general(
                query.astype(BF16), keys, (((1,), (1,)), ((), ())), preferred_element_type=F32
            )
            * scaling
        )

    def prefill_row(row):
        query = spread_query(row)
        scores = score(query, new_keys[0 : 2 * PRE, :])
        token = lax.broadcasted_iota(jnp.int32, scores.shape, 1)
        scores = jnp.where(token <= row, scores, masked_score)
        exponent = jnp.exp(scores - jnp.max(scores, axis=1, keepdims=True))
        probs = (exponent / jnp.sum(exponent, axis=1, keepdims=True)).astype(BF16)
        values = jnp.dot(probs, new_values[0 : 2 * PRE, :], preferred_element_type=F32)
        context_head[pl.ds(row * HEADS, HEADS), :] = join(values)

    def decode_row(request):
        row = PRE + request
        query = spread_query(row)
        scores = score(query, key_cache[request])
        token = lax.broadcasted_iota(jnp.int32, scores.shape, 1)
        scores = jnp.where(token < cache_len_ref[request], scores, masked_score)
        own = jnp.sum(query * own_keys[pl.ds(row, 1), :], axis=1, keepdims=True) * scaling
        top = jnp.maximum(jnp.max(scores, axis=1, keepdims=True), own)
        exponent = jnp.exp(scores - top)
        own_exp = jnp.exp(own - top)
        total = jnp.sum(exponent, axis=1, keepdims=True) + own_exp
        probs = (exponent / total).astype(BF16)
        own_prob = (own_exp / total).astype(BF16).astype(F32)
        values = jnp.dot(probs, value_cache[request], preferred_element_type=F32)
        values = values + own_prob * own_values[pl.ds(row, 1), :]
        context_head[pl.ds(row * HEADS, HEADS), :] = join(values)

    def four(work):
        def body(i, carry):
            for part in range(4):
                work(i * 4 + part)
            return carry

        return body

    lax.fori_loop(0, PRE // 4, four(prefill_row), 0)
    lax.fori_loop(0, (DEV_ROWS - PRE) // 4, four(decode_row), 0)
    for h in range(HEADS // 2):
        pair = [
            context_head[pl.ds(there, DEV_ROWS, stride=HEADS), :] for there in (h, h + HEADS // 2)
        ]
        ctx_all[x, :, h * HEAD_DIM : (h + 1) * HEAD_DIM] = jnp.concatenate(pair, axis=0).astype(
            BF16
        )
    side_all[x] = side_out[x]
    pl.semaphore_wait(barrier, len(peers))

    pending = []

    def send(source, target, index, device):
        made = copy(source, target, index, device)
        made.start()
        pending.append(made)
        return made

    low, high = pl.ds(0, D // 2), pl.ds(D // 2, D // 2)

    def context_part(owner, lanes, index, device):
        part = ctx_all.at[owner, :, lanes]
        return send(part, part, index, device)

    sides = []
    for step in (1, 2, 3):
        there = (x + step) % NX
        sides.append(send(side_out.at[there], side_all.at[x], SIDE + step - 1, x_dev(step)))
    first_r = context_part(x, low, CTX_R, x_dev(1))
    first_l = context_part(x, high, CTX_L, x_dev(3))
    later_r = context_part(x, high, CTX_LATE_R, x_dev(1))
    later_l = context_part(x, low, CTX_LATE_L, x_dev(3))
    from_l, from_r = (x + 3) % NX, (x + 1) % NX
    first_r.wait_recv()
    fwd_r = context_part(from_l, low, CTX_FR, x_dev(1))
    first_l.wait_recv()
    fwd_l = context_part(from_r, high, CTX_FL, x_dev(3))
    later_r.wait_recv()
    later_l.wait_recv()
    loads[0].wait()
    for side in sides:
        side.wait_recv()
    fwd_r.wait_recv()
    fwd_l.wait_recv()

    context = ctx_all[...].reshape(NX * 2 * DEV_ROWS, D)
    first = jnp.dot(context, proj[0:D, :], preferred_element_type=F32)
    second = jnp.dot(context, proj[D : 2 * D, :], preferred_element_type=F32)
    for g in range(NX):
        base = g * 2 * DEV_ROWS
        term = first[base : base + DEV_ROWS] + second[base + DEV_ROWS : base + 2 * DEV_ROWS]
        kept = side_all[g].astype(F32)[0:DEV_ROWS]
        attended[g * DEV_ROWS : (g + 1) * DEV_ROWS, :] = (
            (kept + term).astype(BF16).astype(F32)
        )
    att = attended[...]
    total = jnp.sum(att * att, axis=1, keepdims=True)
    squares[x] = jnp.broadcast_to(total, (COL_ROWS, 128))
    shares = [
        send(squares.at[x], squares.at[x], SQUARES + step - 1, x_dev(step)) for step in (1, 2, 3)
    ]
    meta = (
        side_all[0].astype(F32)[DEV_ROWS:]
        + side_all[1].astype(F32)[DEV_ROWS:]
        + side_all[2].astype(F32)[DEV_ROWS:]
        + side_all[3].astype(F32)[DEV_ROWS:]
    )
    meta = jnp.concatenate([meta[:, 0:128], meta[:, 128:256]], axis=0)
    meta = jnp.concatenate([meta, jnp.zeros((16, DQ - 128), F32)], axis=1)
    rows[core, y, z, COL_ROWS : COL_ROWS + 16, :] = meta.astype(BF16)
    for share in shares:
        share.wait_recv()
    total = squares[0][:, 0:1] + squares[1][:, 0:1] + squares[2][:, 0:1] + squares[3][:, 0:1]
    normed = (att * lax.rsqrt(total / D + epsilon) * gain_ref[...]).astype(BF16)
    rows[core, y, z, 0:COL_ROWS, :] = normed
    loads[1].wait()
    loads[2].wait()

    opposite = (x + 2) % NX
    lower, upper = pl.ds(0, FF), pl.ds(FF, FF)

    def group_of(k):
        u = k // 2
        return (y + u + 2 * (u % 2) * (1 - u // 2) - u // 2) % NY

    def z_of(k, o):
        near = (k + 1 - (k // 2 + 3) // 4) % 2
        return (z + NZ + near * NEAR[o] + (1 - near) * FAR[o]) % NZ

    def first_copies(k):
        return (
            copy(partial.at[k, opposite, :, lower], first_in.at[k, 0], S1_R + k, x_dev(1)),
            copy(partial.at[k, opposite, :, upper], first_in.at[k, 1], S1_L + k, x_dev(3)),
        )

    def second_copies(k):
        return (
            copy(partial.at[k, from_r], second_in.at[k, 0], S2_R + k, x_dev(1)),
            copy(partial.at[k, from_l], second_in.at[k, 1], S2_L + k, x_dev(3)),
        )

    def hidden_copies(k):
        return (
            copy(hidden.at[k, x], hidden.at[k, x], H1_R + k, x_dev(1)),
            copy(hidden.at[k, x], hidden.at[k, x], H1_L + k, x_dev(3)),
        )

    near, far = pl.ds(0, FF // 2), pl.ds(FF // 2, FF // 2)

    def forward_copies(k):
        return (
            copy(hidden.at[k, from_l, :, near], hidden.at[k, from_l, :, near], H2_R + k, x_dev(1)),
            copy(hidden.at[k, from_r, :, far], hidden.at[k, from_r, :, far], H2_L + k, x_dev(3)),
        )

    def core_copy(k, o):
        return copy(mixed.at[k, 1 - core, o], core_in.at[k, o], CORE_MIX + 4 * k + o, partner)

    row_iota = lax.broadcasted_iota(jnp.int32, (COL_ROWS, COL_ROWS), 0)
    lane_iota = lax.broadcasted_iota(jnp.int32, (COL_ROWS, COL_ROWS), 1)
    earlier = (row_iota < lane_iota).astype(F32).astype(BF16)
    place = lax.broadcasted_iota(jnp.int32, (SPAN, COL_ROWS), 0).astype(F32)

    def pick_and_multiply(k):
        group = group_of(k)
        for column in range(2 * NY):
            there, cc = z_of(k, column // 2), column % 2
            meta = rows[cc, group, there, COL_ROWS : COL_ROWS + 16, 0:128].astype(F32)
            meta = meta[:, 0:COL_ROWS]
            ids, weights = meta[0:TOPK], meta[TOPK : 2 * TOPK]
            scale = 1.0 / jnp.sum(weights, axis=0, keepdims=True)
            named, share = [], []
            for j in range(SLOTS_DEV):
                same = (ids == table_ref[j : j + 1, 0:COL_ROWS]).astype(F32)
                named.append(jnp.sum(same, axis=0, keepdims=True))
                share.append(jnp.sum(same * weights, axis=0, keepdims=True) * scale)
            padded = jnp.concatenate(
                named + [jnp.zeros((SPAN - SLOTS_DEV, COL_ROWS), F32)], axis=0
            )
            ranks = jnp.dot(padded.astype(BF16), earlier, preferred_element_type=F32)
            chosen, weighted = [], []
            for j in range(SLOTS_DEV):
                rank = ranks[j : j + 1]
                twice = table_ref[3 + j : 4 + j, 0:COL_ROWS]
                parity = table_ref[6 + j : 7 + j, 0:COL_ROWS]
                halved = jnp.floor(rank * 0.5)
                where = jnp.where(twice > 0.5, halved, rank)
                odd = rank - 2.0 * halved
                good = (named[j] > 0.5) & ((twice < 0.5) | (odd == parity))
                key = jnp.where(good, where, -1.0)
                pick = (jnp.broadcast_to(key, (SPAN, COL_ROWS)) == place).astype(F32)
                chosen.append(pick)
                weighted.append(pick * share[j])
            pick = jnp.concatenate(chosen, axis=0).astype(BF16)
            picks[k % 8, column] = jnp.concatenate(weighted, axis=0)
            got = jnp.dot(pick, rows[cc, group, there, 0:COL_ROWS, :], preferred_element_type=F32)
            for j in range(SLOTS_DEV):
                picked[j, column * SPAN : (column + 1) * SPAN, :] = got[j * SPAN : (j + 1) * SPAN]
        for j in range(SLOTS_DEV):
            inputs = picked[j].astype(BF16)
            for part in range(3):
                lanes = slice(part * DQ, (part + 1) * DQ)
                product = jnp.dot(inputs, gate_up[j, :, lanes], preferred_element_type=F32)
                product = product.astype(BF16)
                for o in range(NX):
                    partial[k, o, j * 16 : (j + 1) * 16, lanes] = product[o * 16 : (o + 1) * 16]
        for made in first_copies(k):
            made.start()

    def add_first(k):
        for made in first_copies(k):
            made.wait_recv()
        partial[k, from_r, :, 0:FF] = (
            partial[k, from_r, :, 0:FF].astype(F32) + first_in[k, 0].astype(F32)
        ).astype(BF16)
        partial[k, from_l, :, FF : 2 * FF] = (
            partial[k, from_l, :, FF : 2 * FF].astype(F32) + first_in[k, 1].astype(F32)
        ).astype(BF16)
        for made in second_copies(k):
            made.start()

    def add_second(k):
        for made in second_copies(k):
            made.wait_recv()
        summed = (
            partial[k, x].astype(F32) + second_in[k, 0].astype(F32) + second_in[k, 1].astype(F32)
        )
        gate, up = summed[:, 0:FF], summed[:, FF : 2 * FF]
        hidden[k, x] = (gate / (1.0 + jnp.exp(-gate)) * up).astype(BF16)
        for made in hidden_copies(k):
            made.start()

    def pass_hidden(k):
        for made in hidden_copies(k):
            made.wait_recv()
        for made in forward_copies(k):
            made.start()

    def mix(k):
        for made in forward_copies(k):
            made.wait_recv()
        for j in range(SLOTS_DEV):
            inputs = hidden[k, :, j * 16 : (j + 1) * 16, :].reshape(NX * 16, FF)
            product = jnp.dot(inputs, down[j], preferred_element_type=F32)
            expert_out[j] = product.astype(BF16).astype(F32)
        for column in range(2 * NY):
            cc = column % 2
            span = slice(column * SPAN, (column + 1) * SPAN)
            results = jnp.concatenate([expert_out[j, span] for j in range(SLOTS_DEV)], axis=0)
            mixture = lax.dot_general(
                picks[k % 8, column].astype(BF16),
                results.astype(BF16),
                (((0,), (0,)), ((), ())),
                preferred_element_type=F32,
            )
            mixed[k, cc, column // 2] = mixture.astype(BF16)
            if cc == 1:
                core_copy(k, column // 2).start()

    def chunk_with(group, offset):
        near = offset in NEAR
        index = (NEAR if near else FAR).index(offset)
        first_half = near if group == 0 else not near
        return 2 * group + (0 if first_half else 1), index

    def chain_copy(group, leg, step):
        index = leg * 4 + step
        device = z_dev(1) if leg == 0 else z_dev(7)
        return copy(
            chain_out.at[group, index],
            chain_in.at[group, index],
            CHAIN + 7 * group + index,
            device,
        )

    def block(group, offset):
        k, index = chunk_with(group, offset)
        if k == NZ - 1:
            core_copy(k, index).wait_recv()
        return mixed[k, core, index].astype(F32) + core_in[k, index].astype(F32)

    def chain(group, step):
        for leg, offset in ((0, 4 - step), (1, step - 3)):
            if offset == 0:
                continue
            value = block(group, offset)
            if step > 0:
                chain_copy(group, leg, step - 1).wait_recv()
                value = value + chain_in[group, leg * 4 + step - 1].astype(F32)
            chain_out[group, leg * 4 + step] = value.astype(BF16)
            chain_copy(group, leg, step).start()

    def y_copy(group):
        step = (0, 3, 1, 2)[group]
        return copy(z_sum.at[group], y_in.at[group - 1], Y_SUM + group - 1, y_dev(step))

    def close(group):
        chain_copy(group, 1, 2).wait_recv()
        chain_copy(group, 0, 3).wait_recv()
        value = block(group, 0)
        value = value + chain_in[group, 3].astype(F32) + chain_in[group, 6].astype(F32)
        z_sum[group] = value.astype(BF16)
        if group > 0:
            y_copy(group).start()

    y_l, y_r = (y + 3) % NY, (y + 1) % NY

    def own_row(where):
        return rows.at[core, y, where % NZ]

    def ring(leg, step):
        where, device = (z + NZ - step, z_dev(1)) if leg == 0 else (z + step, z_dev(7))
        index = (RING_R if leg == 0 else RING_L) + step
        return copy(own_row(where), own_row(where), index, device)

    arrivals = (0, -1, 1, -2, 2, -3, 3, 4)

    def over(number, leg):
        block_ref = own_row(z + NZ + arrivals[number])
        index = (OVER_R if leg == 0 else OVER_L) + number
        return copy(block_ref, block_ref, index, y_dev(1) if leg == 0 else y_dev(3))

    def relay(number):
        where = (z + NZ + arrivals[number]) % NZ
        block_ref = rows.at[core, y_l if number % 2 == 0 else y_r, where]
        return copy(block_ref, block_ref, RELAY + number, y_dev(1) if number % 2 == 0 else y_dev(3))

    def core_row(number):
        block_ref = own_row(z + NZ + arrivals[number])
        return copy(block_ref, block_ref, CORE_ROW + number, partner)

    def core_slab(group):
        slab = rows.at[core, (y + (0, 3, 1, 2)[group]) % NY]
        return copy(slab, slab, CORE_SLAB + group - 1, partner)

    def spread(number):
        core_row(number).start()
        over(number, 0).start()
        over(number, 1).start()

    ring(0, 0).start()
    ring(1, 0).start()
    spread(0)
    for step in (1, 2):
        ring(1, step - 1).wait_recv()
        if step < 3:
            ring(1, step).start()
        spread(2 * step)
        ring(0, step - 1).wait_recv()
        ring(0, step).start()
        spread(2 * step - 1)
    for number in (0, 1, 2, 4):
        core_row(number).wait_recv()
    pick_and_multiply(0)
    ring(1, 2).wait_recv()
    spread(6)
    ring(0, 2).wait_recv()
    ring(0, 3).start()
    spread(5)
    ring(0, 3).wait_recv()
    spread(7)

    def receive_left():
        for number in range(NZ):
            over(number, 0).wait_recv()
            if number % 2 == 0:
                relay(number).start()
        core_slab(1).start()

    def receive_right():
        for number in range(NZ):
            over(number, 1).wait_recv()
            if number % 2 == 1:
                relay(number).start()
        core_slab(2).start()

    def receive_far():
        for number in range(NZ):
            relay(number).wait_recv()
        core_slab(3).start()

    events = {
        1: [receive_left],
        2: [receive_right],
        4: [receive_far],
    }
    ready = {
        1: [functools.partial(lambda n: core_row(n).wait_recv(), n) for n in (3, 5, 6, 7)],
        2: [lambda: core_slab(1).wait_recv()],
        4: [lambda: core_slab(2).wait_recv()],
        6: [lambda: core_slab(3).wait_recv()],
    }
    chains = {}
    for group in range(NY):
        start = 2 * group + 5 + (group == 0)
        for step in range(4):
            chains.setdefault(start + step, []).append(functools.partial(chain, group, step))
        chains.setdefault(start + 4, []).append(functools.partial(close, group))

    def at(t, table):
        for when, works in table.items():

            @pl.when(t == when)
            def _(works=works):
                for work in works:
                    work()

    def core_arrived(k):
        for o in range(4):
            core_copy(k, o).wait_recv()

    def tick(t, carry):
        pl.when((t >= 5) & (t < NZ + 4))(functools.partial(core_arrived, t - 5))
        at(t, chains)
        for stage, work in ((4, mix), (3, pass_hidden), (2, add_second), (1, add_first)):
            pl.when((t >= stage) & (t < NZ + stage))(functools.partial(work, t - stage))
        at(t, ready)
        pl.when(t < NZ)(functools.partial(pick_and_multiply, t))
        at(t, events)
        return carry

    lax.fori_loop(1, max(chains) + 1, tick, 0)

    for group in range(1, NY):
        y_copy(group).wait_recv()
    mixture = z_sum[0].astype(F32)
    for group in range(1, NY):
        mixture = mixture + y_in[group - 1].astype(F32)
    both = attended[...] + mixture
    for g in range(NX):
        span = slice(g * DEV_ROWS, (g + 1) * DEV_ROWS)
        final_out[g] = jnp.concatenate([mixture[span], both[span]], axis=0).astype(BF16)
    finals = []
    for step in (1, 2, 3):
        there = (x + step) % NX
        finals.append(send(final_out.at[there], final_in.at[x], FINAL + step - 1, x_dev(step)))
    final_in[x] = final_out[x]
    for made in finals:
        made.wait_recv()
    for g in range(NX):
        result_ref[:, g * DQ : (g + 1) * DQ] = final_in[g]

    def drain(k, carry):
        for made in (
            *first_copies(k),
            *second_copies(k),
            *hidden_copies(k),
            *forward_copies(k),
            *(core_copy(k, o) for o in range(4)),
        ):
            made.wait_send()

        return carry

    lax.fori_loop(0, NZ, drain, 0)
    for step in range(4):
        ring(0, step).wait_send()
        if step < 3:
            ring(1, step).wait_send()
    for number in range(NZ):
        for made in (over(number, 0), over(number, 1), relay(number), core_row(number)):
            made.wait_send()
    for group in range(NY):
        for step in range(4):
            chain_copy(group, 0, step).wait_send()
            if step < 3:
                chain_copy(group, 1, step).wait_send()
        if group > 0:
            core_slab(group).wait_send()
            y_copy(group).wait_send()
    for made in pending:
        made.wait_send()


def local(
    queries,
    new_keys,
    new_values,
    key_cache,
    value_cache,
    cache_len,
    residual,
    out_proj,
    norm_gain,
    expert_ids,
    route_weights,
    slot_expert,
    gate_up,
    down_proj,
):
    vmem = pl.BlockSpec(memory_space=pltpu.VMEM)
    smem = pl.BlockSpec(memory_space=pltpu.SMEM)
    hbm = pl.BlockSpec(memory_space=pl.ANY)
    requests, cached, width = key_cache.shape
    both = pl.pallas_call(
        layer_kernel,
        out_shape=jax.ShapeDtypeStruct((2 * DEV_ROWS, D), BF16),
        in_specs=[hbm] * 5 + [smem] + [hbm] * 2 + [vmem] * 4 + [hbm] * 2,
        out_specs=vmem,
        scratch_shapes=[
            pltpu.VMEM((DEV_ROWS, 2 * D), BF16),
            pltpu.VMEM((DEV_ROWS, width), BF16),
            pltpu.VMEM((DEV_ROWS, width), BF16),
            pltpu.VMEM((requests, cached, width), BF16),
            pltpu.VMEM((requests, cached, width), BF16),
            pltpu.VMEM((DEV_ROWS, D), BF16),
            pltpu.VMEM((DEV_ROWS * HEADS, HEAD_DIM), F32),
            pltpu.VMEM((DEV_ROWS * HEADS, HEAD_DIM), F32),
            pltpu.VMEM((DEV_ROWS, width), F32),
            pltpu.VMEM((DEV_ROWS, width), F32),
            pltpu.VMEM((16, 128), F32),
            pltpu.VMEM((NX, 32, DQ), BF16),
            pltpu.VMEM((NX, 2 * DEV_ROWS, D), BF16),
            pltpu.VMEM((NX, 32, DQ), BF16),
            pltpu.VMEM((2 * D, DQ), BF16),
            pltpu.VMEM((SLOTS_DEV, DQ, 2 * FF), BF16),
            pltpu.VMEM((SLOTS_DEV, FF, DQ), BF16),
            pltpu.VMEM((NX, COL_ROWS, 128), F32),
            pltpu.VMEM((COL_ROWS, DQ), F32),
            pltpu.VMEM((2, NY, NZ, COL_ROWS + 16, DQ), BF16),
            pltpu.VMEM((NZ, 2 * NY, SLOTS_DEV * SPAN, COL_ROWS), F32),
            pltpu.VMEM((SLOTS_DEV, 2 * NY * SPAN, DQ), F32),
            pltpu.VMEM((NZ, NX, 48, 2 * FF), BF16),
            pltpu.VMEM((NZ, 2, 48, FF), BF16),
            pltpu.VMEM((NZ, 2, 48, 2 * FF), BF16),
            pltpu.VMEM((NZ, NX, 48, FF), BF16),
            pltpu.VMEM((SLOTS_DEV, 2 * NY * SPAN, DQ), F32),
            pltpu.VMEM((NZ, 2, NY, COL_ROWS, DQ), BF16),
            pltpu.VMEM((NZ, NY, COL_ROWS, DQ), BF16),
            pltpu.VMEM((NY, 7, COL_ROWS, DQ), BF16),
            pltpu.VMEM((NY, 7, COL_ROWS, DQ), BF16),
            pltpu.VMEM((NY, COL_ROWS, DQ), BF16),
            pltpu.VMEM((NY - 1, COL_ROWS, DQ), BF16),
            pltpu.VMEM((NX, 48, DQ), BF16),
            pltpu.VMEM((NX, 48, DQ), BF16),
            pltpu.SemaphoreType.DMA((COPIES,)),
            pltpu.SemaphoreType.DMA((COPIES,)),
            pltpu.SemaphoreType.DMA((9,)),
        ],
        compiler_params=pltpu.CompilerParams(
            collective_id=0, has_side_effects=True, vmem_limit_bytes=67043328
        ),
    )(
        queries,
        new_keys,
        new_values,
        key_cache,
        value_cache,
        cache_len,
        residual,
        out_proj,
        norm_gain[None, :],
        expert_ids.T,
        route_weights.T,
        slot_expert[None, :],
        gate_up,
        down_proj,
    )
    return both[:DEV_ROWS], both[DEV_ROWS:]


def solution(mesh):
    placed = (
        P(("grp", "ep"), None),
        P(("grp", "ep"), None),
        P(("grp", "ep"), None),
        P(("grp", "ep"), None, None),
        P(("grp", "ep"), None, None),
        P(("grp", "ep")),
        P(("grp", "ep"), None),
        P(None, "grp"),
        P("grp"),
        P(("grp", "ep"), None),
        P(("grp", "ep"), None),
        P(),
        P("ep", "grp", None),
        P("ep", None, "grp"),
    )
    return jax.shard_map(
        local,
        mesh=mesh,
        in_specs=placed,
        out_specs=(P(("grp", "ep"), None), P(("grp", "ep"), None)),
        check_vma=False,
    )
```

```python
import functools
import math

import jax
import jax.numpy as jnp
from jax import lax
from jax.experimental import pallas as pl
from jax.experimental.pallas import tpu as pltpu
from jax.sharding import PartitionSpec as P

D = 2048
HEADS = 32
KV_HEADS = 4
HEAD_DIM = 128
FF = 768
TOPK = 8
SLOTS_DEV = 3
PRE = 8
DEV_ROWS = 24
COL_ROWS = 96
DQ = 512
HALF = 256
NX = 4
NY = 4
NZ = 8
SPAN = 8

MESH = pl.DeviceIdType.MESH
F32 = jnp.float32
BF16 = jnp.bfloat16

masked_score = -1e30
epsilon = 1e-06

CTX_R, CTX_L, CTX_FR, CTX_FL = 0, 1, 2, 3
SIDE = 4
SQUARES = 7
RING_R, RING_L = 10, 14
OVER_R, OVER_L = 17, 25
RELAY = 33
CORE_ROW = 41
CORE_SLAB = 49
S1_R, S1_L, S2_R, S2_L = 52, 60, 68, 76
H1_R, H1_L, H2_R, H2_L = 84, 92, 100, 108
CORE_MIX = 116
CHAIN = 148
Y_SUM = 176
FINAL = 179
CTX_LATE_R, CTX_LATE_L = 182, 183
COPIES = 184

NEAR = (2, -1, 1, 0)
FAR = (4, -3, 3, -2)


def layer_kernel(
    queries_hbm,
    new_keys_hbm,
    new_values_hbm,
    key_cache_hbm,
    value_cache_hbm,
    cache_len_ref,
    residual_hbm,
    out_proj_hbm,
    gain_ref,
    ids_ref,
    weights_ref,
    slots_ref,
    gate_up_hbm,
    down_hbm,
    result_ref,
    queries,
    new_keys,
    new_values,
    key_cache,
    value_cache,
    residual,
    by_head,
    context_head,
    own_keys,
    own_values,
    table_ref,
    side_out,
    ctx_all,
    side_all,
    proj,
    gate_up,
    down,
    squares,
    attended,
    rows,
    picks,
    picked,
    partial,
    first_in,
    second_in,
    hidden,
    expert_out,
    mixed,
    core_in,
    chain_out,
    chain_in,
    z_sum,
    y_in,
    final_out,
    final_in,
    send_sem,
    recv_sem,
    load_sem,
):
    x = lax.axis_index("grp")
    ep = lax.axis_index("ep")
    core = ep % 2
    z = (ep // 2) % NZ
    y = ep // (2 * NZ)

    def x_dev(step):
        return ((x + step) % NX, ep)

    def y_dev(step):
        return (x, (((y + step) % NY) * NZ + z) * 2 + core)

    def z_dev(step):
        return (x, (y * NZ + (z + step) % NZ) * 2 + core)

    partner = (x, (y * NZ + z) * 2 + 1 - core)

    def copy(source, target, index, device):
        return pltpu.make_async_remote_copy(
            src_ref=source,
            dst_ref=target,
            send_sem=send_sem.at[index],
            recv_sem=recv_sem.at[index],
            device_id=device,
            device_id_type=MESH,
        )

    peers = [x_dev(1), x_dev(2), x_dev(3), y_dev(1), y_dev(2), y_dev(3), z_dev(1), z_dev(7), partner]
    barrier = pltpu.get_barrier_semaphore()
    for peer in peers:
        pl.semaphore_signal(barrier, inc=1, device_id=peer, device_id_type=MESH)

    early = [
        pltpu.make_async_copy(queries_hbm, queries, load_sem.at[0]),
        pltpu.make_async_copy(new_keys_hbm, new_keys, load_sem.at[1]),
        pltpu.make_async_copy(new_values_hbm, new_values, load_sem.at[2]),
        pltpu.make_async_copy(key_cache_hbm, key_cache, load_sem.at[3]),
        pltpu.make_async_copy(value_cache_hbm, value_cache, load_sem.at[4]),
        pltpu.make_async_copy(residual_hbm, residual, load_sem.at[5]),
    ]
    loads = [
        pltpu.make_async_copy(out_proj_hbm, proj, load_sem.at[6]),
        pltpu.make_async_copy(gate_up_hbm, gate_up, load_sem.at[7]),
        pltpu.make_async_copy(down_hbm, down, load_sem.at[8]),
    ]
    for load in early + loads:
        load.start()

    slots = slots_ref[...].astype(F32)
    slot_lane = lax.broadcasted_iota(jnp.int32, slots.shape, 1)
    for j in range(SLOTS_DEV):
        here = ep * SLOTS_DEV + j
        mine = jnp.sum(jnp.where(slot_lane == here, slots, 0.0), axis=1, keepdims=True)
        same = jnp.where(slots == mine, 1.0, 0.0)
        twice = jnp.sum(same, axis=1, keepdims=True) - 1.0
        before = jnp.sum(jnp.where(slot_lane < here, same, 0.0), axis=1, keepdims=True)
        for row, value in ((j, mine + 1.0), (3 + j, twice), (6 + j, before)):
            table_ref[row : row + 1, :] = jnp.broadcast_to(value, (1, 128))
    spread_row = lax.broadcasted_iota(jnp.int32, (DEV_ROWS, 128), 0)
    spread_lane = lax.broadcasted_iota(jnp.int32, (DEV_ROWS, 128), 1)
    to_lane = jnp.where(spread_lane == spread_row + x * DEV_ROWS, 1.0, 0.0).astype(BF16)
    routes = [
        jnp.dot(value.astype(BF16), to_lane, preferred_element_type=F32)
        for value in (ids_ref[...].astype(F32) + 1.0, weights_ref[...].astype(F32))
    ]
    routes = jnp.concatenate(routes, axis=1)
    for load in early:
        load.wait()
    for g in range(NX):
        quarter = residual[:, g * DQ : (g + 1) * DQ].astype(F32)
        routes_wide = jnp.concatenate([routes, jnp.zeros((TOPK, DQ - HALF), F32)], axis=1)
        side_out[g] = jnp.concatenate([quarter, routes_wide], axis=0).astype(BF16)

    own_keys[...] = new_keys[...].astype(F32)
    own_values[...] = new_values[...].astype(F32)
    for h in range(HEADS):
        by_head[pl.ds(h, DEV_ROWS, stride=HEADS), :] = queries[
            :, h * HEAD_DIM : (h + 1) * HEAD_DIM
        ].astype(F32)
    width = KV_HEADS * HEAD_DIM
    head_row = lax.broadcasted_iota(jnp.int32, (HEADS, width), 0)
    head_lane = lax.broadcasted_iota(jnp.int32, (HEADS, width), 1)
    same_head = head_row // (HEADS // KV_HEADS) == head_lane // HEAD_DIM
    scaling = 1.0 / math.sqrt(HEAD_DIM)

    def spread_query(row):
        query = by_head[pl.ds(row * HEADS, HEADS), :]
        return jnp.where(same_head, jnp.concatenate([query] * KV_HEADS, axis=1), 0.0)

    def join(mixed_values):
        mixed_values = jnp.where(same_head, mixed_values, 0.0)
        joined = mixed_values[:, 0:HEAD_DIM]
        for kv in range(1, KV_HEADS):
            joined = joined + mixed_values[:, kv * HEAD_DIM : (kv + 1) * HEAD_DIM]
        return joined

    def score(query, keys):
        return (
            lax.dot_general(
                query.astype(BF16), keys, (((1,), (1,)), ((), ())), preferred_element_type=F32
            )
            * scaling
        )

    def prefill_row(row):
        query = spread_query(row)
        scores = score(query, new_keys[0 : 2 * PRE, :])
        token = lax.broadcasted_iota(jnp.int32, scores.shape, 1)
        scores = jnp.where(token <= row, scores, masked_score)
        exponent = jnp.exp(scores - jnp.max(scores, axis=1, keepdims=True))
        probs = (exponent / jnp.sum(exponent, axis=1, keepdims=True)).astype(BF16)
        values = jnp.dot(probs, new_values[0 : 2 * PRE, :], preferred_element_type=F32)
        context_head[pl.ds(row * HEADS, HEADS), :] = join(values)

    def decode_row(request):
        row = PRE + request
        query = spread_query(row)
        scores = score(query, key_cache[request])
        token = lax.broadcasted_iota(jnp.int32, scores.shape, 1)
        scores = jnp.where(token < cache_len_ref[request], scores, masked_score)
        own = jnp.sum(query * own_keys[pl.ds(row, 1), :], axis=1, keepdims=True) * scaling
        top = jnp.maximum(jnp.max(scores, axis=1, keepdims=True), own)
        exponent = jnp.exp(scores - top)
        own_exp = jnp.exp(own - top)
        total = jnp.sum(exponent, axis=1, keepdims=True) + own_exp
        probs = (exponent / total).astype(BF16)
        own_prob = (own_exp / total).astype(BF16).astype(F32)
        values = jnp.dot(probs, value_cache[request], preferred_element_type=F32)
        values = values + own_prob * own_values[pl.ds(row, 1), :]
        context_head[pl.ds(row * HEADS, HEADS), :] = join(values)

    def four(work):
        def body(i, carry):
            for part in range(4):
                work(i * 4 + part)
            return carry

        return body

    lax.fori_loop(0, PRE // 4, four(prefill_row), 0)
    lax.fori_loop(0, (DEV_ROWS - PRE) // 4, four(decode_row), 0)
    for h in range(HEADS // 2):
        pair = [
            context_head[pl.ds(there, DEV_ROWS, stride=HEADS), :] for there in (h, h + HEADS // 2)
        ]
        ctx_all[x, :, h * HEAD_DIM : (h + 1) * HEAD_DIM] = jnp.concatenate(pair, axis=0).astype(
            BF16
        )
    side_all[x] = side_out[x]
    pl.semaphore_wait(barrier, len(peers))

    pending = []

    def send(source, target, index, device):
        made = copy(source, target, index, device)
        made.start()
        pending.append(made)
        return made

    low, high = pl.ds(0, D // 2), pl.ds(D // 2, D // 2)

    def context_part(owner, lanes, index, device):
        part = ctx_all.at[owner, :, lanes]
        return send(part, part, index, device)

    first_r = context_part(x, low, CTX_R, x_dev(1))
    first_l = context_part(x, high, CTX_L, x_dev(3))
    sides = []
    for step in (1, 2, 3):
        there = (x + step) % NX
        sides.append(send(side_out.at[there], side_all.at[x], SIDE + step - 1, x_dev(step)))
    later_r = context_part(x, high, CTX_LATE_R, x_dev(1))
    later_l = context_part(x, low, CTX_LATE_L, x_dev(3))
    from_l, from_r = (x + 3) % NX, (x + 1) % NX
    first_r.wait_recv()
    fwd_r = context_part(from_l, low, CTX_FR, x_dev(1))
    first_l.wait_recv()
    fwd_l = context_part(from_r, high, CTX_FL, x_dev(3))
    later_r.wait_recv()
    later_l.wait_recv()
    loads[0].wait()
    for side in sides:
        side.wait_recv()
    fwd_r.wait_recv()
    fwd_l.wait_recv()

    context = ctx_all[...].reshape(NX * 2 * DEV_ROWS, D)
    first = jnp.dot(context, proj[0:D, :], preferred_element_type=F32)
    second = jnp.dot(context, proj[D : 2 * D, :], preferred_element_type=F32)
    for g in range(NX):
        base = g * 2 * DEV_ROWS
        term = first[base : base + DEV_ROWS] + second[base + DEV_ROWS : base + 2 * DEV_ROWS]
        kept = side_all[g].astype(F32)[0:DEV_ROWS]
        attended[g * DEV_ROWS : (g + 1) * DEV_ROWS, :] = (
            (kept + term).astype(BF16).astype(F32)
        )
    att = attended[...]
    total = jnp.sum(att * att, axis=1, keepdims=True)
    squares[x] = jnp.broadcast_to(total, (COL_ROWS, 128))
    shares = [
        send(squares.at[x], squares.at[x], SQUARES + step - 1, x_dev(step)) for step in (1, 2, 3)
    ]
    meta = (
        side_all[0].astype(F32)[DEV_ROWS:]
        + side_all[1].astype(F32)[DEV_ROWS:]
        + side_all[2].astype(F32)[DEV_ROWS:]
        + side_all[3].astype(F32)[DEV_ROWS:]
    )
    meta = jnp.concatenate([meta[:, 0:128], meta[:, 128:256]], axis=0)
    meta = jnp.concatenate([meta, jnp.zeros((16, DQ - 128), F32)], axis=1)
    rows[core, y, z, COL_ROWS : COL_ROWS + 16, :] = meta.astype(BF16)
    for share in shares:
        share.wait_recv()
    total = squares[0][:, 0:1] + squares[1][:, 0:1] + squares[2][:, 0:1] + squares[3][:, 0:1]
    normed = (att * lax.rsqrt(total / D + epsilon) * gain_ref[...]).astype(BF16)
    rows[core, y, z, 0:COL_ROWS, :] = normed
    loads[1].wait()
    loads[2].wait()

    opposite = (x + 2) % NX
    lower, upper = pl.ds(0, FF), pl.ds(FF, FF)

    def group_of(k):
        u = k // 2
        return (y + u + 2 * (u % 2) * (1 - u // 2) - u // 2) % NY

    def z_of(k, o):
        near = (k + 1 - (k // 2 + 3) // 4) % 2
        return (z + NZ + near * NEAR[o] + (1 - near) * FAR[o]) % NZ

    def first_copies(k):
        return (
            copy(partial.at[k, opposite, :, lower], first_in.at[k, 0], S1_R + k, x_dev(1)),
            copy(partial.at[k, opposite, :, upper], first_in.at[k, 1], S1_L + k, x_dev(3)),
        )

    def second_copies(k):
        return (
            copy(partial.at[k, from_r], second_in.at[k, 0], S2_R + k, x_dev(1)),
            copy(partial.at[k, from_l], second_in.at[k, 1], S2_L + k, x_dev(3)),
        )

    def hidden_copies(k):
        return (
            copy(hidden.at[k, x], hidden.at[k, x], H1_R + k, x_dev(1)),
            copy(hidden.at[k, x], hidden.at[k, x], H1_L + k, x_dev(3)),
        )

    near, far = pl.ds(0, FF // 2), pl.ds(FF // 2, FF // 2)

    def forward_copies(k):
        return (
            copy(hidden.at[k, from_l, :, near], hidden.at[k, from_l, :, near], H2_R + k, x_dev(1)),
            copy(hidden.at[k, from_r, :, far], hidden.at[k, from_r, :, far], H2_L + k, x_dev(3)),
        )

    def core_copy(k, o):
        return copy(mixed.at[k, 1 - core, o], core_in.at[k, o], CORE_MIX + 4 * k + o, partner)

    row_iota = lax.broadcasted_iota(jnp.int32, (COL_ROWS, COL_ROWS), 0)
    lane_iota = lax.broadcasted_iota(jnp.int32, (COL_ROWS, COL_ROWS), 1)
    earlier = (row_iota < lane_iota).astype(F32).astype(BF16)
    place = lax.broadcasted_iota(jnp.int32, (SPAN, COL_ROWS), 0).astype(F32)

    def pick_and_multiply(k):
        group = group_of(k)
        for column in range(2 * NY):
            there, cc = z_of(k, column // 2), column % 2
            meta = rows[cc, group, there, COL_ROWS : COL_ROWS + 16, 0:128].astype(F32)
            meta = meta[:, 0:COL_ROWS]
            ids, weights = meta[0:TOPK], meta[TOPK : 2 * TOPK]
            scale = 1.0 / jnp.sum(weights, axis=0, keepdims=True)
            named, share = [], []
            for j in range(SLOTS_DEV):
                same = (ids == table_ref[j : j + 1, 0:COL_ROWS]).astype(F32)
                named.append(jnp.sum(same, axis=0, keepdims=True))
                share.append(jnp.sum(same * weights, axis=0, keepdims=True) * scale)
            padded = jnp.concatenate(
                named + [jnp.zeros((SPAN - SLOTS_DEV, COL_ROWS), F32)], axis=0
            )
            ranks = jnp.dot(padded.astype(BF16), earlier, preferred_element_type=F32)
            chosen, weighted = [], []
            for j in range(SLOTS_DEV):
                rank = ranks[j : j + 1]
                twice = table_ref[3 + j : 4 + j, 0:COL_ROWS]
                parity = table_ref[6 + j : 7 + j, 0:COL_ROWS]
                halved = jnp.floor(rank * 0.5)
                where = jnp.where(twice > 0.5, halved, rank)
                odd = rank - 2.0 * halved
                good = (named[j] > 0.5) & ((twice < 0.5) | (odd == parity))
                key = jnp.where(good, where, -1.0)
                pick = (jnp.broadcast_to(key, (SPAN, COL_ROWS)) == place).astype(F32)
                chosen.append(pick)
                weighted.append(pick * share[j])
            pick = jnp.concatenate(chosen, axis=0).astype(BF16)
            picks[k % 8, column] = jnp.concatenate(weighted, axis=0)
            got = jnp.dot(pick, rows[cc, group, there, 0:COL_ROWS, :], preferred_element_type=F32)
            for j in range(SLOTS_DEV):
                picked[j, column * SPAN : (column + 1) * SPAN, :] = got[j * SPAN : (j + 1) * SPAN]
        for j in range(SLOTS_DEV):
            inputs = picked[j].astype(BF16)
            for part in range(3):
                lanes = slice(part * DQ, (part + 1) * DQ)
                product = jnp.dot(inputs, gate_up[j, :, lanes], preferred_element_type=F32)
                product = product.astype(BF16)
                for o in range(NX):
                    partial[k, o, j * 16 : (j + 1) * 16, lanes] = product[o * 16 : (o + 1) * 16]
        for made in first_copies(k):
            made.start()

    def add_first(k):
        for made in first_copies(k):
            made.wait_recv()
        partial[k, from_r, :, 0:FF] = (
            partial[k, from_r, :, 0:FF].astype(F32) + first_in[k, 0].astype(F32)
        ).astype(BF16)
        partial[k, from_l, :, FF : 2 * FF] = (
            partial[k, from_l, :, FF : 2 * FF].astype(F32) + first_in[k, 1].astype(F32)
        ).astype(BF16)
        for made in second_copies(k):
            made.start()

    def add_second(k):
        for made in second_copies(k):
            made.wait_recv()
        summed = (
            partial[k, x].astype(F32) + second_in[k, 0].astype(F32) + second_in[k, 1].astype(F32)
        )
        gate, up = summed[:, 0:FF], summed[:, FF : 2 * FF]
        hidden[k, x] = (gate / (1.0 + jnp.exp(-gate)) * up).astype(BF16)
        for made in hidden_copies(k):
            made.start()

    def pass_hidden(k):
        for made in hidden_copies(k):
            made.wait_recv()
        for made in forward_copies(k):
            made.start()

    def mix(k):
        for made in forward_copies(k):
            made.wait_recv()
        for j in range(SLOTS_DEV):
            inputs = hidden[k, :, j * 16 : (j + 1) * 16, :].reshape(NX * 16, FF)
            product = jnp.dot(inputs, down[j], preferred_element_type=F32)
            expert_out[j] = product.astype(BF16).astype(F32)
        for column in range(2 * NY):
            cc = column % 2
            span = slice(column * SPAN, (column + 1) * SPAN)
            results = jnp.concatenate([expert_out[j, span] for j in range(SLOTS_DEV)], axis=0)
            mixture = lax.dot_general(
                picks[k % 8, column].astype(BF16),
                results.astype(BF16),
                (((0,), (0,)), ((), ())),
                preferred_element_type=F32,
            )
            mixed[k, cc, column // 2] = mixture.astype(BF16)
            if cc == 1:
                core_copy(k, column // 2).start()

    def chunk_with(group, offset):
        near = offset in NEAR
        index = (NEAR if near else FAR).index(offset)
        first_half = near if group == 0 else not near
        return 2 * group + (0 if first_half else 1), index

    def chain_copy(group, leg, step):
        index = leg * 4 + step
        device = z_dev(1) if leg == 0 else z_dev(7)
        return copy(
            chain_out.at[group, index],
            chain_in.at[group, index],
            CHAIN + 7 * group + index,
            device,
        )

    def block(group, offset):
        k, index = chunk_with(group, offset)
        if k == NZ - 1:
            core_copy(k, index).wait_recv()
        return mixed[k, core, index].astype(F32) + core_in[k, index].astype(F32)

    def chain(group, step):
        for leg, offset in ((0, 4 - step), (1, step - 3)):
            if offset == 0:
                continue
            value = block(group, offset)
            if step > 0:
                chain_copy(group, leg, step - 1).wait_recv()
                value = value + chain_in[group, leg * 4 + step - 1].astype(F32)
            chain_out[group, leg * 4 + step] = value.astype(BF16)
            chain_copy(group, leg, step).start()

    def y_copy(group):
        step = (0, 3, 1, 2)[group]
        return copy(z_sum.at[group], y_in.at[group - 1], Y_SUM + group - 1, y_dev(step))

    def close(group):
        chain_copy(group, 1, 2).wait_recv()
        chain_copy(group, 0, 3).wait_recv()
        value = block(group, 0)
        value = value + chain_in[group, 3].astype(F32) + chain_in[group, 6].astype(F32)
        z_sum[group] = value.astype(BF16)
        if group > 0:
            y_copy(group).start()

    y_l, y_r = (y + 3) % NY, (y + 1) % NY

    def own_row(where):
        return rows.at[core, y, where % NZ]

    def ring(leg, step):
        where, device = (z + NZ - step, z_dev(1)) if leg == 0 else (z + step, z_dev(7))
        index = (RING_R if leg == 0 else RING_L) + step
        return copy(own_row(where), own_row(where), index, device)

    arrivals = (0, -1, 1, -2, 2, -3, 3, 4)

    def over(number, leg):
        block_ref = own_row(z + NZ + arrivals[number])
        index = (OVER_R if leg == 0 else OVER_L) + number
        return copy(block_ref, block_ref, index, y_dev(1) if leg == 0 else y_dev(3))

    def relay(number):
        where = (z + NZ + arrivals[number]) % NZ
        block_ref = rows.at[core, y_l if number % 2 == 0 else y_r, where]
        return copy(block_ref, block_ref, RELAY + number, y_dev(1) if number % 2 == 0 else y_dev(3))

    def core_row(number):
        block_ref = own_row(z + NZ + arrivals[number])
        return copy(block_ref, block_ref, CORE_ROW + number, partner)

    def core_slab(group):
        slab = rows.at[core, (y + (0, 3, 1, 2)[group]) % NY]
        return copy(slab, slab, CORE_SLAB + group - 1, partner)

    def spread(number):
        core_row(number).start()
        over(number, 0).start()
        over(number, 1).start()

    ring(0, 0).start()
    ring(1, 0).start()
    spread(0)
    for step in (1, 2):
        ring(1, step - 1).wait_recv()
        if step < 3:
            ring(1, step).start()
        spread(2 * step)
        ring(0, step - 1).wait_recv()
        ring(0, step).start()
        spread(2 * step - 1)
    for number in (0, 1, 2, 4):
        core_row(number).wait_recv()
    pick_and_multiply(0)
    ring(1, 2).wait_recv()
    spread(6)
    ring(0, 2).wait_recv()
    ring(0, 3).start()
    spread(5)
    ring(0, 3).wait_recv()
    spread(7)

    def receive_left():
        for number in range(NZ):
            over(number, 0).wait_recv()
            if number % 2 == 0:
                relay(number).start()
        core_slab(1).start()

    def receive_right():
        for number in range(NZ):
            over(number, 1).wait_recv()
            if number % 2 == 1:
                relay(number).start()
        core_slab(2).start()

    def receive_far():
        for number in range(NZ):
            relay(number).wait_recv()
        core_slab(3).start()

    events = {
        1: [receive_left],
        2: [receive_right],
        4: [receive_far],
    }
    ready = {
        1: [functools.partial(lambda n: core_row(n).wait_recv(), n) for n in (3, 5, 6, 7)],
        2: [lambda: core_slab(1).wait_recv()],
        4: [lambda: core_slab(2).wait_recv()],
        6: [lambda: core_slab(3).wait_recv()],
    }
    chains = {}
    for group in range(NY):
        start = 2 * group + 5 + (group == 0)
        for step in range(4):
            chains.setdefault(start + step, []).append(functools.partial(chain, group, step))
        chains.setdefault(start + 4, []).append(functools.partial(close, group))

    def at(t, table):
        for when, works in table.items():

            @pl.when(t == when)
            def _(works=works):
                for work in works:
                    work()

    def core_arrived(k):
        for o in range(4):
            core_copy(k, o).wait_recv()

    def tick(t, carry):
        pl.when((t >= 5) & (t < NZ + 4))(functools.partial(core_arrived, t - 5))
        at(t, chains)
        for stage, work in ((4, mix), (3, pass_hidden), (2, add_second), (1, add_first)):
            pl.when((t >= stage) & (t < NZ + stage))(functools.partial(work, t - stage))
        at(t, ready)
        pl.when(t < NZ)(functools.partial(pick_and_multiply, t))
        at(t, events)
        return carry

    lax.fori_loop(1, max(chains) + 1, tick, 0)

    for group in range(1, NY):
        y_copy(group).wait_recv()
    mixture = z_sum[0].astype(F32)
    for group in range(1, NY):
        mixture = mixture + y_in[group - 1].astype(F32)
    both = attended[...] + mixture
    for g in range(NX):
        span = slice(g * DEV_ROWS, (g + 1) * DEV_ROWS)
        final_out[g] = jnp.concatenate([mixture[span], both[span]], axis=0).astype(BF16)
    finals = []
    for step in (1, 2, 3):
        there = (x + step) % NX
        finals.append(send(final_out.at[there], final_in.at[x], FINAL + step - 1, x_dev(step)))
    final_in[x] = final_out[x]
    for made in finals:
        made.wait_recv()
    for g in range(NX):
        result_ref[:, g * DQ : (g + 1) * DQ] = final_in[g]

    def drain(k, carry):
        for made in (
            *first_copies(k),
            *second_copies(k),
            *hidden_copies(k),
            *forward_copies(k),
            *(core_copy(k, o) for o in range(4)),
        ):
            made.wait_send()

        return carry

    lax.fori_loop(0, NZ, drain, 0)
    for step in range(4):
        ring(0, step).wait_send()
        if step < 3:
            ring(1, step).wait_send()
    for number in range(NZ):
        for made in (over(number, 0), over(number, 1), relay(number), core_row(number)):
            made.wait_send()
    for group in range(NY):
        for step in range(4):
            chain_copy(group, 0, step).wait_send()
            if step < 3:
                chain_copy(group, 1, step).wait_send()
        if group > 0:
            core_slab(group).wait_send()
            y_copy(group).wait_send()
    for made in pending:
        made.wait_send()


def local(
    queries,
    new_keys,
    new_values,
    key_cache,
    value_cache,
    cache_len,
    residual,
    out_proj,
    norm_gain,
    expert_ids,
    route_weights,
    slot_expert,
    gate_up,
    down_proj,
):
    vmem = pl.BlockSpec(memory_space=pltpu.VMEM)
    smem = pl.BlockSpec(memory_space=pltpu.SMEM)
    hbm = pl.BlockSpec(memory_space=pl.ANY)
    requests, cached, width = key_cache.shape
    both = pl.pallas_call(
        layer_kernel,
        out_shape=jax.ShapeDtypeStruct((2 * DEV_ROWS, D), BF16),
        in_specs=[hbm] * 5 + [smem] + [hbm] * 2 + [vmem] * 4 + [hbm] * 2,
        out_specs=vmem,
        scratch_shapes=[
            pltpu.VMEM((DEV_ROWS, 2 * D), BF16),
            pltpu.VMEM((DEV_ROWS, width), BF16),
            pltpu.VMEM((DEV_ROWS, width), BF16),
            pltpu.VMEM((requests, cached, width), BF16),
            pltpu.VMEM((requests, cached, width), BF16),
            pltpu.VMEM((DEV_ROWS, D), BF16),
            pltpu.VMEM((DEV_ROWS * HEADS, HEAD_DIM), F32),
            pltpu.VMEM((DEV_ROWS * HEADS, HEAD_DIM), F32),
            pltpu.VMEM((DEV_ROWS, width), F32),
            pltpu.VMEM((DEV_ROWS, width), F32),
            pltpu.VMEM((16, 128), F32),
            pltpu.VMEM((NX, 32, DQ), BF16),
            pltpu.VMEM((NX, 2 * DEV_ROWS, D), BF16),
            pltpu.VMEM((NX, 32, DQ), BF16),
            pltpu.VMEM((2 * D, DQ), BF16),
            pltpu.VMEM((SLOTS_DEV, DQ, 2 * FF), BF16),
            pltpu.VMEM((SLOTS_DEV, FF, DQ), BF16),
            pltpu.VMEM((NX, COL_ROWS, 128), F32),
            pltpu.VMEM((COL_ROWS, DQ), F32),
            pltpu.VMEM((2, NY, NZ, COL_ROWS + 16, DQ), BF16),
            pltpu.VMEM((NZ, 2 * NY, SLOTS_DEV * SPAN, COL_ROWS), F32),
            pltpu.VMEM((SLOTS_DEV, 2 * NY * SPAN, DQ), F32),
            pltpu.VMEM((NZ, NX, 48, 2 * FF), BF16),
            pltpu.VMEM((NZ, 2, 48, FF), BF16),
            pltpu.VMEM((NZ, 2, 48, 2 * FF), BF16),
            pltpu.VMEM((NZ, NX, 48, FF), BF16),
            pltpu.VMEM((SLOTS_DEV, 2 * NY * SPAN, DQ), F32),
            pltpu.VMEM((NZ, 2, NY, COL_ROWS, DQ), BF16),
            pltpu.VMEM((NZ, NY, COL_ROWS, DQ), BF16),
            pltpu.VMEM((NY, 7, COL_ROWS, DQ), BF16),
            pltpu.VMEM((NY, 7, COL_ROWS, DQ), BF16),
            pltpu.VMEM((NY, COL_ROWS, DQ), BF16),
            pltpu.VMEM((NY - 1, COL_ROWS, DQ), BF16),
            pltpu.VMEM((NX, 48, DQ), BF16),
            pltpu.VMEM((NX, 48, DQ), BF16),
            pltpu.SemaphoreType.DMA((COPIES,)),
            pltpu.SemaphoreType.DMA((COPIES,)),
            pltpu.SemaphoreType.DMA((9,)),
        ],
        compiler_params=pltpu.CompilerParams(
            collective_id=0, has_side_effects=True, vmem_limit_bytes=67043328
        ),
    )(
        queries,
        new_keys,
        new_values,
        key_cache,
        value_cache,
        cache_len,
        residual,
        out_proj,
        norm_gain[None, :],
        expert_ids.T,
        route_weights.T,
        slot_expert[None, :],
        gate_up,
        down_proj,
    )
    return both[:DEV_ROWS], both[DEV_ROWS:]


def solution(mesh):
    placed = (
        P(("grp", "ep"), None),
        P(("grp", "ep"), None),
        P(("grp", "ep"), None),
        P(("grp", "ep"), None, None),
        P(("grp", "ep"), None, None),
        P(("grp", "ep")),
        P(("grp", "ep"), None),
        P(None, "grp"),
        P("grp"),
        P(("grp", "ep"), None),
        P(("grp", "ep"), None),
        P(),
        P("ep", "grp", None),
        P("ep", None, "grp"),
    )
    return jax.shard_map(
        local,
        mesh=mesh,
        in_specs=placed,
        out_specs=(P(("grp", "ep"), None), P(("grp", "ep"), None)),
        check_vma=False,
    )
```
